32 devices in a mesh: dp: 2 (over x), expert: 16 (over z, y, core).
Axes of the slice: x: 2, y: 2, z: 4, core: 2. Of those that a mesh axis runs over, the one named last changes fastest.
Arguments:
- tokens: bfloat16 [4096, 1024], P(('dp', 'expert')), may hold values from -6 to 6
- cotangent: bfloat16 [4096, 1024], P(('dp', 'expert')), may hold values from -6 to 6
- expert_ids: int32 [4096, 6], P(('dp', 'expert')), may hold values from 0 to 15, all different within a row; in each aligned block of 128 rows (0 to 127, 128 to 255, ...) at most 60 rows name the same one
- gate_weights: float32 [4096, 6], P(('dp', 'expert')), may hold values from 0.05 to 0.3
- partner: int32 [16], replicated, may hold values from 0 to 15, as said below
- weights: bfloat16 [16, 1024, 3, 384], P('expert', 'dp'), may hold values from -0.3125 to 0.3125
- first_moment: bfloat16 [16, 1024, 3, 384], P('expert', 'dp'), may hold values from -6 to 6
- second_moment: bfloat16 [16, 1024, 3, 384], P('expert', 'dp'), may hold values from 0.099609375 to 4
Outputs:
- mixed: bfloat16 [4096, 1024], P(('dp', 'expert'))
- token_grad: bfloat16 [4096, 1024], P(('dp', 'expert'))
- new_weights: bfloat16 [16, 1024, 3, 384], P('expert', 'dp')
- new_first: bfloat16 [16, 1024, 3, 384], P('expert', 'dp')
- new_second: bfloat16 [16, 1024, 3, 384], P('expert', 'dp')
The draws below stay inside these ranges and needn't reach their ends.
Inputs may be any that keep to these rules, and one draw needn't show every extreme that they name: `expert_ids`: each row names 6 different experts. Among the 128 tokens of one device (aligned blocks of rows), no expert is named by more than 60 tokens, and in every draw some block names some expert exactly 60 times. partner[partner[h]] = h and partner[h] != h for every h.
All inputs are finite; a program needn't handle non-finite values.
Results may differ from the reference program's by a relative error of at most 0.024.
Values may be sent and summed in bfloat16 or wider, within the bound.
A program may use at most 64 MiB of HBM per device.

```python
import math
import jax
import jax.numpy as jnp
import numpy as np
from jax import lax

D = 1024
FF = 384
TOP = 6
TOK_DEV = 128
EXPERTS = 16
CAP = 60
TOKENS = 4096
N_DP = 2
N_EXPERT = 16


def draw_partner(key, part):
    order = jax.random.permutation(key, EXPERTS).astype(jnp.int32)
    paired = order.reshape(EXPERTS // 2, 2)[:, ::-1].reshape(EXPERTS)
    return jnp.zeros((EXPERTS,), jnp.int32).at[order].set(paired)


def levels(own_key, dims, pieces, least, top_value):
    def one(axis_at, shards_of):
        heights = jax.random.uniform(jax.random.fold_in(jax.random.fold_in(own_key, 6), axis_at), (shards_of,), jnp.float32, least / len(pieces), top_value / len(pieces))
        return jnp.repeat(jnp.exp(heights), dims[axis_at] // shards_of).reshape((-1,) + (1,) * (len(dims) - axis_at - 1))

    factor_of = one(*pieces[0])
    for cut in pieces[1:]:
        factor_of = factor_of * one(*cut)
    return factor_of


def routed_block(own_key, own, number, rows, count, top, bound, lean):
    order = jax.random.permutation(own_key, count)
    packed, usual = load_shares(count, rows * top, bound, lean, True), load_shares(count, rows * top, bound, lean, False)
    places = jnp.arange(count)

    def named(lengths, turn):
        used = int((lengths > 0).sum())
        fixed = max(1, used // 4)
        shifted = fixed + (places - fixed + turn * (used - fixed)) % max(1, count - fixed)
        return jnp.zeros((count,), jnp.int32).at[order[jnp.where(places < fixed, places, shifted)]].set(jnp.asarray(lengths, jnp.int32))

    lengths = jnp.where(number % 4 == 0, named(packed, number // 4), named(usual, number - number // 4 - 1))
    mixed = jax.random.permutation(jax.random.fold_in(own, 3), count)
    giver, taker = mixed[0:count // 2 * 2:2], mixed[1:count // 2 * 2:2]
    slack = jnp.minimum(lengths[giver] - 1, bound - lengths[taker]) // 2
    slack = jnp.where((giver == order[0]) | (taker == order[0]) | (lengths[taker] == 0), 0, jnp.maximum(slack, 0))
    shifted = jax.random.randint(jax.random.fold_in(own, 4), (count // 2,), 0, 1 << 20) % (slack + 1)
    lengths = lengths.at[giver].add(-shifted).at[taker].add(shifted)
    members = jnp.searchsorted(jnp.cumsum(lengths), jnp.arange(rows * top), side="right").astype(jnp.int32)
    listing = members.reshape(top, rows).T
    listing = listing[jax.random.permutation(jax.random.fold_in(own, 1), rows)]
    turn = jax.random.randint(jax.random.fold_in(own, 2), (rows, 1), 0, top)
    return jnp.take_along_axis(listing, (jnp.arange(top)[None, :] + turn) % top, axis=1)


def load_shares(count, total, reach, skew, full):
    weights = [(1 << 20) // math.isqrt(standing ** skew) + 1 for standing in range(1, count + 1)]
    largest = reach if full else min(reach, max(-(-total // count), total * weights[0] // sum(weights)))
    least = 1 if total - largest >= count - 1 else 0
    holding, rest = [largest] + [least] * (count - 1), total - largest - least * (count - 1)
    while rest > 0:
        free = [i for i in range(1, count) if holding[i] < largest] or [i for i in range(1, count) if holding[i] < reach]
        mass, remaining = sum([weights[i] for i in free]), rest
        for i in free:
            addition = min(reach - holding[i], max(1, remaining * weights[i] // mass), rest)
            holding[i] = holding[i] + addition
            rest = rest - addition
    return np.array(holding)


def normal_values(stream_key, shape, scale, bound, shards=(), kind=jnp.bfloat16):
    factor_of = levels(stream_key, shape, shards, -0.22, 0.18) if shards else 1.0
    array = jax.random.normal(stream_key, shape, jnp.float32) * scale * factor_of
    return jnp.minimum(jnp.maximum(array, -bound), bound).astype(kind)


def setup_inputs(seed: int = 0) -> dict:
    seeds = jax.random.split(jax.random.key(seed), 9)
    tokens = normal_values(seeds[0], (TOKENS, D), 1.0, 6.0, ((0, 32),))
    cotangent = normal_values(seeds[1], (TOKENS, D), 1.0, 6.0, ((0, 32),))
    expert_ids_keys = jax.random.split(jax.random.fold_in(seeds[2], 1), TOKENS // TOK_DEV)
    expert_ids_turns = jax.random.permutation(jax.random.fold_in(seeds[2], 3), TOKENS // TOK_DEV)
    expert_ids = jax.vmap(lambda own, number: routed_block(jax.random.fold_in(seeds[2], 2), own, number, TOK_DEV, EXPERTS, TOP, CAP, 1))(expert_ids_keys, expert_ids_turns).reshape((TOKENS, TOP))
    gate_weights = jnp.clip(0.05 + 0.25 * jax.random.uniform(seeds[3], (TOKENS, TOP), jnp.float32) ** levels(seeds[3], (TOKENS, TOP), ((0, 32),), -0.2, 0.2), 0.05, 0.3)
    partner = draw_partner(jax.random.fold_in(seeds[8], 71), 0)
    weights = normal_values(seeds[5], (EXPERTS, D, 3, FF), FF ** -0.5, 0.3125, ((0, 16), (1, 2)))
    first_moment = normal_values(seeds[6], (EXPERTS, D, 3, FF), 1.0, 6.0, ((0, 16), (1, 2)))
    second_moment = jnp.clip(jnp.exp(math.log(4.0) - 3.6927934 * jax.random.uniform(seeds[7], (EXPERTS, D, 3, FF), jnp.float32) ** levels(seeds[7], (EXPERTS, D, 3, FF), ((0, 16), (1, 2)), -0.2, 0.2)), 0.099609375, 4.0).astype(jnp.bfloat16)
    return {"tokens": tokens, "cotangent": cotangent, "expert_ids": expert_ids, "gate_weights": gate_weights, "partner": partner, "weights": weights, "first_moment": first_moment, "second_moment": second_moment}


beta_one = 0.9
beta_two = 0.95
learn_rate = 0.01
decay_rate = 0.1
eps_adam = 1e-08
step_count = 100

def expert_pass(x_rows, dy_rows, expert_w):
    hidden_width = expert_w.shape[2]
    gate_up = expert_w[:, 0:2, :].reshape(expert_w.shape[0], 2 * hidden_width)
    down_proj = expert_w[:, 2, :]
    both_proj = jnp.dot(x_rows, gate_up, preferred_element_type=jnp.float32)
    pre_act = both_proj[:, :hidden_width]
    lin_act = both_proj[:, hidden_width:]
    sigmoid_pre = jax.nn.sigmoid(pre_act)
    silu_pre = pre_act * sigmoid_pre
    hidden = (silu_pre * lin_act).astype(jnp.bfloat16)
    out_rows = jnp.dot(hidden, down_proj.T, preferred_element_type=jnp.float32).astype(jnp.bfloat16)
    hidden_grad = jnp.dot(dy_rows, down_proj, preferred_element_type=jnp.float32)
    pre_grad = (hidden_grad * lin_act * sigmoid_pre * (1.0 + pre_act * (1.0 - sigmoid_pre))).astype(jnp.bfloat16)
    lin_grad = (hidden_grad * silu_pre).astype(jnp.bfloat16)
    both_grad = jnp.concatenate([pre_grad, lin_grad], axis=1)
    item_grad = jnp.dot(both_grad, gate_up.T, preferred_element_type=jnp.float32).astype(jnp.bfloat16)
    proj_grad = jnp.dot(x_rows.T, both_grad, preferred_element_type=jnp.float32)
    down_grad = jnp.dot(dy_rows.T, hidden, preferred_element_type=jnp.float32)
    partial_grad = jnp.concatenate([proj_grad.reshape(-1, 2, hidden_width), down_grad.reshape(-1, 1, hidden_width)], axis=1)
    return (out_rows, item_grad, partial_grad)

def reference(tokens, cotangent, expert_ids, gate_weights, partner, weights, first_moment, second_moment):
    model_width = tokens.shape[1]
    hidden_width = weights.shape[3]
    per_replica = N_EXPERT * TOK_DEV
    item_total = per_replica * TOP
    slot_total = N_EXPERT * CAP
    zero_row = jnp.zeros((1, model_width), jnp.bfloat16)
    accum_rows = N_DP * (per_replica + 1)

    def one_expert(carry, expert):
        mixed_acc, grad_acc = carry
        expert_w = lax.dynamic_index_in_dim(weights, expert, 0, keepdims=False)
        grad_sum = jnp.zeros((model_width, 3, hidden_width), jnp.float32)
        for replica in range(N_DP):
            low = replica * per_replica
            flat_ids = expert_ids[low:low + per_replica].reshape(item_total)
            chosen = jnp.nonzero(flat_ids == expert, size=slot_total, fill_value=item_total)[0].astype(jnp.int32)
            token_of = (chosen // TOP).astype(jnp.int32)
            x_pad = jnp.concatenate([tokens[low:low + per_replica], zero_row], axis=0)
            cot_pad = jnp.concatenate([cotangent[low:low + per_replica], zero_row], axis=0)
            gate_pad = jnp.concatenate([gate_weights[low:low + per_replica].reshape(item_total), jnp.zeros((1,), jnp.float32)])
            gate_rows = gate_pad[chosen]
            x_rows = x_pad[token_of]
            dy_rows = (gate_rows[:, None] * cot_pad[token_of].astype(jnp.float32)).astype(jnp.bfloat16)
            out_rows, item_grad, partial_grad = expert_pass(x_rows, dy_rows, expert_w)
            target = token_of + replica * (per_replica + 1)
            out_back = lax.optimization_barrier(out_rows).astype(jnp.float32)
            grad_back = lax.optimization_barrier(item_grad).astype(jnp.float32)
            mixed_acc = mixed_acc.at[target].add(gate_rows[:, None] * out_back)
            grad_acc = grad_acc.at[target].add(grad_back)
            rounded = lax.optimization_barrier(partial_grad.astype(jnp.bfloat16))
            grad_sum = grad_sum + rounded.astype(jnp.float32)
        w_old = expert_w.astype(jnp.float32)
        m_old = lax.dynamic_index_in_dim(first_moment, expert, 0, keepdims=False).astype(jnp.float32)
        v_old = lax.dynamic_index_in_dim(second_moment, expert, 0, keepdims=False).astype(jnp.float32)
        m_new = beta_one * m_old + (1.0 - beta_one) * grad_sum
        v_new = beta_two * v_old + (1.0 - beta_two) * grad_sum * grad_sum
        m_hat = m_new / (1.0 - beta_one ** step_count)
        v_hat = v_new / (1.0 - beta_two ** step_count)
        w_new = w_old - learn_rate * (m_hat / (jnp.sqrt(v_hat) + eps_adam) + decay_rate * w_old)
        states = (w_new.astype(jnp.bfloat16), m_new.astype(jnp.bfloat16), v_new.astype(jnp.bfloat16))
        return ((mixed_acc, grad_acc), states)
    start = (jnp.zeros((accum_rows, model_width), jnp.float32), jnp.zeros((accum_rows, model_width), jnp.float32))
    (mixed_acc, grad_acc), states = lax.scan(one_expert, start, jnp.arange(EXPERTS, dtype=jnp.int32))
    mixed = mixed_acc.reshape(N_DP, per_replica + 1, model_width)[:, :per_replica].reshape(TOKENS, model_width)
    token_grad = grad_acc.reshape(N_DP, per_replica + 1, model_width)[:, :per_replica].reshape(TOKENS, model_width)
    new_weights = states[0][partner]
    new_first = states[1][partner]
    new_second = states[2][partner]
    return (mixed.astype(jnp.bfloat16), token_grad.astype(jnp.bfloat16), new_weights, new_first, new_second)
```

```python
import functools

import jax
import jax.numpy as jnp
from jax import lax
from jax.experimental import pallas as pl
from jax.experimental.pallas import tpu as pltpu
from jax.sharding import PartitionSpec as P

beta_one = 0.9
beta_two = 0.95
learn_rate = 0.01
decay_rate = 0.1
eps_adam = 1e-08
step_count = 100


def send_rows(parts):
    return (lax.all_to_all(parts[0], "expert", split_axis=0, concat_axis=0, tiled=True),)


def send_back(parts):
    return (lax.all_to_all(parts[0], "expert", split_axis=0, concat_axis=0, tiled=True),)


def shards_by_slot(
    tokens, cotangent, expert_ids, gate_weights, partner, weights, first_moment, second_moment
):
    experts_here = lax.axis_size("expert")
    tok_dev, model_width = tokens.shape
    top_count = expert_ids.shape[1]
    hidden_width = weights.shape[3]
    capacity = min(tok_dev, max(2, 5 * tok_dev * top_count // (4 * experts_here)))
    item_total = tok_dev * top_count
    slot_total = experts_here * capacity
    flat_ids = expert_ids.reshape(item_total)
    onehot = (flat_ids[:, None] == jnp.arange(experts_here, dtype=jnp.int32)[None, :]).astype(
        jnp.bfloat16
    )
    item_number = jnp.arange(item_total, dtype=jnp.int32)
    earlier = (item_number[:, None] > item_number[None, :]).astype(jnp.bfloat16)
    before = jnp.dot(earlier, onehot, preferred_element_type=jnp.float32)
    slot_of = jnp.sum(before * onehot.astype(jnp.float32), axis=1).astype(jnp.int32)
    position = flat_ids * capacity + slot_of
    source = (
        jnp.full((slot_total,), item_total, jnp.int32)
        .at[position]
        .set(jnp.arange(item_total, dtype=jnp.int32))
    )
    token_of = source // top_count
    zero_row = jnp.zeros((1, model_width), jnp.bfloat16)
    x_send = jnp.concatenate([tokens, zero_row], axis=0)[token_of].reshape(
        experts_here, capacity, model_width
    )
    gate_flat = gate_weights.reshape(item_total)
    gate_pad = jnp.concatenate([gate_flat, jnp.zeros((1,), jnp.float32)])
    cot_rows = jnp.concatenate([cotangent, zero_row], axis=0)[token_of].astype(jnp.float32)
    dy_send = (
        (gate_pad[source][:, None] * cot_rows)
        .astype(jnp.bfloat16)
        .reshape(experts_here, capacity, model_width)
    )
    gathered = lax.all_gather(weights, "dp", axis=1, tiled=True)[0]
    gate_up = gathered[:, 0:2, :].reshape(model_width, 2 * hidden_width)
    down_proj = gathered[:, 2, :]
    block_shape = (experts_here, capacity, model_width)
    (x_recv,) = send_rows((x_send,))
    forward_x_rows = x_recv.reshape(slot_total, model_width)
    both_proj = jnp.dot(forward_x_rows, gate_up, preferred_element_type=jnp.float32)
    pre_act = both_proj[:, :hidden_width]
    lin_act = both_proj[:, hidden_width:]
    sigmoid_pre = jax.nn.sigmoid(pre_act)
    silu_pre = pre_act * sigmoid_pre
    forward_hidden = (silu_pre * lin_act).astype(jnp.bfloat16)
    out_rows = jnp.dot(forward_hidden, down_proj.T, preferred_element_type=jnp.float32).astype(
        jnp.bfloat16
    )
    x_rows, saved, hidden, out_rows = (
        forward_x_rows,
        (pre_act, lin_act, sigmoid_pre, silu_pre),
        forward_hidden,
        out_rows,
    )
    (out_back,) = send_back((out_rows.reshape(block_shape),))
    (dy_recv,) = send_rows((dy_send,))
    pre_act, lin_act, sigmoid_pre, silu_pre = saved
    backward_dy_rows = dy_recv.reshape(slot_total, model_width)
    hidden_grad = jnp.dot(backward_dy_rows, down_proj, preferred_element_type=jnp.float32)
    pre_grad = (hidden_grad * lin_act * sigmoid_pre * (1.0 + pre_act * (1.0 - sigmoid_pre))).astype(
        jnp.bfloat16
    )
    lin_grad = (hidden_grad * silu_pre).astype(jnp.bfloat16)
    backward_both_grad = jnp.concatenate([pre_grad, lin_grad], axis=1)
    item_grad = jnp.dot(backward_both_grad, gate_up.T, preferred_element_type=jnp.float32).astype(
        jnp.bfloat16
    )
    dy_rows, both_grad, item_grad = (backward_dy_rows, backward_both_grad, item_grad)
    (grad_back,) = send_back((item_grad.reshape(block_shape),))
    out_items = (
        out_back.reshape(slot_total, model_width)[position].astype(jnp.float32) * gate_flat[:, None]
    )
    mixed = jnp.sum(out_items.reshape(tok_dev, top_count, model_width), axis=1).astype(jnp.bfloat16)
    grad_items = grad_back.reshape(slot_total, model_width)[position].astype(jnp.float32)
    token_grad = jnp.sum(grad_items.reshape(tok_dev, top_count, model_width), axis=1).astype(
        jnp.bfloat16
    )
    count = lax.axis_size("dp") * weights.shape[1]
    proj_grad = jnp.dot(x_rows.T, both_grad, preferred_element_type=jnp.float32)
    down_grad = jnp.dot(dy_rows.T, hidden, preferred_element_type=jnp.float32)
    grad_sum = lax.psum_scatter(
        jnp.concatenate(
            [proj_grad.reshape(count, 2, hidden_width), down_grad.reshape(count, 1, hidden_width)],
            axis=1,
        ).astype(jnp.bfloat16),
        "dp",
        scatter_dimension=0,
        tiled=True,
    ).astype(jnp.float32)
    w_old = weights[0].astype(jnp.float32)
    m_old = first_moment[0].astype(jnp.float32)
    v_old = second_moment[0].astype(jnp.float32)
    m_new = beta_one * m_old + (1.0 - beta_one) * grad_sum
    v_new = beta_two * v_old + (1.0 - beta_two) * grad_sum * grad_sum
    m_hat = m_new / (1.0 - beta_one**step_count)
    v_hat = v_new / (1.0 - beta_two**step_count)
    w_new = w_old - learn_rate * (m_hat / (jnp.sqrt(v_hat) + eps_adam) + decay_rate * w_old)
    pieces = (
        w_new.astype(jnp.bfloat16).reshape(experts_here, -1),
        m_new.astype(jnp.bfloat16).reshape(experts_here, -1),
        v_new.astype(jnp.bfloat16).reshape(experts_here, -1),
    )
    spread = (
        lax.all_to_all(pieces[0], "expert", split_axis=0, concat_axis=0, tiled=True),
        lax.all_to_all(pieces[1], "expert", split_axis=0, concat_axis=0, tiled=True),
        lax.all_to_all(pieces[2], "expert", split_axis=0, concat_axis=0, tiled=True),
    )
    ordered = (spread[0][partner], spread[1][partner], spread[2][partner])
    homed = (
        lax.all_to_all(ordered[0], "expert", split_axis=0, concat_axis=0, tiled=True),
        lax.all_to_all(ordered[1], "expert", split_axis=0, concat_axis=0, tiled=True),
        lax.all_to_all(ordered[2], "expert", split_axis=0, concat_axis=0, tiled=True),
    )
    new_weights = homed[0].reshape(weights.shape)
    new_first = homed[1].reshape(weights.shape)
    new_second = homed[2].reshape(weights.shape)
    return (mixed, token_grad, new_weights, new_first, new_second)


def adam(w_old, m_old, v_old, grad_sum):
    m_new = beta_one * m_old + (1.0 - beta_one) * grad_sum
    v_new = beta_two * v_old + (1.0 - beta_two) * grad_sum * grad_sum
    m_hat = m_new / (1.0 - beta_one**step_count)
    v_hat = v_new / (1.0 - beta_two**step_count)
    w_new = w_old - learn_rate * (m_hat / (jnp.sqrt(v_hat) + eps_adam) + decay_rate * w_old)
    return w_new, m_new, v_new


def plane_barrier(n, me):
    barrier = pltpu.get_barrier_semaphore()

    def body(step, carry):
        pl.semaphore_signal(
            barrier,
            inc=1,
            device_id={"expert": lax.rem(me + step, n)},
            device_id_type=pl.DeviceIdType.MESH,
        )
        return carry

    lax.fori_loop(1, n, body, 0)
    pl.semaphore_signal(
        barrier,
        inc=1,
        device_id={"dp": 1 - lax.axis_index("dp")},
        device_id_type=pl.DeviceIdType.MESH,
    )
    pl.semaphore_wait(barrier, n)


def remote(src, dst, send_sem, recv_sem, **where):
    return pltpu.make_async_remote_copy(
        src_ref=src,
        dst_ref=dst,
        send_sem=send_sem,
        recv_sem=recv_sem,
        device_id=where,
        device_id_type=pl.DeviceIdType.MESH,
    )


class Mover:
    def __init__(self, table, state, home, row_base, held, ordered, sems):
        self.table, self.state, self.home, self.row_base = table, state, home, row_base
        self.held, self.ordered = held, ordered
        self.p1_send, self.p1_recv, self.b_send, self.b_recv, self.p2_send, self.p2_recv = sems
        me = lax.axis_index("expert")
        self.me = me
        self.z = me // 4
        self.lane = lax.rem(me, 4)
        self.half = me // 8
        self.inner = self.half + 1
        self.is_lane = self.z == self.inner
        self.quarter = state.shape[1] // 4

    def rows(self, q, base=0):
        return pl.ds(pl.multiple_of(base + q * self.quarter, 128), self.quarter)

    def one(self, q):
        dest = self.inner * 4 + q
        return remote(
            self.state.at[:, self.rows(q), :],
            self.held.at[lax.rem(self.me, 8)],
            self.p1_send.at[q],
            self.p1_recv.at[lax.rem(self.me, 8)],
            expert=dest,
        )

    def to_lanes(self):
        for q in range(4):
            dest = self.inner * 4 + q

            @pl.when(dest != self.me)
            def _():
                self.one(q).start()

            @pl.when(dest == self.me)
            def _():
                self.held[lax.rem(self.me, 8)] = self.state[:, self.rows(q), :]

    def two(self, slot):
        return remote(
            self.held.at[slot],
            self.held.at[8 + slot],
            self.b_send.at[slot],
            self.b_recv.at[slot],
            expert=(3 - self.inner) * 4 + self.lane,
        )

    def arrival(self, slot):
        return remote(
            self.held.at[slot],
            self.held.at[slot],
            self.p1_send.at[0],
            self.p1_recv.at[slot],
            expert=lax.rem(self.me + 1, 16),
        )

    def cross(self):
        @pl.when(self.is_lane)
        def _():
            for slot in range(8):

                @pl.when(slot != lax.rem(self.me, 8))
                def _():
                    self.arrival(slot).wait_recv()

                self.two(slot).start()

    def three(self, d):
        return remote(
            self.ordered.at[d],
            self.home.at[:, self.rows(self.lane, self.row_base), :],
            self.p2_send.at[d],
            self.p2_recv.at[self.lane],
            expert=self.half * 8 + d,
        )

    def to_homes(self):
        @pl.when(self.is_lane)
        def _():
            for slot in range(8):
                self.two(slot).wait_recv()

            for d in range(8):
                self.ordered[d] = self.held[self.table[d]]
                here = d == lax.rem(self.me, 8)

                @pl.when(jnp.logical_not(here))
                def _():
                    self.three(d).start()

                @pl.when(here)
                def _():
                    self.home[:, self.rows(self.lane, self.row_base), :] = self.ordered[d]

    def at_home(self, q):
        @pl.when(self.inner * 4 + q != self.me)
        def _():
            part = self.home.at[:, self.rows(q, self.row_base), :]
            remote(
                part, part, self.p2_send.at[0], self.p2_recv.at[q], expert=lax.rem(self.me + 1, 16)
            ).wait_recv()

    def sends_done(self):
        for q in range(4):

            @pl.when(self.inner * 4 + q != self.me)
            def _():
                self.one(q).wait_send()

        @pl.when(self.is_lane)
        def _():
            for slot in range(8):
                self.two(slot).wait_send()

            for d in range(8):

                @pl.when(d != lax.rem(self.me, 8))
                def _():
                    self.three(d).wait_send()


def mover_scratch(shape):
    planes, own_rows, width = shape
    part = (planes, own_rows // 4, width)
    return [
        pltpu.VMEM((16, *part), jnp.bfloat16),
        pltpu.VMEM((8, *part), jnp.bfloat16),
        pltpu.SemaphoreType.DMA((4,)),
        pltpu.SemaphoreType.DMA((8,)),
        pltpu.SemaphoreType.DMA((8,)),
        pltpu.SemaphoreType.DMA((8,)),
        pltpu.SemaphoreType.DMA((8,)),
        pltpu.SemaphoreType.DMA((4,)),
    ]


def gather_kernel(table, x, cot, gates, w, m, x_all, cot_all, gate_all, w_full, m_home, *scratch):
    me = lax.axis_index("expert")
    half = lax.axis_index("dp")
    own_rows = w.shape[1]
    z, y, core = me // 4, lax.rem(me // 2, 2), lax.rem(me, 2)
    w_move = Mover(table, w, w_full, half * own_rows, scratch[0], scratch[1], scratch[2:8])
    m_move = Mover(table, m, m_home, 0, scratch[8], scratch[9], scratch[10:16])
    block_recv, z_send, y_send, c_send, x_send, x_recv = scratch[16:]
    arrays = ((x, x_all), (cot, cot_all), (gates, gate_all))

    def hop(i, number, own, send_sem, dest):
        source, full = arrays[i]
        return remote(
            source if own else full.at[number],
            full.at[number],
            send_sem,
            block_recv.at[i, number],
            expert=dest,
        )

    def number_of(zz, yy, cc):
        return zz * 4 + yy * 2 + cc

    def down(i, s):
        return hop(i, number_of(z + s, y, core), s == 0, z_send.at[i, 0, s], me - 4)

    def up(i, s):
        return hop(i, number_of(z - s, y, core), s == 0, z_send.at[i, 1, s], me + 4)

    def over(i, zz, own=False):
        return hop(i, number_of(zz, y, core), own, y_send.at[i, zz], number_of(z, 1 - y, core))

    def beside(i, zz, yy, own=False):
        return hop(
            i, number_of(zz, yy, core), own, c_send.at[i, zz * 2 + yy], number_of(z, y, 1 - core)
        )

    def wait_block(i, number):
        hop(i, number, False, y_send.at[i, 0], lax.rem(me + 1, 16)).wait_recv()

    def passed_on(zz):
        for i in range(3):
            over(i, zz).start()
        for i in range(3):
            beside(i, zz, y).start()

    def line_step(s):
        @pl.when(z + 1 + s <= 3)
        def _():
            for i in range(3):
                wait_block(i, number_of(z + 1 + s, y, core))
                if s < 2:

                    @pl.when(z >= 1)
                    def _():
                        down(i, s + 1).start()

            passed_on(z + 1 + s)

        @pl.when(z - 1 - s >= 0)
        def _():
            for i in range(3):
                wait_block(i, number_of(z - 1 - s, y, core))
                if s < 2:

                    @pl.when(z <= 2)
                    def _():
                        up(i, s + 1).start()

            passed_on(z - 1 - s)

    plane_barrier(16, me)
    w_move.to_lanes()
    for i in range(3):

        @pl.when(z >= 1)
        def _():
            down(i, 0).start()

        @pl.when(z <= 2)
        def _():
            up(i, 0).start()

        over(i, z, True).start()
        beside(i, z, y, True).start()
    m_move.to_lanes()
    x_all[me] = x[...]
    cot_all[me] = cot[...]
    gate_all[me] = gates[...]
    line_step(0)
    w_move.cross()
    line_step(1)
    m_move.cross()
    w_move.to_homes()
    line_step(2)

    def from_over(zz):
        for i in range(3):
            wait_block(i, number_of(zz, 1 - y, core))
            beside(i, zz, 1 - y).start()

    from_over(z)
    for s in range(3):

        @pl.when(z + 1 + s <= 3)
        def _():
            from_over(z + 1 + s)

        @pl.when(z - 1 - s >= 0)
        def _():
            from_over(z - 1 - s)

    def exchange(q):
        part = w_full.at[:, w_move.rows(q, half * own_rows), :]
        return remote(part, part, x_send.at[q], x_recv.at[q], dp=1 - half)

    for q in range(4):
        w_move.at_home(q)
        exchange(q).start()
    m_move.to_homes()
    for zz in range(4):
        for yy in range(2):
            for i in range(3):
                wait_block(i, number_of(zz, yy, 1 - core))
    for q in range(4):
        part = w_full.at[:, w_move.rows(q, (1 - half) * own_rows), :]
        remote(part, part, x_send.at[q], x_recv.at[q], dp=1 - half).wait_recv()
        m_move.at_home(q)
    for q in range(4):
        exchange(q).wait_send()
    w_move.sends_done()
    m_move.sends_done()
    for i in range(3):
        for s in range(3):

            @pl.when(jnp.logical_and(z >= 1, z + s <= 3))
            def _():
                down(i, s).wait_send()

            @pl.when(jnp.logical_and(z <= 2, z - s >= 0))
            def _():
                up(i, s).wait_send()

        for zz in range(4):
            over(i, zz).wait_send()
            for yy in range(2):
                beside(i, zz, yy).wait_send()


def gather_all(table, x, cot, gates, w, m):
    n = lax.axis_size("expert")
    vmem = pl.BlockSpec(memory_space=pltpu.VMEM)
    planes, own_rows, width = w.shape
    outs = [
        jax.ShapeDtypeStruct((n, *x.shape), x.dtype),
        jax.ShapeDtypeStruct((n, *cot.shape), cot.dtype),
        jax.ShapeDtypeStruct((n, *gates.shape), gates.dtype),
        jax.ShapeDtypeStruct((planes, 2 * own_rows, width), w.dtype),
        jax.ShapeDtypeStruct(m.shape, m.dtype),
    ]
    return pl.pallas_call(
        gather_kernel,
        out_shape=outs,
        in_specs=[pl.BlockSpec(memory_space=pltpu.SMEM)] + [vmem] * 5,
        out_specs=[vmem] * 5,
        scratch_shapes=[
            *mover_scratch(w.shape),
            *mover_scratch(m.shape),
            pltpu.SemaphoreType.DMA((3, n)),
            pltpu.SemaphoreType.DMA((3, 2, 3)),
            pltpu.SemaphoreType.DMA((3, 4)),
            pltpu.SemaphoreType.DMA((3, 8)),
            pltpu.SemaphoreType.DMA((4,)),
            pltpu.SemaphoreType.DMA((4,)),
        ],
        compiler_params=pltpu.CompilerParams(
            collective_id=0, has_side_effects=True, vmem_limit_bytes=44 * 2**20
        ),
        cost_estimate=pl.CostEstimate(flops=0, bytes_accessed=200 * 2**20, transcendentals=0),
    )(table, x, cot, gates, w, m)


def layer_kernel(
    table, x_all, cot_all, gate, w_full, v, mixed, token_grad, keep, given, v_home, *scratch
):
    f32, bf16 = jnp.float32, jnp.bfloat16
    me = lax.axis_index("expert")
    half = lax.axis_index("dp")
    own_rows = v.shape[1]
    width = v.shape[2]
    z, y, core = me // 4, lax.rem(me // 2, 2), lax.rem(me, 2)
    v_move = Mover(table, v, v_home, 0, scratch[0], scratch[1], scratch[2:8])
    dy_all, both_all, hidden_all, part, from_core, from_over, from_line, give = scratch[8:16]
    c_send, c_recv, y_send, y_recv, l_send, l_recv, g_send, g_recv = scratch[16:]
    tok = part.shape[3]

    def to_core(i, b):
        return remote(
            part.at[i, b, 1 - core],
            from_core.at[i, b],
            c_send.at[i, b],
            c_recv.at[i, b],
            expert=z * 4 + y * 2 + 1 - core,
        )

    def to_over(i, zz):
        return remote(
            part.at[i, zz * 2 + 1 - y, core],
            from_over.at[i, zz],
            y_send.at[i, zz],
            y_recv.at[i, zz],
            expert=z * 4 + (1 - y) * 2 + core,
        )

    def on_line(i, zz, way):
        return remote(
            part.at[i, zz * 2 + y, core],
            from_line.at[i, zz, way],
            l_send.at[i, zz],
            l_recv.at[i, zz, way],
            expert=me + (4 if way else -4),
        )

    def added(i, b, source):
        part[i, b, core] = (part[i, b, core].astype(f32) + source.astype(f32)).astype(bf16)

    def place(t):
        mid = jnp.where(t <= 1, 3 - t, t - 2)
        return jnp.where(z == 0, 3 - t, jnp.where(z == 1, mid, jnp.where(z == 2, 3 - mid, t)))

    def chip_of(t):
        over = t < 4
        return place(lax.rem(t, 4)) * 2 + jnp.where(over, 1 - y, y)

    def block_step(t):
        b = chip_of(t)
        rows = pl.ds(pl.multiple_of(b * 2 * tok, 256), 2 * tok)
        x_rows = x_all[rows, :]
        g_rows = gate[rows, :]
        pre_act = jnp.dot(x_rows, w_full[0], preferred_element_type=f32)
        lin_act = jnp.dot(x_rows, w_full[1], preferred_element_type=f32)
        sig = jax.nn.sigmoid(pre_act)
        silu = pre_act * sig
        hidden = (silu * lin_act).astype(bf16)
        hidden_all[rows, :] = hidden
        last = (((1,), (1,)), ((), ()))
        out = lax.dot_general(hidden, w_full[2], last, preferred_element_type=f32)
        part[0, b] = (g_rows * out).astype(bf16).reshape(2, tok, out.shape[1])
        dy = (g_rows * cot_all[rows, :].astype(f32)).astype(bf16)
        dy_all[rows, :] = dy
        hidden_grad = jnp.dot(dy, w_full[2], preferred_element_type=f32)
        pre_grad = (hidden_grad * lin_act * sig * (1.0 + pre_act * (1.0 - sig))).astype(bf16)
        lin_grad = (hidden_grad * silu).astype(bf16)
        both_all[0, rows, :] = pre_grad
        both_all[1, rows, :] = lin_grad
        item = lax.dot_general(pre_grad, w_full[0], last, preferred_element_type=f32)
        item = item + lax.dot_general(lin_grad, w_full[1], last, preferred_element_type=f32)
        part[1, b] = item.astype(bf16).reshape(2, tok, out.shape[1])
        for i in range(2):
            to_core(i, b).start()

    def core_sum(t):
        b = chip_of(t)
        for i in range(2):
            to_core(i, b).wait_recv()
            added(i, b, from_core[i, b])

            @pl.when(t < 4)
            def _():
                to_over(i, b // 2).start()

    plane_barrier(16, me)
    v_move.to_lanes()

    def step(t, carry):
        block_step(t)

        @pl.when(t >= 1)
        def _():
            core_sum(t - 1)

        return carry

    lax.fori_loop(0, 8, step, 0)
    core_sum(7)
    v_move.cross()

    tile = own_rows // 2

    def weight_grads(base, put):
        def body(j, carry):
            rows = pl.ds(pl.multiple_of(base + j * tile, 256), tile)
            first = (((0,), (0,)), ((), ()))
            x_cols = x_all[:, rows]
            dy_cols = dy_all[:, rows]
            put(0, j, lax.dot_general(x_cols, both_all[0], first, preferred_element_type=f32))
            put(1, j, lax.dot_general(x_cols, both_all[1], first, preferred_element_type=f32))
            put(2, j, lax.dot_general(dy_cols, hidden_all[...], first, preferred_element_type=f32))
            return carry

        lax.fori_loop(0, 2, body, 0)

    def gift(j):
        rows = pl.ds(pl.multiple_of(j * tile, 256), tile)
        return remote(
            give.at[:, rows, :], given.at[:, rows, :], g_send.at[j], g_recv.at[j], dp=1 - half
        )

    def put_give(plane, j, value):
        give[plane, pl.ds(pl.multiple_of(j * tile, 256), tile), :] = value.astype(bf16)
        if plane == 2:
            gift(j).start()

    def put_keep(plane, j, value):
        keep[plane, pl.ds(pl.multiple_of(j * tile, 256), tile), :] = value.astype(bf16)

    weight_grads((1 - half) * own_rows, put_give)
    weight_grads(half * own_rows, put_keep)
    v_move.to_homes()

    def over_sum(i, zz):
        to_over(i, zz).wait_recv()
        added(i, zz * 2 + y, from_over[i, zz])

    for far in (3, 2, 1):
        for way in (1, 0):
            zz = z + far if way else z - far
            inside = zz <= 3 if way else zz >= 0

            @pl.when(inside)
            def _():
                for i in range(2):
                    over_sum(i, zz)

                    @pl.when(z >= 1 if way else z <= 2)
                    def _():
                        on_line(i, zz, way).wait_recv()
                        added(i, zz * 2 + y, from_line[i, zz, way])

                    on_line(i, zz, way).start()

    for i, out in ((0, mixed), (1, token_grad)):
        over_sum(i, z)

        @pl.when(z >= 1)
        def _():
            on_line(i, z, 1).wait_recv()
            added(i, z * 2 + y, from_line[i, z, 1])

        @pl.when(z <= 2)
        def _():
            on_line(i, z, 0).wait_recv()
            added(i, z * 2 + y, from_line[i, z, 0])

        out[...] = part[i, z * 2 + y, core]
    for q in range(4):
        v_move.at_home(q)
    for j in range(2):
        gift(j).wait()
    v_move.sends_done()
    for i in range(2):
        for b in range(8):
            to_core(i, b).wait_send()
        for zz in range(4):
            to_over(i, zz).wait_send()

            @pl.when(zz != z)
            def _():
                on_line(i, zz, 1).wait_send()


def layer(table, x_all, cot_all, gate, w_full, v):
    n = lax.axis_size("expert")
    vmem = pl.BlockSpec(memory_space=pltpu.VMEM)
    rows, model = x_all.shape
    tok = rows // n
    width = v.shape[2]
    bf16 = jnp.bfloat16
    outs = [
        jax.ShapeDtypeStruct((tok, model), bf16),
        jax.ShapeDtypeStruct((tok, model), bf16),
        jax.ShapeDtypeStruct(v.shape, bf16),
        jax.ShapeDtypeStruct(v.shape, bf16),
        jax.ShapeDtypeStruct(v.shape, bf16),
    ]
    return pl.pallas_call(
        layer_kernel,
        out_shape=outs,
        in_specs=[pl.BlockSpec(memory_space=pltpu.SMEM)] + [vmem] * 5,
        out_specs=[vmem] * 5,
        scratch_shapes=[
            *mover_scratch(v.shape),
            pltpu.VMEM((rows, model), bf16),
            pltpu.VMEM((2, rows, width), bf16),
            pltpu.VMEM((rows, width), bf16),
            pltpu.VMEM((2, n // 2, 2, tok, model), bf16),
            pltpu.VMEM((2, n // 2, tok, model), bf16),
            pltpu.VMEM((2, 4, tok, model), bf16),
            pltpu.VMEM((2, 4, 2, tok, model), bf16),
            pltpu.VMEM(v.shape, bf16),
            pltpu.SemaphoreType.DMA((2, 8)),
            pltpu.SemaphoreType.DMA((2, 8)),
            pltpu.SemaphoreType.DMA((2, 4)),
            pltpu.SemaphoreType.DMA((2, 4)),
            pltpu.SemaphoreType.DMA((2, 4)),
            pltpu.SemaphoreType.DMA((2, 4, 2)),
            pltpu.SemaphoreType.DMA((2,)),
            pltpu.SemaphoreType.DMA((2,)),
        ],
        compiler_params=pltpu.CompilerParams(
            collective_id=1, has_side_effects=True, vmem_limit_bytes=60 * 2**20
        ),
        cost_estimate=pl.CostEstimate(
            flops=15 * 10**9, bytes_accessed=100 * 2**20, transcendentals=0
        ),
    )(table, x_all, cot_all, gate, w_full, v)


def shards_dense(
    tokens, cotangent, expert_ids, gate_weights, partner, weights, first_moment, second_moment
):
    n = lax.axis_size("expert")
    tok, model = tokens.shape
    f32, bf16 = jnp.float32, jnp.bfloat16
    me = lax.axis_index("expert")
    hits = expert_ids[:, :, None] == jnp.arange(n, dtype=jnp.int32)[None, None, :]
    gates = jnp.sum(jnp.where(hits, gate_weights[:, :, None], 0.0), axis=1).T
    side = me // 8
    mine = lax.dynamic_slice_in_dim(partner, side * 8, 8)
    table = lax.rem(mine, 8) + jnp.where(mine // 8 == side, 0, 8)
    old = [a[0].transpose(1, 0, 2) for a in (weights, first_moment, second_moment)]
    x_all, cot_all, gate_all, w_full, m_here = gather_all(
        table, tokens, cotangent, gates, old[0], old[1]
    )
    gate = lax.dynamic_index_in_dim(gate_all, partner[me], 1, keepdims=False)
    mixed, token_grad, keep, given, v_here = layer(
        table,
        x_all.reshape(n * tok, model),
        cot_all.reshape(n * tok, model),
        gate.reshape(n * tok, 1),
        w_full,
        old[2],
    )
    w_here = lax.dynamic_slice_in_dim(w_full, lax.axis_index("dp") * old[0].shape[1], old[0].shape[1], axis=1)
    grad = keep.astype(f32) + given.astype(f32)
    new_state = adam(*[a.astype(f32) for a in (w_here, m_here, v_here)], grad)
    outs = [a.astype(bf16).transpose(1, 0, 2)[None] for a in new_state]
    return (mixed, token_grad, *outs)


def shards(*args):
    fits = lax.axis_size("dp") == 2 and lax.axis_size("expert") == 16
    if fits and args[0].shape[0] == 128 and args[5].shape[1] % 512 == 0:
        return shards_dense(*args)
    return shards_by_slot(*args)


def solution(mesh):
    in_specs = (
        P(("dp", "expert"), None),
        P(("dp", "expert"), None),
        P(("dp", "expert"), None),
        P(("dp", "expert"), None),
        P(),
        P("expert", "dp", None, None),
        P("expert", "dp", None, None),
        P("expert", "dp", None, None),
    )
    out_specs = (
        P(("dp", "expert"), None),
        P(("dp", "expert"), None),
        P("expert", "dp", None, None),
        P("expert", "dp", None, None),
        P("expert", "dp", None, None),
    )
    return jax.shard_map(shards, mesh=mesh, in_specs=in_specs, out_specs=out_specs, check_vma=False)
```

```python
import functools

import jax
import jax.numpy as jnp
from jax import lax
from jax.experimental import pallas as pl
from jax.experimental.pallas import tpu as pltpu
from jax.sharding import PartitionSpec as P

beta_one = 0.9
beta_two = 0.95
learn_rate = 0.01
decay_rate = 0.1
eps_adam = 1e-08
step_count = 100


def send_rows(parts):
    return (lax.all_to_all(parts[0], "expert", split_axis=0, concat_axis=0, tiled=True),)


def send_back(parts):
    return (lax.all_to_all(parts[0], "expert", split_axis=0, concat_axis=0, tiled=True),)


def shards_by_slot(
    tokens, cotangent, expert_ids, gate_weights, partner, weights, first_moment, second_moment
):
    experts_here = lax.axis_size("expert")
    tok_dev, model_width = tokens.shape
    top_count = expert_ids.shape[1]
    hidden_width = weights.shape[3]
    capacity = min(tok_dev, max(2, 5 * tok_dev * top_count // (4 * experts_here)))
    item_total = tok_dev * top_count
    slot_total = experts_here * capacity
    flat_ids = expert_ids.reshape(item_total)
    onehot = (flat_ids[:, None] == jnp.arange(experts_here, dtype=jnp.int32)[None, :]).astype(
        jnp.bfloat16
    )
    item_number = jnp.arange(item_total, dtype=jnp.int32)
    earlier = (item_number[:, None] > item_number[None, :]).astype(jnp.bfloat16)
    before = jnp.dot(earlier, onehot, preferred_element_type=jnp.float32)
    slot_of = jnp.sum(before * onehot.astype(jnp.float32), axis=1).astype(jnp.int32)
    position = flat_ids * capacity + slot_of
    source = (
        jnp.full((slot_total,), item_total, jnp.int32)
        .at[position]
        .set(jnp.arange(item_total, dtype=jnp.int32))
    )
    token_of = source // top_count
    zero_row = jnp.zeros((1, model_width), jnp.bfloat16)
    x_send = jnp.concatenate([tokens, zero_row], axis=0)[token_of].reshape(
        experts_here, capacity, model_width
    )
    gate_flat = gate_weights.reshape(item_total)
    gate_pad = jnp.concatenate([gate_flat, jnp.zeros((1,), jnp.float32)])
    cot_rows = jnp.concatenate([cotangent, zero_row], axis=0)[token_of].astype(jnp.float32)
    dy_send = (
        (gate_pad[source][:, None] * cot_rows)
        .astype(jnp.bfloat16)
        .reshape(experts_here, capacity, model_width)
    )
    gathered = lax.all_gather(weights, "dp", axis=1, tiled=True)[0]
    gate_up = gathered[:, 0:2, :].reshape(model_width, 2 * hidden_width)
    down_proj = gathered[:, 2, :]
    block_shape = (experts_here, capacity, model_width)
    (x_recv,) = send_rows((x_send,))
    forward_x_rows = x_recv.reshape(slot_total, model_width)
    both_proj = jnp.dot(forward_x_rows, gate_up, preferred_element_type=jnp.float32)
    pre_act = both_proj[:, :hidden_width]
    lin_act = both_proj[:, hidden_width:]
    sigmoid_pre = jax.nn.sigmoid(pre_act)
    silu_pre = pre_act * sigmoid_pre
    forward_hidden = (silu_pre * lin_act).astype(jnp.bfloat16)
    out_rows = jnp.dot(forward_hidden, down_proj.T, preferred_element_type=jnp.float32).astype(
        jnp.bfloat16
    )
    x_rows, saved, hidden, out_rows = (
        forward_x_rows,
        (pre_act, lin_act, sigmoid_pre, silu_pre),
        forward_hidden,
        out_rows,
    )
    (out_back,) = send_back((out_rows.reshape(block_shape),))
    (dy_recv,) = send_rows((dy_send,))
    pre_act, lin_act, sigmoid_pre, silu_pre = saved
    backward_dy_rows = dy_recv.reshape(slot_total, model_width)
    hidden_grad = jnp.dot(backward_dy_rows, down_proj, preferred_element_type=jnp.float32)
    pre_grad = (hidden_grad * lin_act * sigmoid_pre * (1.0 + pre_act * (1.0 - sigmoid_pre))).astype(
        jnp.bfloat16
    )
    lin_grad = (hidden_grad * silu_pre).astype(jnp.bfloat16)
    backward_both_grad = jnp.concatenate([pre_grad, lin_grad], axis=1)
    item_grad = jnp.dot(backward_both_grad, gate_up.T, preferred_element_type=jnp.float32).astype(
        jnp.bfloat16
    )
    dy_rows, both_grad, item_grad = (backward_dy_rows, backward_both_grad, item_grad)
    (grad_back,) = send_back((item_grad.reshape(block_shape),))
    out_items = (
        out_back.reshape(slot_total, model_width)[position].astype(jnp.float32) * gate_flat[:, None]
    )
    mixed = jnp.sum(out_items.reshape(tok_dev, top_count, model_width), axis=1).astype(jnp.bfloat16)
    grad_items = grad_back.reshape(slot_total, model_width)[position].astype(jnp.float32)
    token_grad = jnp.sum(grad_items.reshape(tok_dev, top_count, model_width), axis=1).astype(
        jnp.bfloat16
    )
    count = lax.axis_size("dp") * weights.shape[1]
    proj_grad = jnp.dot(x_rows.T, both_grad, preferred_element_type=jnp.float32)
    down_grad = jnp.dot(dy_rows.T, hidden, preferred_element_type=jnp.float32)
    grad_sum = lax.psum_scatter(
        jnp.concatenate(
            [proj_grad.reshape(count, 2, hidden_width), down_grad.reshape(count, 1, hidden_width)],
            axis=1,
        ).astype(jnp.bfloat16),
        "dp",
        scatter_dimension=0,
        tiled=True,
    ).astype(jnp.float32)
    w_old = weights[0].astype(jnp.float32)
    m_old = first_moment[0].astype(jnp.float32)
    v_old = second_moment[0].astype(jnp.float32)
    m_new = beta_one * m_old + (1.0 - beta_one) * grad_sum
    v_new = beta_two * v_old + (1.0 - beta_two) * grad_sum * grad_sum
    m_hat = m_new / (1.0 - beta_one**step_count)
    v_hat = v_new / (1.0 - beta_two**step_count)
    w_new = w_old - learn_rate * (m_hat / (jnp.sqrt(v_hat) + eps_adam) + decay_rate * w_old)
    pieces = (
        w_new.astype(jnp.bfloat16).reshape(experts_here, -1),
        m_new.astype(jnp.bfloat16).reshape(experts_here, -1),
        v_new.astype(jnp.bfloat16).reshape(experts_here, -1),
    )
    spread = (
        lax.all_to_all(pieces[0], "expert", split_axis=0, concat_axis=0, tiled=True),
        lax.all_to_all(pieces[1], "expert", split_axis=0, concat_axis=0, tiled=True),
        lax.all_to_all(pieces[2], "expert", split_axis=0, concat_axis=0, tiled=True),
    )
    ordered = (spread[0][partner], spread[1][partner], spread[2][partner])
    homed = (
        lax.all_to_all(ordered[0], "expert", split_axis=0, concat_axis=0, tiled=True),
        lax.all_to_all(ordered[1], "expert", split_axis=0, concat_axis=0, tiled=True),
        lax.all_to_all(ordered[2], "expert", split_axis=0, concat_axis=0, tiled=True),
    )
    new_weights = homed[0].reshape(weights.shape)
    new_first = homed[1].reshape(weights.shape)
    new_second = homed[2].reshape(weights.shape)
    return (mixed, token_grad, new_weights, new_first, new_second)


def adam(w_old, m_old, v_old, grad_sum):
    m_new = beta_one * m_old + (1.0 - beta_one) * grad_sum
    v_new = beta_two * v_old + (1.0 - beta_two) * grad_sum * grad_sum
    m_hat = m_new / (1.0 - beta_one**step_count)
    v_hat = v_new / (1.0 - beta_two**step_count)
    w_new = w_old - learn_rate * (m_hat / (jnp.sqrt(v_hat) + eps_adam) + decay_rate * w_old)
    return w_new, m_new, v_new


def plane_barrier(n, me):
    barrier = pltpu.get_barrier_semaphore()

    def body(step, carry):
        pl.semaphore_signal(
            barrier,
            inc=1,
            device_id={"expert": lax.rem(me + step, n)},
            device_id_type=pl.DeviceIdType.MESH,
        )
        return carry

    lax.fori_loop(1, n, body, 0)
    pl.semaphore_signal(
        barrier,
        inc=1,
        device_id={"dp": 1 - lax.axis_index("dp")},
        device_id_type=pl.DeviceIdType.MESH,
    )
    pl.semaphore_wait(barrier, n)


def remote(src, dst, send_sem, recv_sem, **where):
    return pltpu.make_async_remote_copy(
        src_ref=src,
        dst_ref=dst,
        send_sem=send_sem,
        recv_sem=recv_sem,
        device_id=where,
        device_id_type=pl.DeviceIdType.MESH,
    )


class Mover:
    def __init__(self, partner, state, home, row_base, spread, ordered, sems):
        self.partner, self.state, self.home, self.row_base = partner, state, home, row_base
        self.spread, self.ordered = spread, ordered
        self.one_send, self.one_recv, self.two_send, self.two_recv = sems
        self.me = lax.axis_index("expert")
        self.n = spread.shape[0]
        self.share = state.shape[1] // self.n

    def rows(self, number, base=0):
        return pl.ds(pl.multiple_of(base + number * self.share, self.share), self.share)

    def each(self, fn):
        def body(step, carry):
            fn(step, lax.rem(self.me + step, self.n))
            return carry

        lax.fori_loop(1, self.n, body, 0)

    def one(self, step, peer):
        return remote(
            self.state.at[:, self.rows(peer), :],
            self.spread.at[self.me],
            self.one_send.at[step],
            self.one_recv.at[step],
            expert=peer,
        )

    def two(self, step, peer):
        return remote(
            self.ordered.at[peer],
            self.home.at[:, self.rows(self.me, self.row_base), :],
            self.two_send.at[step],
            self.two_recv.at[step],
            expert=peer,
        )

    def spread_out(self):
        self.each(lambda step, peer: self.one(step, peer).start())
        self.spread[self.me] = self.state[:, self.rows(self.me), :]

    def send_home(self):
        self.each(lambda step, peer: self.one(step, peer).wait_recv())

        def pick(step, carry):
            peer = lax.rem(self.me + step, self.n)
            self.ordered[peer] = self.spread[self.partner[peer]]
            self.two(step, peer).start()
            return carry

        lax.fori_loop(1, self.n, pick, 0)
        self.home[:, self.rows(self.me, self.row_base), :] = self.spread[self.partner[self.me]]

    def at_home(self):
        self.each(lambda step, peer: self.two(step, peer).wait_recv())

    def sends_done(self):
        self.each(lambda step, peer: self.one(step, peer).wait_send())
        self.each(lambda step, peer: self.two(step, peer).wait_send())


def mover_scratch(shape, n):
    planes, own_rows, width = shape
    part = (n, planes, own_rows // n, width)
    return [pltpu.VMEM(part, jnp.bfloat16)] * 2 + [pltpu.SemaphoreType.DMA((n,))] * 4


def gather_kernel(table, x, cot, gates, w, m, x_all, cot_all, gate_all, w_full, m_home, *scratch):
    me = lax.axis_index("expert")
    half = lax.axis_index("dp")
    own_rows = w.shape[1]
    z, y, core = me // 4, lax.rem(me // 2, 2), lax.rem(me, 2)
    w_move = Mover(table, w, w_full, half * own_rows, *scratch[:2], scratch[2:6])
    m_move = Mover(table, m, m_home, 0, *scratch[6:8], scratch[8:12])
    block_recv, z_send, y_send, c_send, x_send, x_recv = scratch[12:]
    arrays = ((x, x_all), (cot, cot_all), (gates, gate_all))

    def hop(i, number, own, send_sem, dest):
        source, full = arrays[i]
        return remote(
            source if own else full.at[number],
            full.at[number],
            send_sem,
            block_recv.at[i, number],
            expert=dest,
        )

    def number_of(zz, yy, cc):
        return zz * 4 + yy * 2 + cc

    def down(i, s):
        return hop(i, number_of(z + s, y, core), s == 0, z_send.at[i, 0, s], me - 4)

    def up(i, s):
        return hop(i, number_of(z - s, y, core), s == 0, z_send.at[i, 1, s], me + 4)

    def over(i, zz, own=False):
        return hop(i, number_of(zz, y, core), own, y_send.at[i, zz], number_of(z, 1 - y, core))

    def beside(i, zz, yy, own=False):
        return hop(
            i, number_of(zz, yy, core), own, c_send.at[i, zz * 2 + yy], number_of(z, y, 1 - core)
        )

    def wait_block(i, number):
        hop(i, number, False, y_send.at[i, 0], lax.rem(me + 1, 16)).wait_recv()

    def passed_on(zz):
        for i in range(3):
            over(i, zz).start()
        for i in range(3):
            beside(i, zz, y).start()

    def line_step(s):
        @pl.when(z + 1 + s <= 3)
        def _():
            for i in range(3):
                wait_block(i, number_of(z + 1 + s, y, core))
                if s < 2:

                    @pl.when(z >= 1)
                    def _():
                        down(i, s + 1).start()

            passed_on(z + 1 + s)

        @pl.when(z - 1 - s >= 0)
        def _():
            for i in range(3):
                wait_block(i, number_of(z - 1 - s, y, core))
                if s < 2:

                    @pl.when(z <= 2)
                    def _():
                        up(i, s + 1).start()

            passed_on(z - 1 - s)

    plane_barrier(16, me)
    w_move.spread_out()
    for i in range(3):

        @pl.when(z >= 1)
        def _():
            down(i, 0).start()

        @pl.when(z <= 2)
        def _():
            up(i, 0).start()

        over(i, z, True).start()
        beside(i, z, y, True).start()
    m_move.spread_out()
    x_all[me] = x[...]
    cot_all[me] = cot[...]
    gate_all[me] = gates[...]
    line_step(0)
    w_move.send_home()
    line_step(1)
    line_step(2)

    def from_over(zz):
        for i in range(3):
            wait_block(i, number_of(zz, 1 - y, core))
            beside(i, zz, 1 - y).start()

    from_over(z)
    for s in range(3):

        @pl.when(z + 1 + s <= 3)
        def _():
            from_over(z + 1 + s)

        @pl.when(z - 1 - s >= 0)
        def _():
            from_over(z - 1 - s)

    m_move.send_home()
    w_move.at_home()

    def exchange():
        part = w_full.at[:, pl.ds(pl.multiple_of(half * own_rows, own_rows), own_rows), :]
        return remote(part, part, x_send, x_recv, dp=1 - half)

    exchange().start()
    for zz in range(4):
        for yy in range(2):
            for i in range(3):
                wait_block(i, number_of(zz, yy, 1 - core))
    m_move.at_home()
    exchange().wait()
    w_move.sends_done()
    m_move.sends_done()
    for i in range(3):
        for s in range(3):

            @pl.when(jnp.logical_and(z >= 1, z + s <= 3))
            def _():
                down(i, s).wait_send()

            @pl.when(jnp.logical_and(z <= 2, z - s >= 0))
            def _():
                up(i, s).wait_send()

        for zz in range(4):
            over(i, zz).wait_send()
            for yy in range(2):
                beside(i, zz, yy).wait_send()


def gather_all(table, x, cot, gates, w, m):
    n = lax.axis_size("expert")
    vmem = pl.BlockSpec(memory_space=pltpu.VMEM)
    planes, own_rows, width = w.shape
    outs = [
        jax.ShapeDtypeStruct((n, *x.shape), x.dtype),
        jax.ShapeDtypeStruct((n, *cot.shape), cot.dtype),
        jax.ShapeDtypeStruct((n, *gates.shape), gates.dtype),
        jax.ShapeDtypeStruct((planes, 2 * own_rows, width), w.dtype),
        jax.ShapeDtypeStruct(m.shape, m.dtype),
    ]
    return pl.pallas_call(
        gather_kernel,
        out_shape=outs,
        in_specs=[pl.BlockSpec(memory_space=pltpu.SMEM)] + [vmem] * 5,
        out_specs=[vmem] * 5,
        scratch_shapes=[
            *mover_scratch(w.shape, n),
            *mover_scratch(m.shape, n),
            pltpu.SemaphoreType.DMA((3, n)),
            pltpu.SemaphoreType.DMA((3, 2, 3)),
            pltpu.SemaphoreType.DMA((3, 4)),
            pltpu.SemaphoreType.DMA((3, 8)),
            pltpu.SemaphoreType.DMA,
            pltpu.SemaphoreType.DMA,
        ],
        compiler_params=pltpu.CompilerParams(
            collective_id=0, has_side_effects=True, vmem_limit_bytes=44 * 2**20
        ),
        cost_estimate=pl.CostEstimate(flops=0, bytes_accessed=200 * 2**20, transcendentals=0),
    )(table, x, cot, gates, w, m)


def layer_kernel(
    table, x_all, cot_all, gate, w_full, v, mixed, token_grad, keep, given, v_home, *scratch
):
    f32, bf16 = jnp.float32, jnp.bfloat16
    me = lax.axis_index("expert")
    half = lax.axis_index("dp")
    own_rows = v.shape[1]
    width = v.shape[2]
    z, y, core = me // 4, lax.rem(me // 2, 2), lax.rem(me, 2)
    v_move = Mover(table, v, v_home, 0, *scratch[:2], scratch[2:6])
    dy_all, both_all, hidden_all, part, from_core, from_over, from_line, give = scratch[6:14]
    c_send, c_recv, y_send, y_recv, l_send, l_recv, g_send, g_recv = scratch[14:]
    tok = part.shape[3]

    def to_core(i, b):
        return remote(
            part.at[i, b, 1 - core],
            from_core.at[i, b],
            c_send.at[i, b],
            c_recv.at[i, b],
            expert=z * 4 + y * 2 + 1 - core,
        )

    def to_over(i, zz):
        return remote(
            part.at[i, zz * 2 + 1 - y, core],
            from_over.at[i, zz],
            y_send.at[i, zz],
            y_recv.at[i, zz],
            expert=z * 4 + (1 - y) * 2 + core,
        )

    def on_line(i, zz, way):
        return remote(
            part.at[i, zz * 2 + y, core],
            from_line.at[i, zz, way],
            l_send.at[i, zz],
            l_recv.at[i, zz, way],
            expert=me + (4 if way else -4),
        )

    def added(i, b, source):
        part[i, b, core] = (part[i, b, core].astype(f32) + source.astype(f32)).astype(bf16)

    def place(t):
        mid = jnp.where(t <= 1, 3 - t, t - 2)
        return jnp.where(z == 0, 3 - t, jnp.where(z == 1, mid, jnp.where(z == 2, 3 - mid, t)))

    def chip_of(t):
        over = t < 4
        return place(lax.rem(t, 4)) * 2 + jnp.where(over, 1 - y, y)

    def block_step(t):
        b = chip_of(t)
        rows = pl.ds(pl.multiple_of(b * 2 * tok, 256), 2 * tok)
        x_rows = x_all[rows, :]
        g_rows = gate[rows, :]
        pre_act = jnp.dot(x_rows, w_full[0], preferred_element_type=f32)
        lin_act = jnp.dot(x_rows, w_full[1], preferred_element_type=f32)
        sig = jax.nn.sigmoid(pre_act)
        silu = pre_act * sig
        hidden = (silu * lin_act).astype(bf16)
        hidden_all[rows, :] = hidden
        last = (((1,), (1,)), ((), ()))
        out = lax.dot_general(hidden, w_full[2], last, preferred_element_type=f32)
        part[0, b] = (g_rows * out).astype(bf16).reshape(2, tok, out.shape[1])
        dy = (g_rows * cot_all[rows, :].astype(f32)).astype(bf16)
        dy_all[rows, :] = dy
        hidden_grad = jnp.dot(dy, w_full[2], preferred_element_type=f32)
        pre_grad = (hidden_grad * lin_act * sig * (1.0 + pre_act * (1.0 - sig))).astype(bf16)
        lin_grad = (hidden_grad * silu).astype(bf16)
        both_all[0, rows, :] = pre_grad
        both_all[1, rows, :] = lin_grad
        item = lax.dot_general(pre_grad, w_full[0], last, preferred_element_type=f32)
        item = item + lax.dot_general(lin_grad, w_full[1], last, preferred_element_type=f32)
        part[1, b] = item.astype(bf16).reshape(2, tok, out.shape[1])
        for i in range(2):
            to_core(i, b).start()

    def core_sum(t):
        b = chip_of(t)
        for i in range(2):
            to_core(i, b).wait_recv()
            added(i, b, from_core[i, b])

            @pl.when(t < 4)
            def _():
                to_over(i, b // 2).start()

    plane_barrier(16, me)
    v_move.spread_out()

    def step(t, carry):
        block_step(t)

        @pl.when(t >= 1)
        def _():
            core_sum(t - 1)

        return carry

    lax.fori_loop(0, 8, step, 0)
    core_sum(7)

    tile = own_rows // 2

    def weight_grads(base, put):
        def body(j, carry):
            rows = pl.ds(pl.multiple_of(base + j * tile, 256), tile)
            first = (((0,), (0,)), ((), ()))
            x_cols = x_all[:, rows]
            dy_cols = dy_all[:, rows]
            put(0, j, lax.dot_general(x_cols, both_all[0], first, preferred_element_type=f32))
            put(1, j, lax.dot_general(x_cols, both_all[1], first, preferred_element_type=f32))
            put(2, j, lax.dot_general(dy_cols, hidden_all[...], first, preferred_element_type=f32))
            return carry

        lax.fori_loop(0, 2, body, 0)

    def gift(j):
        rows = pl.ds(pl.multiple_of(j * tile, 256), tile)
        return remote(
            give.at[:, rows, :], given.at[:, rows, :], g_send.at[j], g_recv.at[j], dp=1 - half
        )

    def put_give(plane, j, value):
        give[plane, pl.ds(pl.multiple_of(j * tile, 256), tile), :] = value.astype(bf16)
        if plane == 2:
            gift(j).start()

    def put_keep(plane, j, value):
        keep[plane, pl.ds(pl.multiple_of(j * tile, 256), tile), :] = value.astype(bf16)

    weight_grads((1 - half) * own_rows, put_give)
    v_move.send_home()
    weight_grads(half * own_rows, put_keep)

    def over_sum(i, zz):
        to_over(i, zz).wait_recv()
        added(i, zz * 2 + y, from_over[i, zz])

    for far in (3, 2, 1):
        for way in (1, 0):
            zz = z + far if way else z - far
            inside = zz <= 3 if way else zz >= 0

            @pl.when(inside)
            def _():
                for i in range(2):
                    over_sum(i, zz)

                    @pl.when(z >= 1 if way else z <= 2)
                    def _():
                        on_line(i, zz, way).wait_recv()
                        added(i, zz * 2 + y, from_line[i, zz, way])

                    on_line(i, zz, way).start()

    for i, out in ((0, mixed), (1, token_grad)):
        over_sum(i, z)

        @pl.when(z >= 1)
        def _():
            on_line(i, z, 1).wait_recv()
            added(i, z * 2 + y, from_line[i, z, 1])

        @pl.when(z <= 2)
        def _():
            on_line(i, z, 0).wait_recv()
            added(i, z * 2 + y, from_line[i, z, 0])

        out[...] = part[i, z * 2 + y, core]
    v_move.at_home()
    for j in range(2):
        gift(j).wait()
    v_move.sends_done()
    for i in range(2):
        for b in range(8):
            to_core(i, b).wait_send()
        for zz in range(4):
            to_over(i, zz).wait_send()

            @pl.when(zz != z)
            def _():
                on_line(i, zz, 1).wait_send()


def layer(table, x_all, cot_all, gate, w_full, v):
    n = lax.axis_size("expert")
    vmem = pl.BlockSpec(memory_space=pltpu.VMEM)
    rows, model = x_all.shape
    tok = rows // n
    width = v.shape[2]
    bf16 = jnp.bfloat16
    outs = [
        jax.ShapeDtypeStruct((tok, model), bf16),
        jax.ShapeDtypeStruct((tok, model), bf16),
        jax.ShapeDtypeStruct(v.shape, bf16),
        jax.ShapeDtypeStruct(v.shape, bf16),
        jax.ShapeDtypeStruct(v.shape, bf16),
    ]
    return pl.pallas_call(
        layer_kernel,
        out_shape=outs,
        in_specs=[pl.BlockSpec(memory_space=pltpu.SMEM)] + [vmem] * 5,
        out_specs=[vmem] * 5,
        scratch_shapes=[
            *mover_scratch(v.shape, n),
            pltpu.VMEM((rows, model), bf16),
            pltpu.VMEM((2, rows, width), bf16),
            pltpu.VMEM((rows, width), bf16),
            pltpu.VMEM((2, n // 2, 2, tok, model), bf16),
            pltpu.VMEM((2, n // 2, tok, model), bf16),
            pltpu.VMEM((2, 4, tok, model), bf16),
            pltpu.VMEM((2, 4, 2, tok, model), bf16),
            pltpu.VMEM(v.shape, bf16),
            pltpu.SemaphoreType.DMA((2, 8)),
            pltpu.SemaphoreType.DMA((2, 8)),
            pltpu.SemaphoreType.DMA((2, 4)),
            pltpu.SemaphoreType.DMA((2, 4)),
            pltpu.SemaphoreType.DMA((2, 4)),
            pltpu.SemaphoreType.DMA((2, 4, 2)),
            pltpu.SemaphoreType.DMA((2,)),
            pltpu.SemaphoreType.DMA((2,)),
        ],
        compiler_params=pltpu.CompilerParams(
            collective_id=1, has_side_effects=True, vmem_limit_bytes=60 * 2**20
        ),
        cost_estimate=pl.CostEstimate(
            flops=15 * 10**9, bytes_accessed=100 * 2**20, transcendentals=0
        ),
    )(table, x_all, cot_all, gate, w_full, v)


def shards_dense(
    tokens, cotangent, expert_ids, gate_weights, partner, weights, first_moment, second_moment
):
    n = lax.axis_size("expert")
    tok, model = tokens.shape
    f32, bf16 = jnp.float32, jnp.bfloat16
    me = lax.axis_index("expert")
    hits = expert_ids[:, :, None] == jnp.arange(n, dtype=jnp.int32)[None, None, :]
    gates = jnp.sum(jnp.where(hits, gate_weights[:, :, None], 0.0), axis=1).T
    old = [a[0].transpose(1, 0, 2) for a in (weights, first_moment, second_moment)]
    x_all, cot_all, gate_all, w_full, m_here = gather_all(
        partner, tokens, cotangent, gates, old[0], old[1]
    )
    gate = lax.dynamic_index_in_dim(gate_all, partner[me], 1, keepdims=False)
    mixed, token_grad, keep, given, v_here = layer(
        partner,
        x_all.reshape(n * tok, model),
        cot_all.reshape(n * tok, model),
        gate.reshape(n * tok, 1),
        w_full,
        old[2],
    )
    w_here = lax.dynamic_slice_in_dim(w_full, lax.axis_index("dp") * old[0].shape[1], old[0].shape[1], axis=1)
    grad = keep.astype(f32) + given.astype(f32)
    new_state = adam(*[a.astype(f32) for a in (w_here, m_here, v_here)], grad)
    outs = [a.astype(bf16).transpose(1, 0, 2)[None] for a in new_state]
    return (mixed, token_grad, *outs)


def shards(*args):
    fits = lax.axis_size("dp") == 2 and lax.axis_size("expert") == 16
    if fits and args[0].shape[0] == 128 and args[5].shape[1] % 512 == 0:
        return shards_dense(*args)
    return shards_by_slot(*args)


def solution(mesh):
    in_specs = (
        P(("dp", "expert"), None),
        P(("dp", "expert"), None),
        P(("dp", "expert"), None),
        P(("dp", "expert"), None),
        P(),
        P("expert", "dp", None, None),
        P("expert", "dp", None, None),
        P("expert", "dp", None, None),
    )
    out_specs = (
        P(("dp", "expert"), None),
        P(("dp", "expert"), None),
        P("expert", "dp", None, None),
        P("expert", "dp", None, None),
        P("expert", "dp", None, None),
    )
    return jax.shard_map(shards, mesh=mesh, in_specs=in_specs, out_specs=out_specs, check_vma=False)
```

```python
import functools

import jax
import jax.numpy as jnp
from jax import lax
from jax.experimental import pallas as pl
from jax.experimental.pallas import tpu as pltpu
from jax.sharding import PartitionSpec as P

beta_one = 0.9
beta_two = 0.95
learn_rate = 0.01
decay_rate = 0.1
eps_adam = 1e-08
step_count = 100


def send_rows(parts):
    return (lax.all_to_all(parts[0], "expert", split_axis=0, concat_axis=0, tiled=True),)


def send_back(parts):
    return (lax.all_to_all(parts[0], "expert", split_axis=0, concat_axis=0, tiled=True),)


def shards_by_slot(
    tokens, cotangent, expert_ids, gate_weights, partner, weights, first_moment, second_moment
):
    experts_here = lax.axis_size("expert")
    tok_dev, model_width = tokens.shape
    top_count = expert_ids.shape[1]
    hidden_width = weights.shape[3]
    capacity = min(tok_dev, max(2, 5 * tok_dev * top_count // (4 * experts_here)))
    item_total = tok_dev * top_count
    slot_total = experts_here * capacity
    flat_ids = expert_ids.reshape(item_total)
    onehot = (flat_ids[:, None] == jnp.arange(experts_here, dtype=jnp.int32)[None, :]).astype(
        jnp.bfloat16
    )
    item_number = jnp.arange(item_total, dtype=jnp.int32)
    earlier = (item_number[:, None] > item_number[None, :]).astype(jnp.bfloat16)
    before = jnp.dot(earlier, onehot, preferred_element_type=jnp.float32)
    slot_of = jnp.sum(before * onehot.astype(jnp.float32), axis=1).astype(jnp.int32)
    position = flat_ids * capacity + slot_of
    source = (
        jnp.full((slot_total,), item_total, jnp.int32)
        .at[position]
        .set(jnp.arange(item_total, dtype=jnp.int32))
    )
    token_of = source // top_count
    zero_row = jnp.zeros((1, model_width), jnp.bfloat16)
    x_send = jnp.concatenate([tokens, zero_row], axis=0)[token_of].reshape(
        experts_here, capacity, model_width
    )
    gate_flat = gate_weights.reshape(item_total)
    gate_pad = jnp.concatenate([gate_flat, jnp.zeros((1,), jnp.float32)])
    cot_rows = jnp.concatenate([cotangent, zero_row], axis=0)[token_of].astype(jnp.float32)
    dy_send = (
        (gate_pad[source][:, None] * cot_rows)
        .astype(jnp.bfloat16)
        .reshape(experts_here, capacity, model_width)
    )
    gathered = lax.all_gather(weights, "dp", axis=1, tiled=True)[0]
    gate_up = gathered[:, 0:2, :].reshape(model_width, 2 * hidden_width)
    down_proj = gathered[:, 2, :]
    block_shape = (experts_here, capacity, model_width)
    (x_recv,) = send_rows((x_send,))
    forward_x_rows = x_recv.reshape(slot_total, model_width)
    both_proj = jnp.dot(forward_x_rows, gate_up, preferred_element_type=jnp.float32)
    pre_act = both_proj[:, :hidden_width]
    lin_act = both_proj[:, hidden_width:]
    sigmoid_pre = jax.nn.sigmoid(pre_act)
    silu_pre = pre_act * sigmoid_pre
    forward_hidden = (silu_pre * lin_act).astype(jnp.bfloat16)
    out_rows = jnp.dot(forward_hidden, down_proj.T, preferred_element_type=jnp.float32).astype(
        jnp.bfloat16
    )
    x_rows, saved, hidden, out_rows = (
        forward_x_rows,
        (pre_act, lin_act, sigmoid_pre, silu_pre),
        forward_hidden,
        out_rows,
    )
    (out_back,) = send_back((out_rows.reshape(block_shape),))
    (dy_recv,) = send_rows((dy_send,))
    pre_act, lin_act, sigmoid_pre, silu_pre = saved
    backward_dy_rows = dy_recv.reshape(slot_total, model_width)
    hidden_grad = jnp.dot(backward_dy_rows, down_proj, preferred_element_type=jnp.float32)
    pre_grad = (hidden_grad * lin_act * sigmoid_pre * (1.0 + pre_act * (1.0 - sigmoid_pre))).astype(
        jnp.bfloat16
    )
    lin_grad = (hidden_grad * silu_pre).astype(jnp.bfloat16)
    backward_both_grad = jnp.concatenate([pre_grad, lin_grad], axis=1)
    item_grad = jnp.dot(backward_both_grad, gate_up.T, preferred_element_type=jnp.float32).astype(
        jnp.bfloat16
    )
    dy_rows, both_grad, item_grad = (backward_dy_rows, backward_both_grad, item_grad)
    (grad_back,) = send_back((item_grad.reshape(block_shape),))
    out_items = (
        out_back.reshape(slot_total, model_width)[position].astype(jnp.float32) * gate_flat[:, None]
    )
    mixed = jnp.sum(out_items.reshape(tok_dev, top_count, model_width), axis=1).astype(jnp.bfloat16)
    grad_items = grad_back.reshape(slot_total, model_width)[position].astype(jnp.float32)
    token_grad = jnp.sum(grad_items.reshape(tok_dev, top_count, model_width), axis=1).astype(
        jnp.bfloat16
    )
    count = lax.axis_size("dp") * weights.shape[1]
    proj_grad = jnp.dot(x_rows.T, both_grad, preferred_element_type=jnp.float32)
    down_grad = jnp.dot(dy_rows.T, hidden, preferred_element_type=jnp.float32)
    grad_sum = lax.psum_scatter(
        jnp.concatenate(
            [proj_grad.reshape(count, 2, hidden_width), down_grad.reshape(count, 1, hidden_width)],
            axis=1,
        ).astype(jnp.bfloat16),
        "dp",
        scatter_dimension=0,
        tiled=True,
    ).astype(jnp.float32)
    w_old = weights[0].astype(jnp.float32)
    m_old = first_moment[0].astype(jnp.float32)
    v_old = second_moment[0].astype(jnp.float32)
    m_new = beta_one * m_old + (1.0 - beta_one) * grad_sum
    v_new = beta_two * v_old + (1.0 - beta_two) * grad_sum * grad_sum
    m_hat = m_new / (1.0 - beta_one**step_count)
    v_hat = v_new / (1.0 - beta_two**step_count)
    w_new = w_old - learn_rate * (m_hat / (jnp.sqrt(v_hat) + eps_adam) + decay_rate * w_old)
    pieces = (
        w_new.astype(jnp.bfloat16).reshape(experts_here, -1),
        m_new.astype(jnp.bfloat16).reshape(experts_here, -1),
        v_new.astype(jnp.bfloat16).reshape(experts_here, -1),
    )
    spread = (
        lax.all_to_all(pieces[0], "expert", split_axis=0, concat_axis=0, tiled=True),
        lax.all_to_all(pieces[1], "expert", split_axis=0, concat_axis=0, tiled=True),
        lax.all_to_all(pieces[2], "expert", split_axis=0, concat_axis=0, tiled=True),
    )
    ordered = (spread[0][partner], spread[1][partner], spread[2][partner])
    homed = (
        lax.all_to_all(ordered[0], "expert", split_axis=0, concat_axis=0, tiled=True),
        lax.all_to_all(ordered[1], "expert", split_axis=0, concat_axis=0, tiled=True),
        lax.all_to_all(ordered[2], "expert", split_axis=0, concat_axis=0, tiled=True),
    )
    new_weights = homed[0].reshape(weights.shape)
    new_first = homed[1].reshape(weights.shape)
    new_second = homed[2].reshape(weights.shape)
    return (mixed, token_grad, new_weights, new_first, new_second)


def adam(w_old, m_old, v_old, grad_sum):
    m_new = beta_one * m_old + (1.0 - beta_one) * grad_sum
    v_new = beta_two * v_old + (1.0 - beta_two) * grad_sum * grad_sum
    m_hat = m_new / (1.0 - beta_one**step_count)
    v_hat = v_new / (1.0 - beta_two**step_count)
    w_new = w_old - learn_rate * (m_hat / (jnp.sqrt(v_hat) + eps_adam) + decay_rate * w_old)
    return w_new, m_new, v_new


def plane_barrier(n, me):
    barrier = pltpu.get_barrier_semaphore()

    def body(step, carry):
        pl.semaphore_signal(
            barrier,
            inc=1,
            device_id={"expert": lax.rem(me + step, n)},
            device_id_type=pl.DeviceIdType.MESH,
        )
        return carry

    lax.fori_loop(1, n, body, 0)
    pl.semaphore_signal(
        barrier,
        inc=1,
        device_id={"dp": 1 - lax.axis_index("dp")},
        device_id_type=pl.DeviceIdType.MESH,
    )
    pl.semaphore_wait(barrier, n)


def remote(src, dst, send_sem, recv_sem, **where):
    return pltpu.make_async_remote_copy(
        src_ref=src,
        dst_ref=dst,
        send_sem=send_sem,
        recv_sem=recv_sem,
        device_id=where,
        device_id_type=pl.DeviceIdType.MESH,
    )


class Mover:
    def __init__(self, partner, state, home, row_base, spread, ordered, sems):
        self.partner, self.state, self.home, self.row_base = partner, state, home, row_base
        self.spread, self.ordered = spread, ordered
        self.one_send, self.one_recv, self.two_send, self.two_recv, self.own_sem = sems
        self.me = lax.axis_index("expert")
        self.n = spread.shape[0]
        self.share = state.shape[1] // self.n

    def rows(self, number, base=0):
        return pl.ds(pl.multiple_of(base + number * self.share, self.share), self.share)

    def each(self, fn):
        def body(step, carry):
            fn(step, lax.rem(self.me + step, self.n))
            return carry

        lax.fori_loop(1, self.n, body, 0)

    def one(self, step, peer):
        return remote(
            self.state.at[:, self.rows(peer), :],
            self.spread.at[self.me],
            self.one_send.at[step],
            self.one_recv.at[step],
            expert=peer,
        )

    def two(self, step, peer):
        return remote(
            self.ordered.at[peer],
            self.home.at[:, self.rows(self.me, self.row_base), :],
            self.two_send.at[step],
            self.two_recv.at[step],
            expert=peer,
        )

    def spread_out(self):
        self.each(lambda step, peer: self.one(step, peer).start())
        self.own_share().start()

    def own_share(self):
        return pltpu.make_async_copy(
            self.state.at[:, self.rows(self.me), :], self.spread.at[self.me], self.own_sem
        )

    def send_home(self):
        self.each(lambda step, peer: self.one(step, peer).wait_recv())
        self.own_share().wait()

        def pick(step, carry):
            peer = lax.rem(self.me + step, self.n)
            self.ordered[peer] = self.spread[self.partner[peer]]
            self.two(step, peer).start()
            return carry

        lax.fori_loop(1, self.n, pick, 0)
        self.home[:, self.rows(self.me, self.row_base), :] = self.spread[self.partner[self.me]]

    def at_home(self, group):
        def body(number, carry):
            step = lax.rem(self.me - number + self.n, self.n)

            @pl.when(step > 0)
            def _():
                self.two(step, lax.rem(self.me + step, self.n)).wait_recv()

            return carry

        quarter = self.n // 4
        lax.fori_loop(group * quarter, (group + 1) * quarter, body, 0)

    def sends_done(self):
        self.each(lambda step, peer: self.one(step, peer).wait_send())
        self.each(lambda step, peer: self.two(step, peer).wait_send())


def mover_scratch(shape, n):
    planes, own_rows, width = shape
    part = (n, planes, own_rows // n, width)
    return [pltpu.VMEM(part, jnp.bfloat16)] * 2 + [pltpu.SemaphoreType.DMA((n,))] * 4 + [pltpu.SemaphoreType.DMA]


def layer_kernel(
    partner,
    gates,
    x,
    cot,
    w,
    m,
    v,
    mixed,
    token_grad,
    keep,
    given,
    w_full,
    m_home,
    v_home,
    x_all,
    dy_all,
    gate_all,
    both_all,
    hidden_all,
    part,
    from_core,
    from_over,
    from_line,
    give,
    *scratch,
):
    f32, bf16 = jnp.float32, jnp.bfloat16
    me = lax.axis_index("expert")
    half = lax.axis_index("dp")
    own_rows, width = w.shape[1], w.shape[2]
    tok = x.shape[0]
    z, y, core = me // 4, lax.rem(me // 2, 2), lax.rem(me, 2)
    movers = []
    for state, home, base in ((w, w_full, half * own_rows), (m, m_home, 0), (v, v_home, 0)):
        own, scratch = scratch[:7], scratch[7:]
        movers.append(Mover(partner, state, home, base, own[0], own[1], own[2:]))
    w_move, m_move, v_move = movers
    block_recv, z_send, y_send, c_send, x_send, x_recv, own_sem = scratch[:7]
    s_send, s_recv, o_send, o_recv, l_send, l_recv, g_send, g_recv = scratch[7:]
    arrays = ((x, x_all), (cot, dy_all), (gates, gate_all))

    def hop(i, number, own, send_sem, dest):
        source, full = arrays[i]
        return remote(
            source if own else full.at[number],
            full.at[number],
            send_sem,
            block_recv.at[i, number],
            expert=dest,
        )

    def number_of(zz, yy, cc):
        return zz * 4 + yy * 2 + cc

    def down(i, s):
        return hop(i, number_of(z + s, y, core), s == 0, z_send.at[i, 0, s], me - 4)

    def up(i, s):
        return hop(i, number_of(z - s, y, core), s == 0, z_send.at[i, 1, s], me + 4)

    def over(i, zz, own=False):
        return hop(i, number_of(zz, y, core), own, y_send.at[i, zz], number_of(z, 1 - y, core))

    def beside(i, zz, yy, own=False):
        return hop(
            i, number_of(zz, yy, core), own, c_send.at[i, zz * 2 + yy], number_of(z, y, 1 - core)
        )

    def wait_block(i, number):
        hop(i, number, False, y_send.at[i, 0], lax.rem(me + 1, 16)).wait_recv()

    def passed_on(zz):
        for i in range(3):
            over(i, zz).start()
        for i in range(3):
            beside(i, zz, y).start()

    def line_step(s):
        @pl.when(z + 1 + s <= 3)
        def _():
            for i in range(3):
                wait_block(i, number_of(z + 1 + s, y, core))
                if s < 2:

                    @pl.when(z >= 1)
                    def _():
                        down(i, s + 1).start()

            passed_on(z + 1 + s)

        @pl.when(z - 1 - s >= 0)
        def _():
            for i in range(3):
                wait_block(i, number_of(z - 1 - s, y, core))
                if s < 2:

                    @pl.when(z <= 2)
                    def _():
                        up(i, s + 1).start()

            passed_on(z - 1 - s)

    def gate_column(b):
        mine = lax.broadcasted_iota(jnp.int32, gates.shape, 0) == partner[me]
        columns = []
        for side in range(2):
            row = jnp.sum(jnp.where(mine, gate_all[b * 2 + side], 0.0), axis=0, keepdims=True)
            columns.append(jnp.broadcast_to(row, (tok, tok)).T[:, :1])
        return jnp.concatenate(columns, axis=0)

    def to_core(i, b):
        return remote(
            part.at[i, b, 1 - core],
            from_core.at[i, b],
            s_send.at[i, b],
            s_recv.at[i, b],
            expert=z * 4 + y * 2 + 1 - core,
        )

    def to_over(i, zz):
        return remote(
            part.at[i, zz * 2 + 1 - y, core],
            from_over.at[i, zz],
            o_send.at[i, zz],
            o_recv.at[i, zz],
            expert=z * 4 + (1 - y) * 2 + core,
        )

    def on_line(i, zz, way):
        return remote(
            part.at[i, zz * 2 + y, core],
            from_line.at[i, zz, way],
            l_send.at[i, zz],
            l_recv.at[i, zz, way],
            expert=me + (4 if way else -4),
        )

    def added(i, b, source):
        part[i, b, core] = (part[i, b, core].astype(f32) + source.astype(f32)).astype(bf16)

    def place(t):
        mid = jnp.where(t <= 1, 3 - t, t - 2)
        return jnp.where(z == 0, 3 - t, jnp.where(z == 1, mid, jnp.where(z == 2, 3 - mid, t)))

    def chip_of(t):
        over = t < 4
        return place(lax.rem(t, 4)) * 2 + jnp.where(over, 1 - y, y)

    def block_step(t):
        b = chip_of(t)
        rows = pl.ds(pl.multiple_of(b * 2 * tok, 256), 2 * tok)
        x_rows = x_all[pl.ds(b * 2, 2)].reshape(2 * tok, x_all.shape[2])
        cot_rows = dy_all[pl.ds(b * 2, 2)].reshape(2 * tok, x_all.shape[2])
        g_rows = gate_column(b)
        pre_act = jnp.dot(x_rows, w_full[0], preferred_element_type=f32)
        lin_act = jnp.dot(x_rows, w_full[1], preferred_element_type=f32)
        sig = jax.nn.sigmoid(pre_act)
        silu = pre_act * sig
        hidden = (silu * lin_act).astype(bf16)
        hidden_all[rows, :] = hidden
        last = (((1,), (1,)), ((), ()))
        out = lax.dot_general(hidden, w_full[2], last, preferred_element_type=f32)
        part[0, b] = (g_rows * out).astype(bf16).reshape(2, tok, out.shape[1])
        dy = (g_rows * cot_rows.astype(f32)).astype(bf16)
        dy_all[pl.ds(b * 2, 2)] = dy.reshape(2, tok, x_all.shape[2])
        hidden_grad = jnp.dot(dy, w_full[2], preferred_element_type=f32)
        pre_grad = (hidden_grad * lin_act * sig * (1.0 + pre_act * (1.0 - sig))).astype(bf16)
        lin_grad = (hidden_grad * silu).astype(bf16)
        both_all[0, rows, :] = pre_grad
        both_all[1, rows, :] = lin_grad
        item = lax.dot_general(pre_grad, w_full[0], last, preferred_element_type=f32)
        item = item + lax.dot_general(lin_grad, w_full[1], last, preferred_element_type=f32)
        part[1, b] = item.astype(bf16).reshape(2, tok, out.shape[1])
        for i in range(2):
            to_core(i, b).start()

    def core_sum(t):
        b = chip_of(t)
        for i in range(2):
            to_core(i, b).wait_recv()
            added(i, b, from_core[i, b])

            @pl.when(t < 4)
            def _():
                to_over(i, b // 2).start()

    def own_block(i):
        return pltpu.make_async_copy(arrays[i][0], arrays[i][1].at[me], own_sem.at[i])

    def from_y(zz):
        for i in range(3):
            wait_block(i, number_of(zz, 1 - y, core))
            beside(i, zz, 1 - y).start()

    def exchange(g):
        rows = pl.ds(pl.multiple_of(half * own_rows + g * (own_rows // 4), 128), own_rows // 4)
        part_rows = w_full.at[:, rows, :]
        return remote(part_rows, part_rows, x_send.at[g], x_recv.at[g], dp=1 - half)

    plane_barrier(16, me)
    w_move.spread_out()
    for i in range(3):

        @pl.when(z >= 1)
        def _():
            down(i, 0).start()

        @pl.when(z <= 2)
        def _():
            up(i, 0).start()

        over(i, z, True).start()
        beside(i, z, y, True).start()
        own_block(i).start()
    line_step(0)
    w_move.send_home()
    m_move.spread_out()
    line_step(1)
    line_step(2)
    from_y(z)
    for s in range(3):

        @pl.when(z + 1 + s <= 3)
        def _():
            from_y(z + 1 + s)

        @pl.when(z - 1 - s >= 0)
        def _():
            from_y(z - 1 - s)

    for g in range(4):
        w_move.at_home(g)
        exchange(g).start()
    v_move.spread_out()
    m_move.send_home()
    for i in range(3):
        own_block(i).wait()
        for zz in range(4):
            for yy in range(2):
                wait_block(i, number_of(zz, yy, 1 - core))
    for i in range(3):
        for s in range(3):

            @pl.when(jnp.logical_and(z >= 1, z + s <= 3))
            def _():
                down(i, s).wait_send()

            @pl.when(jnp.logical_and(z <= 2, z - s >= 0))
            def _():
                up(i, s).wait_send()

        for zz in range(4):
            over(i, zz).wait_send()
            for yy in range(2):
                beside(i, zz, yy).wait_send()
    for g in range(4):
        exchange(g).wait()

    def step(t, carry):
        block_step(t)

        @pl.when(t >= 1)
        def _():
            core_sum(t - 1)

        return carry

    lax.fori_loop(0, 8, step, 0)
    core_sum(7)

    tile = own_rows // 2

    def weight_grads(base, put):
        def body(j, carry):
            rows = pl.ds(pl.multiple_of(base + j * tile, 256), tile)
            first = (((0,), (0,)), ((), ()))
            x_cols = x_all[:, :, rows].reshape(-1, tile)
            dy_cols = dy_all[:, :, rows].reshape(-1, tile)
            put(0, j, lax.dot_general(x_cols, both_all[0], first, preferred_element_type=f32))
            put(1, j, lax.dot_general(x_cols, both_all[1], first, preferred_element_type=f32))
            put(2, j, lax.dot_general(dy_cols, hidden_all[...], first, preferred_element_type=f32))
            return carry

        lax.fori_loop(0, 2, body, 0)

    def gift(j):
        rows = pl.ds(pl.multiple_of(j * tile, 256), tile)
        return remote(
            give.at[:, rows, :], given.at[:, rows, :], g_send.at[j], g_recv.at[j], dp=1 - half
        )

    def put_give(plane, j, value):
        give[plane, pl.ds(pl.multiple_of(j * tile, 256), tile), :] = value.astype(bf16)
        if plane == 2:
            gift(j).start()

    def put_keep(plane, j, value):
        keep[plane, pl.ds(pl.multiple_of(j * tile, 256), tile), :] = value.astype(bf16)

    weight_grads((1 - half) * own_rows, put_give)
    v_move.send_home()
    weight_grads(half * own_rows, put_keep)

    def over_sum(i, zz):
        to_over(i, zz).wait_recv()
        added(i, zz * 2 + y, from_over[i, zz])

    for far in (3, 2, 1):
        for way in (1, 0):
            zz = z + far if way else z - far
            inside = zz <= 3 if way else zz >= 0

            @pl.when(inside)
            def _():
                for i in range(2):
                    over_sum(i, zz)

                    @pl.when(z >= 1 if way else z <= 2)
                    def _():
                        on_line(i, zz, way).wait_recv()
                        added(i, zz * 2 + y, from_line[i, zz, way])

                    on_line(i, zz, way).start()

    for i, out in ((0, mixed), (1, token_grad)):
        over_sum(i, z)

        @pl.when(z >= 1)
        def _():
            on_line(i, z, 1).wait_recv()
            added(i, z * 2 + y, from_line[i, z, 1])

        @pl.when(z <= 2)
        def _():
            on_line(i, z, 0).wait_recv()
            added(i, z * 2 + y, from_line[i, z, 0])

        out[...] = part[i, z * 2 + y, core]
    for g in range(4):
        m_move.at_home(g)
        v_move.at_home(g)
    for j in range(2):
        gift(j).wait()
    w_move.sends_done()
    m_move.sends_done()
    v_move.sends_done()
    for i in range(2):
        for b in range(8):
            to_core(i, b).wait_send()
        for zz in range(4):
            to_over(i, zz).wait_send()

            @pl.when(zz != z)
            def _():
                on_line(i, zz, 1).wait_send()


def layer(partner, gates, x, cot, w, m, v):
    n = lax.axis_size("expert")
    vmem = pl.BlockSpec(memory_space=pltpu.VMEM)
    hbm = pl.BlockSpec(memory_space=pl.ANY)
    tok, model = x.shape
    planes, own_rows, width = v.shape
    bf16 = jnp.bfloat16
    dma = pltpu.SemaphoreType.DMA
    outs = [
        jax.ShapeDtypeStruct((tok, model), bf16),
        jax.ShapeDtypeStruct((tok, model), bf16),
        jax.ShapeDtypeStruct(v.shape, bf16),
        jax.ShapeDtypeStruct(v.shape, bf16),
        jax.ShapeDtypeStruct((planes, 2 * own_rows, width), bf16),
        jax.ShapeDtypeStruct(v.shape, bf16),
        jax.ShapeDtypeStruct(v.shape, bf16),
    ]
    return pl.pallas_call(
        layer_kernel,
        out_shape=outs,
        in_specs=[pl.BlockSpec(memory_space=pltpu.SMEM), vmem] + [hbm] * 5,
        out_specs=[vmem] * 7,
        scratch_shapes=[
            pltpu.VMEM((n, tok, model), bf16),
            pltpu.VMEM((n, tok, model), bf16),
            pltpu.VMEM((n, *gates.shape), jnp.float32),
            pltpu.VMEM((2, n * tok, width), bf16),
            pltpu.VMEM((n * tok, width), bf16),
            pltpu.VMEM((2, n // 2, 2, tok, model), bf16),
            pltpu.VMEM((2, n // 2, tok, model), bf16),
            pltpu.VMEM((2, 4, tok, model), bf16),
            pltpu.VMEM((2, 4, 2, tok, model), bf16),
            pltpu.VMEM(v.shape, bf16),
            *(mover_scratch(v.shape, n) * 3),
            dma((3, n)),
            dma((3, 2, 3)),
            dma((3, 4)),
            dma((3, 8)),
            dma((4,)),
            dma((4,)),
            dma((3,)),
            dma((2, 8)),
            dma((2, 8)),
            dma((2, 4)),
            dma((2, 4)),
            dma((2, 4)),
            dma((2, 4, 2)),
            dma((2,)),
            dma((2,)),
        ],
        compiler_params=pltpu.CompilerParams(
            collective_id=0, has_side_effects=True, vmem_limit_bytes=60 * 2**20
        ),
        cost_estimate=pl.CostEstimate(
            flops=15 * 10**9, bytes_accessed=200 * 2**20, transcendentals=0
        ),
    )(partner, gates, x, cot, w, m, v)


def shards_dense(
    tokens, cotangent, expert_ids, gate_weights, partner, weights, first_moment, second_moment
):
    n = lax.axis_size("expert")
    tok, model = tokens.shape
    f32, bf16 = jnp.float32, jnp.bfloat16
    me = lax.axis_index("expert")
    hits = expert_ids[:, :, None] == jnp.arange(n, dtype=jnp.int32)[None, None, :]
    gates = jnp.sum(jnp.where(hits, gate_weights[:, :, None], 0.0), axis=1).T
    old = [a[0].transpose(1, 0, 2) for a in (weights, first_moment, second_moment)]
    mixed, token_grad, keep, given, w_full, m_here, v_here = layer(
        partner, gates, tokens, cotangent, *old
    )
    w_here = lax.dynamic_slice_in_dim(w_full, lax.axis_index("dp") * old[0].shape[1], old[0].shape[1], axis=1)
    grad = keep.astype(f32) + given.astype(f32)
    new_state = adam(*[a.astype(f32) for a in (w_here, m_here, v_here)], grad)
    outs = [a.astype(bf16).transpose(1, 0, 2)[None] for a in new_state]
    return (mixed, token_grad, *outs)


def shards(*args):
    fits = lax.axis_size("dp") == 2 and lax.axis_size("expert") == 16
    if fits and args[0].shape[0] == 128 and args[5].shape[1] % 512 == 0:
        return shards_dense(*args)
    return shards_by_slot(*args)


def solution(mesh):
    in_specs = (
        P(("dp", "expert"), None),
        P(("dp", "expert"), None),
        P(("dp", "expert"), None),
        P(("dp", "expert"), None),
        P(),
        P("expert", "dp", None, None),
        P("expert", "dp", None, None),
        P("expert", "dp", None, None),
    )
    out_specs = (
        P(("dp", "expert"), None),
        P(("dp", "expert"), None),
        P("expert", "dp", None, None),
        P("expert", "dp", None, None),
        P("expert", "dp", None, None),
    )
    return jax.shard_map(shards, mesh=mesh, in_specs=in_specs, out_specs=out_specs, check_vma=False)
```

```python
import functools

import jax
import jax.numpy as jnp
from jax import lax
from jax.experimental import pallas as pl
from jax.experimental.pallas import tpu as pltpu
from jax.sharding import PartitionSpec as P

beta_one = 0.9
beta_two = 0.95
learn_rate = 0.01
decay_rate = 0.1
eps_adam = 1e-08
step_count = 100


def send_rows(parts):
    return (lax.all_to_all(parts[0], "expert", split_axis=0, concat_axis=0, tiled=True),)


def send_back(parts):
    return (lax.all_to_all(parts[0], "expert", split_axis=0, concat_axis=0, tiled=True),)


def shards_by_slot(
    tokens, cotangent, expert_ids, gate_weights, partner, weights, first_moment, second_moment
):
    experts_here = lax.axis_size("expert")
    tok_dev, model_width = tokens.shape
    top_count = expert_ids.shape[1]
    hidden_width = weights.shape[3]
    capacity = min(tok_dev, max(2, 5 * tok_dev * top_count // (4 * experts_here)))
    item_total = tok_dev * top_count
    slot_total = experts_here * capacity
    flat_ids = expert_ids.reshape(item_total)
    onehot = (flat_ids[:, None] == jnp.arange(experts_here, dtype=jnp.int32)[None, :]).astype(
        jnp.bfloat16
    )
    item_number = jnp.arange(item_total, dtype=jnp.int32)
    earlier = (item_number[:, None] > item_number[None, :]).astype(jnp.bfloat16)
    before = jnp.dot(earlier, onehot, preferred_element_type=jnp.float32)
    slot_of = jnp.sum(before * onehot.astype(jnp.float32), axis=1).astype(jnp.int32)
    position = flat_ids * capacity + slot_of
    source = (
        jnp.full((slot_total,), item_total, jnp.int32)
        .at[position]
        .set(jnp.arange(item_total, dtype=jnp.int32))
    )
    token_of = source // top_count
    zero_row = jnp.zeros((1, model_width), jnp.bfloat16)
    x_send = jnp.concatenate([tokens, zero_row], axis=0)[token_of].reshape(
        experts_here, capacity, model_width
    )
    gate_flat = gate_weights.reshape(item_total)
    gate_pad = jnp.concatenate([gate_flat, jnp.zeros((1,), jnp.float32)])
    cot_rows = jnp.concatenate([cotangent, zero_row], axis=0)[token_of].astype(jnp.float32)
    dy_send = (
        (gate_pad[source][:, None] * cot_rows)
        .astype(jnp.bfloat16)
        .reshape(experts_here, capacity, model_width)
    )
    gathered = lax.all_gather(weights, "dp", axis=1, tiled=True)[0]
    gate_up = gathered[:, 0:2, :].reshape(model_width, 2 * hidden_width)
    down_proj = gathered[:, 2, :]
    block_shape = (experts_here, capacity, model_width)
    (x_recv,) = send_rows((x_send,))
    forward_x_rows = x_recv.reshape(slot_total, model_width)
    both_proj = jnp.dot(forward_x_rows, gate_up, preferred_element_type=jnp.float32)
    pre_act = both_proj[:, :hidden_width]
    lin_act = both_proj[:, hidden_width:]
    sigmoid_pre = jax.nn.sigmoid(pre_act)
    silu_pre = pre_act * sigmoid_pre
    forward_hidden = (silu_pre * lin_act).astype(jnp.bfloat16)
    out_rows = jnp.dot(forward_hidden, down_proj.T, preferred_element_type=jnp.float32).astype(
        jnp.bfloat16
    )
    x_rows, saved, hidden, out_rows = (
        forward_x_rows,
        (pre_act, lin_act, sigmoid_pre, silu_pre),
        forward_hidden,
        out_rows,
    )
    (out_back,) = send_back((out_rows.reshape(block_shape),))
    (dy_recv,) = send_rows((dy_send,))
    pre_act, lin_act, sigmoid_pre, silu_pre = saved
    backward_dy_rows = dy_recv.reshape(slot_total, model_width)
    hidden_grad = jnp.dot(backward_dy_rows, down_proj, preferred_element_type=jnp.float32)
    pre_grad = (hidden_grad * lin_act * sigmoid_pre * (1.0 + pre_act * (1.0 - sigmoid_pre))).astype(
        jnp.bfloat16
    )
    lin_grad = (hidden_grad * silu_pre).astype(jnp.bfloat16)
    backward_both_grad = jnp.concatenate([pre_grad, lin_grad], axis=1)
    item_grad = jnp.dot(backward_both_grad, gate_up.T, preferred_element_type=jnp.float32).astype(
        jnp.bfloat16
    )
    dy_rows, both_grad, item_grad = (backward_dy_rows, backward_both_grad, item_grad)
    (grad_back,) = send_back((item_grad.reshape(block_shape),))
    out_items = (
        out_back.reshape(slot_total, model_width)[position].astype(jnp.float32) * gate_flat[:, None]
    )
    mixed = jnp.sum(out_items.reshape(tok_dev, top_count, model_width), axis=1).astype(jnp.bfloat16)
    grad_items = grad_back.reshape(slot_total, model_width)[position].astype(jnp.float32)
    token_grad = jnp.sum(grad_items.reshape(tok_dev, top_count, model_width), axis=1).astype(
        jnp.bfloat16
    )
    count = lax.axis_size("dp") * weights.shape[1]
    proj_grad = jnp.dot(x_rows.T, both_grad, preferred_element_type=jnp.float32)
    down_grad = jnp.dot(dy_rows.T, hidden, preferred_element_type=jnp.float32)
    grad_sum = lax.psum_scatter(
        jnp.concatenate(
            [proj_grad.reshape(count, 2, hidden_width), down_grad.reshape(count, 1, hidden_width)],
            axis=1,
        ).astype(jnp.bfloat16),
        "dp",
        scatter_dimension=0,
        tiled=True,
    ).astype(jnp.float32)
    w_old = weights[0].astype(jnp.float32)
    m_old = first_moment[0].astype(jnp.float32)
    v_old = second_moment[0].astype(jnp.float32)
    m_new = beta_one * m_old + (1.0 - beta_one) * grad_sum
    v_new = beta_two * v_old + (1.0 - beta_two) * grad_sum * grad_sum
    m_hat = m_new / (1.0 - beta_one**step_count)
    v_hat = v_new / (1.0 - beta_two**step_count)
    w_new = w_old - learn_rate * (m_hat / (jnp.sqrt(v_hat) + eps_adam) + decay_rate * w_old)
    pieces = (
        w_new.astype(jnp.bfloat16).reshape(experts_here, -1),
        m_new.astype(jnp.bfloat16).reshape(experts_here, -1),
        v_new.astype(jnp.bfloat16).reshape(experts_here, -1),
    )
    spread = (
        lax.all_to_all(pieces[0], "expert", split_axis=0, concat_axis=0, tiled=True),
        lax.all_to_all(pieces[1], "expert", split_axis=0, concat_axis=0, tiled=True),
        lax.all_to_all(pieces[2], "expert", split_axis=0, concat_axis=0, tiled=True),
    )
    ordered = (spread[0][partner], spread[1][partner], spread[2][partner])
    homed = (
        lax.all_to_all(ordered[0], "expert", split_axis=0, concat_axis=0, tiled=True),
        lax.all_to_all(ordered[1], "expert", split_axis=0, concat_axis=0, tiled=True),
        lax.all_to_all(ordered[2], "expert", split_axis=0, concat_axis=0, tiled=True),
    )
    new_weights = homed[0].reshape(weights.shape)
    new_first = homed[1].reshape(weights.shape)
    new_second = homed[2].reshape(weights.shape)
    return (mixed, token_grad, new_weights, new_first, new_second)


def adam(w_old, m_old, v_old, grad_sum):
    m_new = beta_one * m_old + (1.0 - beta_one) * grad_sum
    v_new = beta_two * v_old + (1.0 - beta_two) * grad_sum * grad_sum
    m_hat = m_new / (1.0 - beta_one**step_count)
    v_hat = v_new / (1.0 - beta_two**step_count)
    w_new = w_old - learn_rate * (m_hat / (jnp.sqrt(v_hat) + eps_adam) + decay_rate * w_old)
    return w_new, m_new, v_new


def plane_barrier(n, me):
    barrier = pltpu.get_barrier_semaphore()

    def body(step, carry):
        pl.semaphore_signal(
            barrier,
            inc=1,
            device_id={"expert": lax.rem(me + step, n)},
            device_id_type=pl.DeviceIdType.MESH,
        )
        return carry

    lax.fori_loop(1, n, body, 0)
    pl.semaphore_signal(
        barrier,
        inc=1,
        device_id={"dp": 1 - lax.axis_index("dp")},
        device_id_type=pl.DeviceIdType.MESH,
    )
    pl.semaphore_wait(barrier, n)


def remote(src, dst, send_sem, recv_sem, **where):
    return pltpu.make_async_remote_copy(
        src_ref=src,
        dst_ref=dst,
        send_sem=send_sem,
        recv_sem=recv_sem,
        device_id=where,
        device_id_type=pl.DeviceIdType.MESH,
    )


class Mover:
    def __init__(self, table, state, home, row_base, held, far, staged, sems):
        self.table, self.state, self.home, self.row_base = table, state, home, row_base
        self.held, self.far, self.staged = held, far, staged
        self.one_send, self.one_recv, self.b_send, self.b_recv = sems[:4]
        self.two_send, self.two_recv, self.own_sem = sems[4:]
        self.me = lax.axis_index("expert")
        self.n = staged.shape[0]
        self.slots = far.shape[0]
        self.side = self.me // self.n
        self.here = lax.rem(self.me, self.n)
        self.share = state.shape[1] // self.n

    def rows(self, number, base=0):
        return pl.ds(pl.multiple_of(base + number * self.share, self.share), self.share)

    def each(self, fn):
        def body(step, carry):
            fn(step, lax.rem(self.here + step, self.n))
            return carry

        lax.fori_loop(1, self.n, body, 0)

    def one(self, step, peer):
        return remote(
            self.state.at[:, self.rows(peer), :],
            self.held.at[self.here],
            self.one_send.at[step],
            self.one_recv.at[step],
            expert=self.side * self.n + peer,
        )

    def over(self, slot):
        return remote(
            self.staged.at[slot],
            self.far.at[slot],
            self.b_send.at[slot],
            self.b_recv.at[slot],
            expert=lax.rem(self.me + self.n, 2 * self.n),
        )

    def two(self, step, peer):
        return remote(
            self.staged.at[peer],
            self.home.at[:, self.rows(self.here, self.row_base), :],
            self.two_send.at[step],
            self.two_recv.at[step],
            expert=self.side * self.n + peer,
        )

    def own_share(self):
        return pltpu.make_async_copy(
            self.state.at[:, self.rows(self.here), :], self.held.at[self.here], self.own_sem
        )

    def spread_out(self):
        self.each(lambda step, peer: self.one(step, peer).start())
        self.own_share().start()

    def each_slot(self, fn):
        def body(slot, carry):
            fn(slot)
            return carry

        lax.fori_loop(0, self.slots, body, 0)

    def cross(self):
        self.each(lambda step, peer: self.one(step, peer).wait_recv())
        self.own_share().wait()

        def pick(slot):
            self.staged[slot] = self.held[self.table[self.n + slot]]
            self.over(slot).start()

        self.each_slot(pick)

    def send_home(self):
        self.each_slot(lambda slot: self.over(slot).wait())

        def chosen(home):
            at = self.table[home]
            near = self.held[jnp.minimum(at, self.n - 1)]
            return jnp.where(at < self.n, near, self.far[jnp.maximum(at - self.n, 0)])

        def pick(step, peer):
            self.staged[peer] = chosen(peer)
            self.two(step, peer).start()

        self.each(pick)
        self.home[:, self.rows(self.here, self.row_base), :] = chosen(self.here)

    def at_home(self, group):
        def body(number, carry):
            step = lax.rem(self.here - number + self.n, self.n)

            @pl.when(step > 0)
            def _():
                self.two(step, lax.rem(self.here + step, self.n)).wait_recv()

            return carry

        quarter = self.n // 4
        lax.fori_loop(group * quarter, (group + 1) * quarter, body, 0)

    def sends_done(self):
        self.each(lambda step, peer: self.one(step, peer).wait_send())
        self.each(lambda step, peer: self.two(step, peer).wait_send())


def mover_scratch(shape, n, slots):
    planes, own_rows, width = shape
    part = (planes, own_rows // n, width)
    dma = pltpu.SemaphoreType.DMA
    return [
        pltpu.VMEM((n, *part), jnp.bfloat16),
        pltpu.VMEM((slots, *part), jnp.bfloat16),
        pltpu.VMEM((n, *part), jnp.bfloat16),
        dma((n,)),
        dma((n,)),
        dma((slots,)),
        dma((slots,)),
        dma((n,)),
        dma((n,)),
        dma,
    ]


def fill_tables(partner, table, rank, slots):
    n = partner.shape[0] // 2
    side = lax.axis_index("expert") // n
    for s in range(2):
        count = jnp.int32(0)
        for i in range(n):
            rank[s * n + i] = count
            count = count + jnp.where(partner[s * n + i] // n != s, 1, 0)
    for d in range(n):
        p = partner[side * n + d]
        table[d] = jnp.where(p // n == side, lax.rem(p, n), n + rank[p])
    for j in range(slots):
        chosen = jnp.int32(0)
        for i in range(n):
            hit = jnp.logical_and(partner[side * n + i] // n != side, rank[side * n + i] == j)
            chosen = jnp.where(hit, i, chosen)
        table[n + j] = chosen


def layer_kernel(
    slots,
    partner,
    ids,
    gate_values,
    x,
    cot,
    w,
    m,
    v,
    mixed,
    token_grad,
    keep,
    given,
    w_full,
    m_home,
    v_home,
    table,
    rank,
    gates,
    x_all,
    dy_all,
    gate_all,
    both_all,
    hidden_all,
    part,
    from_core,
    from_over,
    from_line,
    give,
    *scratch,
):
    f32, bf16 = jnp.float32, jnp.bfloat16
    me = lax.axis_index("expert")
    half = lax.axis_index("dp")
    own_rows, width = w.shape[1], w.shape[2]
    tok = x.shape[0]
    z, y, core = me // 4, lax.rem(me // 2, 2), lax.rem(me, 2)
    movers = []
    moved = [(w.at[pl.ds(i, 1)], w_full.at[pl.ds(i, 1)], half * own_rows) for i in range(3)]
    for state, home, base in (*moved, (m, m_home, 0), (v, v_home, 0)):
        own, scratch = scratch[:10], scratch[10:]
        movers.append(Mover(table, state, home, base, *own[:3], own[3:]))
    w_moves, m_move, v_move = movers[:3], movers[3], movers[4]
    block_recv, z_send, y_send, c_send, x_send, x_recv, own_sem = scratch[:7]
    s_send, s_recv, o_send, o_recv, l_send, l_recv, g_send, g_recv = scratch[7:]
    arrays = ((x, x_all), (cot, dy_all), (gates, gate_all))

    def hop(i, number, own, send_sem, dest):
        source, full = arrays[i]
        return remote(
            source if own else full.at[number],
            full.at[number],
            send_sem,
            block_recv.at[i, number],
            expert=dest,
        )

    def number_of(zz, yy, cc):
        return zz * 4 + yy * 2 + cc

    def down(i, s):
        return hop(i, number_of(z + s, y, core), s == 0, z_send.at[i, 0, s], me - 4)

    def up(i, s):
        return hop(i, number_of(z - s, y, core), s == 0, z_send.at[i, 1, s], me + 4)

    def over(i, zz, own=False):
        return hop(i, number_of(zz, y, core), own, y_send.at[i, zz], number_of(z, 1 - y, core))

    def beside(i, zz, yy, own=False):
        return hop(
            i, number_of(zz, yy, core), own, c_send.at[i, zz * 2 + yy], number_of(z, y, 1 - core)
        )

    def wait_block(i, number):
        hop(i, number, False, y_send.at[i, 0], lax.rem(me + 1, 16)).wait_recv()

    def passed_on(zz):
        for i in range(3):
            over(i, zz).start()
        for i in range(3):
            beside(i, zz, y).start()

    def line_step(s):
        @pl.when(z + 1 + s <= 3)
        def _():
            for i in range(3):
                wait_block(i, number_of(z + 1 + s, y, core))
                if s < 2:

                    @pl.when(z >= 1)
                    def _():
                        down(i, s + 1).start()

            passed_on(z + 1 + s)

        @pl.when(z - 1 - s >= 0)
        def _():
            for i in range(3):
                wait_block(i, number_of(z - 1 - s, y, core))
                if s < 2:

                    @pl.when(z <= 2)
                    def _():
                        up(i, s + 1).start()

            passed_on(z - 1 - s)

    def gate_column(b):
        mine = lax.broadcasted_iota(jnp.int32, gates.shape, 0) == partner[me]
        columns = []
        for side in range(2):
            row = jnp.sum(jnp.where(mine, gate_all[b * 2 + side], 0.0), axis=0, keepdims=True)
            columns.append(jnp.broadcast_to(row, (tok, tok)).T[:, :1])
        return jnp.concatenate(columns, axis=0)

    def to_core(i, b):
        return remote(
            part.at[i, b, 1 - core],
            from_core.at[i, b],
            s_send.at[i, b],
            s_recv.at[i, b],
            expert=z * 4 + y * 2 + 1 - core,
        )

    def to_over(i, zz):
        return remote(
            part.at[i, zz * 2 + 1 - y, core],
            from_over.at[i, zz],
            o_send.at[i, zz],
            o_recv.at[i, zz],
            expert=z * 4 + (1 - y) * 2 + core,
        )

    def on_line(i, zz, way):
        return remote(
            part.at[i, zz * 2 + y, core],
            from_line.at[i, zz, way],
            l_send.at[i, zz],
            l_recv.at[i, zz, way],
            expert=me + (4 if way else -4),
        )

    def added(i, b, source):
        part[i, b, core] = (part[i, b, core].astype(f32) + source.astype(f32)).astype(bf16)

    def place(t):
        mid = jnp.where(t <= 1, 3 - t, t - 2)
        return jnp.where(z == 0, 3 - t, jnp.where(z == 1, mid, jnp.where(z == 2, 3 - mid, t)))

    def chip_of(t):
        over = t < 4
        return place(lax.rem(t, 4)) * 2 + jnp.where(over, 1 - y, y)

    def block_step(t):
        b = chip_of(t)
        rows = pl.ds(pl.multiple_of(b * 2 * tok, 256), 2 * tok)
        x_rows = x_all[pl.ds(b * 2, 2)].reshape(2 * tok, x_all.shape[2])
        cot_rows = dy_all[pl.ds(b * 2, 2)].reshape(2 * tok, x_all.shape[2])
        g_rows = gate_column(b)
        pre_act = jnp.dot(x_rows, w_full[0], preferred_element_type=f32)
        lin_act = jnp.dot(x_rows, w_full[1], preferred_element_type=f32)
        sig = jax.nn.sigmoid(pre_act)
        silu = pre_act * sig
        hidden = (silu * lin_act).astype(bf16)
        hidden_all[rows, :] = hidden
        last = (((1,), (1,)), ((), ()))
        out = lax.dot_general(hidden, w_full[2], last, preferred_element_type=f32)
        part[0, b] = (g_rows * out).astype(bf16).reshape(2, tok, out.shape[1])
        dy = (g_rows * cot_rows.astype(f32)).astype(bf16)
        dy_all[pl.ds(b * 2, 2)] = dy.reshape(2, tok, x_all.shape[2])
        hidden_grad = jnp.dot(dy, w_full[2], preferred_element_type=f32)
        pre_grad = (hidden_grad * lin_act * sig * (1.0 + pre_act * (1.0 - sig))).astype(bf16)
        lin_grad = (hidden_grad * silu).astype(bf16)
        both_all[0, rows, :] = pre_grad
        both_all[1, rows, :] = lin_grad
        item = lax.dot_general(pre_grad, w_full[0], last, preferred_element_type=f32)
        item = item + lax.dot_general(lin_grad, w_full[1], last, preferred_element_type=f32)
        part[1, b] = item.astype(bf16).reshape(2, tok, out.shape[1])
        for i in range(2):
            to_core(i, b).start()

    def core_sum(t):
        b = chip_of(t)
        for i in range(2):
            to_core(i, b).wait_recv()
            added(i, b, from_core[i, b])

            @pl.when(t < 4)
            def _():
                to_over(i, b // 2).start()

    def own_block(i):
        return pltpu.make_async_copy(arrays[i][0], arrays[i][1].at[me], own_sem.at[i])

    def from_y(zz):
        for i in range(3):
            wait_block(i, number_of(zz, 1 - y, core))
            beside(i, zz, 1 - y).start()

    def exchange(plane):
        rows = pl.ds(pl.multiple_of(half * own_rows, own_rows), own_rows)
        part_rows = w_full.at[plane, rows, :]
        return remote(part_rows, part_rows, x_send.at[plane], x_recv.at[plane], dp=1 - half)

    def w_home(plane):
        for g in range(4):
            w_moves[plane].at_home(g)
        exchange(plane).start()

    plane_barrier(16, me)
    for move in w_moves:
        move.spread_out()
    number = lax.broadcasted_iota(jnp.int32, gates.shape, 0)
    total = jnp.zeros(gates.shape, f32)
    for k in range(ids.shape[0]):
        named = jnp.broadcast_to(ids[k : k + 1, :], gates.shape) == number
        total = total + jnp.where(named, gate_values[k : k + 1, :], 0.0)
    gates[...] = total
    for i in range(3):

        @pl.when(z >= 1)
        def _():
            down(i, 0).start()

        @pl.when(z <= 2)
        def _():
            up(i, 0).start()

        over(i, z, True).start()
        beside(i, z, y, True).start()
        own_block(i).start()
    fill_tables(partner, table, rank, slots)
    for move in w_moves:
        move.cross()
    line_step(0)
    m_move.spread_out()
    w_moves[0].send_home()
    line_step(1)
    w_moves[1].send_home()
    w_home(0)
    line_step(2)
    w_moves[2].send_home()
    w_home(1)
    from_y(z)
    w_home(2)
    m_move.cross()
    for s in range(3):

        @pl.when(z + 1 + s <= 3)
        def _():
            from_y(z + 1 + s)

        @pl.when(z - 1 - s >= 0)
        def _():
            from_y(z - 1 - s)

    v_move.spread_out()
    m_move.send_home()
    for i in range(3):
        own_block(i).wait()
        for zz in range(4):
            for yy in range(2):
                wait_block(i, number_of(zz, yy, 1 - core))
    for i in range(3):
        for s in range(3):

            @pl.when(jnp.logical_and(z >= 1, z + s <= 3))
            def _():
                down(i, s).wait_send()

            @pl.when(jnp.logical_and(z <= 2, z - s >= 0))
            def _():
                up(i, s).wait_send()

        for zz in range(4):
            over(i, zz).wait_send()
            for yy in range(2):
                beside(i, zz, yy).wait_send()
    for plane in range(3):
        exchange(plane).wait()

    def step(t, carry):
        block_step(t)

        @pl.when(t >= 1)
        def _():
            core_sum(t - 1)

        return carry

    lax.fori_loop(0, 4, step, 0)
    v_move.cross()
    lax.fori_loop(4, 8, step, 0)
    core_sum(7)

    tile = own_rows // 2

    def weight_grads(base, put):
        def body(j, carry):
            rows = pl.ds(pl.multiple_of(base + j * tile, 256), tile)
            first = (((0,), (0,)), ((), ()))
            x_cols = x_all[:, :, rows].reshape(-1, tile)
            dy_cols = dy_all[:, :, rows].reshape(-1, tile)
            put(0, j, lax.dot_general(x_cols, both_all[0], first, preferred_element_type=f32))
            put(1, j, lax.dot_general(x_cols, both_all[1], first, preferred_element_type=f32))
            put(2, j, lax.dot_general(dy_cols, hidden_all[...], first, preferred_element_type=f32))
            return carry

        lax.fori_loop(0, 2, body, 0)

    def gift(j):
        rows = pl.ds(pl.multiple_of(j * tile, 256), tile)
        return remote(
            give.at[:, rows, :], given.at[:, rows, :], g_send.at[j], g_recv.at[j], dp=1 - half
        )

    def put_give(plane, j, value):
        give[plane, pl.ds(pl.multiple_of(j * tile, 256), tile), :] = value.astype(bf16)
        if plane == 2:
            gift(j).start()

    def put_keep(plane, j, value):
        keep[plane, pl.ds(pl.multiple_of(j * tile, 256), tile), :] = value.astype(bf16)

    weight_grads((1 - half) * own_rows, put_give)
    v_move.send_home()
    weight_grads(half * own_rows, put_keep)

    def over_sum(i, zz):
        to_over(i, zz).wait_recv()
        added(i, zz * 2 + y, from_over[i, zz])

    for far in (3, 2, 1):
        for way in (1, 0):
            zz = z + far if way else z - far
            inside = zz <= 3 if way else zz >= 0

            @pl.when(inside)
            def _():
                for i in range(2):
                    over_sum(i, zz)

                    @pl.when(z >= 1 if way else z <= 2)
                    def _():
                        on_line(i, zz, way).wait_recv()
                        added(i, zz * 2 + y, from_line[i, zz, way])

                    on_line(i, zz, way).start()

    for i, out in ((0, mixed), (1, token_grad)):
        over_sum(i, z)

        @pl.when(z >= 1)
        def _():
            on_line(i, z, 1).wait_recv()
            added(i, z * 2 + y, from_line[i, z, 1])

        @pl.when(z <= 2)
        def _():
            on_line(i, z, 0).wait_recv()
            added(i, z * 2 + y, from_line[i, z, 0])

        out[...] = part[i, z * 2 + y, core]
    for g in range(4):
        m_move.at_home(g)
        v_move.at_home(g)
    for j in range(2):
        gift(j).wait()
    for move in w_moves:
        move.sends_done()
    m_move.sends_done()
    v_move.sends_done()
    for i in range(2):
        for b in range(8):
            to_core(i, b).wait_send()
        for zz in range(4):
            to_over(i, zz).wait_send()

            @pl.when(zz != z)
            def _():
                on_line(i, zz, 1).wait_send()


def layer(slots, number, partner, ids, gate_values, x, cot, w, m, v):
    n = lax.axis_size("expert")
    vmem = pl.BlockSpec(memory_space=pltpu.VMEM)
    hbm = pl.BlockSpec(memory_space=pl.ANY)
    tok, model = x.shape
    planes, own_rows, width = v.shape
    bf16 = jnp.bfloat16
    dma = pltpu.SemaphoreType.DMA
    outs = [
        jax.ShapeDtypeStruct((tok, model), bf16),
        jax.ShapeDtypeStruct((tok, model), bf16),
        jax.ShapeDtypeStruct(v.shape, bf16),
        jax.ShapeDtypeStruct(v.shape, bf16),
        jax.ShapeDtypeStruct((planes, 2 * own_rows, width), bf16),
        jax.ShapeDtypeStruct(v.shape, bf16),
        jax.ShapeDtypeStruct(v.shape, bf16),
    ]
    return pl.pallas_call(
        functools.partial(layer_kernel, slots),
        out_shape=outs,
        in_specs=[pl.BlockSpec(memory_space=pltpu.SMEM)] + [vmem] * 2 + [hbm] * 5,
        out_specs=[vmem] * 7,
        scratch_shapes=[
            pltpu.SMEM((n,), jnp.int32),
            pltpu.SMEM((n,), jnp.int32),
            pltpu.VMEM((n, tok), jnp.float32),
            pltpu.VMEM((n, tok, model), bf16),
            pltpu.VMEM((n, tok, model), bf16),
            pltpu.VMEM((n, n, tok), jnp.float32),
            pltpu.VMEM((2, n * tok, width), bf16),
            pltpu.VMEM((n * tok, width), bf16),
            pltpu.VMEM((2, n // 2, 2, tok, model), bf16),
            pltpu.VMEM((2, n // 2, tok, model), bf16),
            pltpu.VMEM((2, 4, tok, model), bf16),
            pltpu.VMEM((2, 4, 2, tok, model), bf16),
            pltpu.VMEM(v.shape, bf16),
            *(mover_scratch((1, *v.shape[1:]), n // 2, slots) * 3),
            *(mover_scratch(v.shape, n // 2, slots) * 2),
            dma((3, n)),
            dma((3, 2, 3)),
            dma((3, 4)),
            dma((3, 8)),
            dma((3,)),
            dma((3,)),
            dma((3,)),
            dma((2, 8)),
            dma((2, 8)),
            dma((2, 4)),
            dma((2, 4)),
            dma((2, 4)),
            dma((2, 4, 2)),
            dma((2,)),
            dma((2,)),
        ],
        compiler_params=pltpu.CompilerParams(
            collective_id=number, has_side_effects=True, vmem_limit_bytes=60 * 2**20
        ),
        cost_estimate=pl.CostEstimate(
            flops=15 * 10**9, bytes_accessed=200 * 2**20, transcendentals=0
        ),
    )(partner, ids, gate_values, x, cot, w, m, v)


def layer_and_step(slots, number, partner, ids, gate_values, x, cot, w, m, v):
    f32, bf16 = jnp.float32, jnp.bfloat16
    own_rows = w.shape[1]
    mixed, token_grad, keep, given, w_full, m_here, v_here = layer(
        slots, number, partner, ids, gate_values, x, cot, w, m, v
    )
    w_here = lax.dynamic_slice_in_dim(w_full, lax.axis_index("dp") * own_rows, own_rows, axis=1)
    grad = keep.astype(f32) + given.astype(f32)
    new_state = adam(*[a.astype(f32) for a in (w_here, m_here, v_here)], grad)
    return (mixed, token_grad, *[a.astype(bf16).transpose(1, 0, 2)[None] for a in new_state])


def shards_dense(
    tokens, cotangent, expert_ids, gate_weights, partner, weights, first_moment, second_moment
):
    half = lax.axis_size("expert") // 2
    number = jnp.arange(2 * half, dtype=jnp.int32)
    crossing = jnp.sum(jnp.where(partner >= half, number < half, False).astype(jnp.int32))
    old = [a[0].transpose(1, 0, 2) for a in (weights, first_moment, second_moment)]
    return lax.switch(
        jnp.where(crossing <= 4, 0, jnp.where(crossing <= 6, 1, 2)),
        [functools.partial(layer_and_step, slots, i) for i, slots in enumerate((4, 6, 8))],
        partner,
        expert_ids.T,
        gate_weights.T,
        tokens,
        cotangent,
        *old,
    )


def shards(*args):
    fits = lax.axis_size("dp") == 2 and lax.axis_size("expert") == 16
    if fits and args[0].shape[0] == 128 and args[5].shape[1] % 512 == 0:
        return shards_dense(*args)
    return shards_by_slot(*args)


def solution(mesh):
    in_specs = (
        P(("dp", "expert"), None),
        P(("dp", "expert"), None),
        P(("dp", "expert"), None),
        P(("dp", "expert"), None),
        P(),
        P("expert", "dp", None, None),
        P("expert", "dp", None, None),
        P("expert", "dp", None, None),
    )
    out_specs = (
        P(("dp", "expert"), None),
        P(("dp", "expert"), None),
        P("expert", "dp", None, None),
        P("expert", "dp", None, None),
        P("expert", "dp", None, None),
    )
    return jax.shard_map(shards, mesh=mesh, in_specs=in_specs, out_specs=out_specs, check_vma=False)
```

```python
import functools

import jax
import jax.numpy as jnp
from jax import lax
from jax.experimental import pallas as pl
from jax.experimental.pallas import tpu as pltpu
from jax.sharding import PartitionSpec as P

beta_one = 0.9
beta_two = 0.95
learn_rate = 0.01
decay_rate = 0.1
eps_adam = 1e-08
step_count = 100


def send_rows(parts):
    return (lax.all_to_all(parts[0], "expert", split_axis=0, concat_axis=0, tiled=True),)


def send_back(parts):
    return (lax.all_to_all(parts[0], "expert", split_axis=0, concat_axis=0, tiled=True),)


def shards_by_slot(
    tokens, cotangent, expert_ids, gate_weights, partner, weights, first_moment, second_moment
):
    experts_here = lax.axis_size("expert")
    tok_dev, model_width = tokens.shape
    top_count = expert_ids.shape[1]
    hidden_width = weights.shape[3]
    capacity = min(tok_dev, max(2, 5 * tok_dev * top_count // (4 * experts_here)))
    item_total = tok_dev * top_count
    slot_total = experts_here * capacity
    flat_ids = expert_ids.reshape(item_total)
    onehot = (flat_ids[:, None] == jnp.arange(experts_here, dtype=jnp.int32)[None, :]).astype(
        jnp.bfloat16
    )
    item_number = jnp.arange(item_total, dtype=jnp.int32)
    earlier = (item_number[:, None] > item_number[None, :]).astype(jnp.bfloat16)
    before = jnp.dot(earlier, onehot, preferred_element_type=jnp.float32)
    slot_of = jnp.sum(before * onehot.astype(jnp.float32), axis=1).astype(jnp.int32)
    position = flat_ids * capacity + slot_of
    source = (
        jnp.full((slot_total,), item_total, jnp.int32)
        .at[position]
        .set(jnp.arange(item_total, dtype=jnp.int32))
    )
    token_of = source // top_count
    zero_row = jnp.zeros((1, model_width), jnp.bfloat16)
    x_send = jnp.concatenate([tokens, zero_row], axis=0)[token_of].reshape(
        experts_here, capacity, model_width
    )
    gate_flat = gate_weights.reshape(item_total)
    gate_pad = jnp.concatenate([gate_flat, jnp.zeros((1,), jnp.float32)])
    cot_rows = jnp.concatenate([cotangent, zero_row], axis=0)[token_of].astype(jnp.float32)
    dy_send = (
        (gate_pad[source][:, None] * cot_rows)
        .astype(jnp.bfloat16)
        .reshape(experts_here, capacity, model_width)
    )
    gathered = lax.all_gather(weights, "dp", axis=1, tiled=True)[0]
    gate_up = gathered[:, 0:2, :].reshape(model_width, 2 * hidden_width)
    down_proj = gathered[:, 2, :]
    block_shape = (experts_here, capacity, model_width)
    (x_recv,) = send_rows((x_send,))
    forward_x_rows = x_recv.reshape(slot_total, model_width)
    both_proj = jnp.dot(forward_x_rows, gate_up, preferred_element_type=jnp.float32)
    pre_act = both_proj[:, :hidden_width]
    lin_act = both_proj[:, hidden_width:]
    sigmoid_pre = jax.nn.sigmoid(pre_act)
    silu_pre = pre_act * sigmoid_pre
    forward_hidden = (silu_pre * lin_act).astype(jnp.bfloat16)
    out_rows = jnp.dot(forward_hidden, down_proj.T, preferred_element_type=jnp.float32).astype(
        jnp.bfloat16
    )
    x_rows, saved, hidden, out_rows = (
        forward_x_rows,
        (pre_act, lin_act, sigmoid_pre, silu_pre),
        forward_hidden,
        out_rows,
    )
    (out_back,) = send_back((out_rows.reshape(block_shape),))
    (dy_recv,) = send_rows((dy_send,))
    pre_act, lin_act, sigmoid_pre, silu_pre = saved
    backward_dy_rows = dy_recv.reshape(slot_total, model_width)
    hidden_grad = jnp.dot(backward_dy_rows, down_proj, preferred_element_type=jnp.float32)
    pre_grad = (hidden_grad * lin_act * sigmoid_pre * (1.0 + pre_act * (1.0 - sigmoid_pre))).astype(
        jnp.bfloat16
    )
    lin_grad = (hidden_grad * silu_pre).astype(jnp.bfloat16)
    backward_both_grad = jnp.concatenate([pre_grad, lin_grad], axis=1)
    item_grad = jnp.dot(backward_both_grad, gate_up.T, preferred_element_type=jnp.float32).astype(
        jnp.bfloat16
    )
    dy_rows, both_grad, item_grad = (backward_dy_rows, backward_both_grad, item_grad)
    (grad_back,) = send_back((item_grad.reshape(block_shape),))
    out_items = (
        out_back.reshape(slot_total, model_width)[position].astype(jnp.float32) * gate_flat[:, None]
    )
    mixed = jnp.sum(out_items.reshape(tok_dev, top_count, model_width), axis=1).astype(jnp.bfloat16)
    grad_items = grad_back.reshape(slot_total, model_width)[position].astype(jnp.float32)
    token_grad = jnp.sum(grad_items.reshape(tok_dev, top_count, model_width), axis=1).astype(
        jnp.bfloat16
    )
    count = lax.axis_size("dp") * weights.shape[1]
    proj_grad = jnp.dot(x_rows.T, both_grad, preferred_element_type=jnp.float32)
    down_grad = jnp.dot(dy_rows.T, hidden, preferred_element_type=jnp.float32)
    grad_sum = lax.psum_scatter(
        jnp.concatenate(
            [proj_grad.reshape(count, 2, hidden_width), down_grad.reshape(count, 1, hidden_width)],
            axis=1,
        ).astype(jnp.bfloat16),
        "dp",
        scatter_dimension=0,
        tiled=True,
    ).astype(jnp.float32)
    w_old = weights[0].astype(jnp.float32)
    m_old = first_moment[0].astype(jnp.float32)
    v_old = second_moment[0].astype(jnp.float32)
    m_new = beta_one * m_old + (1.0 - beta_one) * grad_sum
    v_new = beta_two * v_old + (1.0 - beta_two) * grad_sum * grad_sum
    m_hat = m_new / (1.0 - beta_one**step_count)
    v_hat = v_new / (1.0 - beta_two**step_count)
    w_new = w_old - learn_rate * (m_hat / (jnp.sqrt(v_hat) + eps_adam) + decay_rate * w_old)
    pieces = (
        w_new.astype(jnp.bfloat16).reshape(experts_here, -1),
        m_new.astype(jnp.bfloat16).reshape(experts_here, -1),
        v_new.astype(jnp.bfloat16).reshape(experts_here, -1),
    )
    spread = (
        lax.all_to_all(pieces[0], "expert", split_axis=0, concat_axis=0, tiled=True),
        lax.all_to_all(pieces[1], "expert", split_axis=0, concat_axis=0, tiled=True),
        lax.all_to_all(pieces[2], "expert", split_axis=0, concat_axis=0, tiled=True),
    )
    ordered = (spread[0][partner], spread[1][partner], spread[2][partner])
    homed = (
        lax.all_to_all(ordered[0], "expert", split_axis=0, concat_axis=0, tiled=True),
        lax.all_to_all(ordered[1], "expert", split_axis=0, concat_axis=0, tiled=True),
        lax.all_to_all(ordered[2], "expert", split_axis=0, concat_axis=0, tiled=True),
    )
    new_weights = homed[0].reshape(weights.shape)
    new_first = homed[1].reshape(weights.shape)
    new_second = homed[2].reshape(weights.shape)
    return (mixed, token_grad, new_weights, new_first, new_second)


def adam(w_old, m_old, v_old, grad_sum):
    m_new = beta_one * m_old + (1.0 - beta_one) * grad_sum
    v_new = beta_two * v_old + (1.0 - beta_two) * grad_sum * grad_sum
    m_hat = m_new / (1.0 - beta_one**step_count)
    v_hat = v_new / (1.0 - beta_two**step_count)
    w_new = w_old - learn_rate * (m_hat / (jnp.sqrt(v_hat) + eps_adam) + decay_rate * w_old)
    return w_new, m_new, v_new


def plane_barrier(n, me):
    barrier = pltpu.get_barrier_semaphore()

    def body(step, carry):
        pl.semaphore_signal(
            barrier,
            inc=1,
            device_id={"expert": lax.rem(me + step, n)},
            device_id_type=pl.DeviceIdType.MESH,
        )
        return carry

    lax.fori_loop(1, n, body, 0)
    pl.semaphore_signal(
        barrier,
        inc=1,
        device_id={"dp": 1 - lax.axis_index("dp")},
        device_id_type=pl.DeviceIdType.MESH,
    )
    pl.semaphore_wait(barrier, n)


def remote(src, dst, send_sem, recv_sem, **where):
    return pltpu.make_async_remote_copy(
        src_ref=src,
        dst_ref=dst,
        send_sem=send_sem,
        recv_sem=recv_sem,
        device_id=where,
        device_id_type=pl.DeviceIdType.MESH,
    )


class Mover:
    def __init__(self, table, state, home, row_base, held, far, staged, sems):
        self.table, self.state, self.home, self.row_base = table, state, home, row_base
        self.held, self.far, self.staged = held, far, staged
        self.one_send, self.one_recv, self.b_send, self.b_recv = sems[:4]
        self.two_send, self.two_recv, self.own_sem = sems[4:]
        self.me = lax.axis_index("expert")
        self.n = staged.shape[0]
        self.slots = far.shape[0]
        self.side = self.me // self.n
        self.here = lax.rem(self.me, self.n)
        self.share = state.shape[1] // self.n

    def rows(self, number, base=0):
        return pl.ds(pl.multiple_of(base + number * self.share, self.share), self.share)

    def each(self, fn):
        def body(step, carry):
            fn(step, lax.rem(self.here + step, self.n))
            return carry

        lax.fori_loop(1, self.n, body, 0)

    def one(self, step, peer):
        return remote(
            self.state.at[:, self.rows(peer), :],
            self.held.at[self.here],
            self.one_send.at[step],
            self.one_recv.at[step],
            expert=self.side * self.n + peer,
        )

    def over(self, slot):
        return remote(
            self.staged.at[slot],
            self.far.at[slot],
            self.b_send.at[slot],
            self.b_recv.at[slot],
            expert=lax.rem(self.me + self.n, 2 * self.n),
        )

    def two(self, step, peer):
        return remote(
            self.staged.at[peer],
            self.home.at[:, self.rows(self.here, self.row_base), :],
            self.two_send.at[step],
            self.two_recv.at[step],
            expert=self.side * self.n + peer,
        )

    def own_share(self):
        return pltpu.make_async_copy(
            self.state.at[:, self.rows(self.here), :], self.held.at[self.here], self.own_sem
        )

    def spread_out(self):
        self.each(lambda step, peer: self.one(step, peer).start())
        self.own_share().start()

    def each_slot(self, fn):
        def body(slot, carry):
            fn(slot)
            return carry

        lax.fori_loop(0, self.slots, body, 0)

    def cross(self):
        self.each(lambda step, peer: self.one(step, peer).wait_recv())
        self.own_share().wait()

        def pick(slot):
            self.staged[slot] = self.held[self.table[self.n + slot]]
            self.over(slot).start()

        self.each_slot(pick)

    def send_home(self):
        self.each_slot(lambda slot: self.over(slot).wait())

        def chosen(home):
            at = self.table[home]
            near = self.held[jnp.minimum(at, self.n - 1)]
            return jnp.where(at < self.n, near, self.far[jnp.maximum(at - self.n, 0)])

        def pick(step, peer):
            self.staged[peer] = chosen(peer)
            self.two(step, peer).start()

        self.each(pick)
        self.home[:, self.rows(self.here, self.row_base), :] = chosen(self.here)

    def at_home(self, group):
        def body(number, carry):
            step = lax.rem(self.here - number + self.n, self.n)

            @pl.when(step > 0)
            def _():
                self.two(step, lax.rem(self.here + step, self.n)).wait_recv()

            return carry

        quarter = self.n // 4
        lax.fori_loop(group * quarter, (group + 1) * quarter, body, 0)

    def sends_done(self):
        self.each(lambda step, peer: self.one(step, peer).wait_send())
        self.each(lambda step, peer: self.two(step, peer).wait_send())


def mover_scratch(shape, n, slots):
    planes, own_rows, width = shape
    part = (planes, own_rows // n, width)
    dma = pltpu.SemaphoreType.DMA
    return [
        pltpu.VMEM((n, *part), jnp.bfloat16),
        pltpu.VMEM((slots, *part), jnp.bfloat16),
        pltpu.VMEM((n, *part), jnp.bfloat16),
        dma((n,)),
        dma((n,)),
        dma((slots,)),
        dma((slots,)),
        dma((n,)),
        dma((n,)),
        dma,
    ]


def fill_tables(partner, table, rank, slots):
    n = partner.shape[0] // 2
    side = lax.axis_index("expert") // n
    for s in range(2):
        count = jnp.int32(0)
        for i in range(n):
            rank[s * n + i] = count
            count = count + jnp.where(partner[s * n + i] // n != s, 1, 0)
    for d in range(n):
        p = partner[side * n + d]
        table[d] = jnp.where(p // n == side, lax.rem(p, n), n + rank[p])
    for j in range(slots):
        chosen = jnp.int32(0)
        for i in range(n):
            hit = jnp.logical_and(partner[side * n + i] // n != side, rank[side * n + i] == j)
            chosen = jnp.where(hit, i, chosen)
        table[n + j] = chosen


def layer_kernel(
    slots,
    partner,
    ids,
    gate_values,
    x,
    cot,
    w,
    m,
    v,
    mixed,
    token_grad,
    keep,
    given,
    w_full,
    m_home,
    v_home,
    table,
    rank,
    gates,
    x_all,
    cot_all,
    dy_all,
    gate_all,
    both_all,
    hidden_all,
    part,
    from_core,
    from_over,
    from_line,
    give,
    *scratch,
):
    f32, bf16 = jnp.float32, jnp.bfloat16
    me = lax.axis_index("expert")
    half = lax.axis_index("dp")
    own_rows, width = w.shape[1], w.shape[2]
    tok = x.shape[0]
    z, y, core = me // 4, lax.rem(me // 2, 2), lax.rem(me, 2)
    movers = []
    moved = [(w.at[pl.ds(i, 1)], w_full.at[pl.ds(i, 1)], half * own_rows) for i in range(3)]
    for state, home, base in (*moved, (m, m_home, 0), (v, v_home, 0)):
        own, scratch = scratch[:10], scratch[10:]
        movers.append(Mover(table, state, home, base, *own[:3], own[3:]))
    w_moves, m_move, v_move = movers[:3], movers[3], movers[4]
    block_recv, z_send, y_send, c_send, x_send, x_recv, own_sem = scratch[:7]
    s_send, s_recv, o_send, o_recv, l_send, l_recv, g_send, g_recv = scratch[7:]
    arrays = ((x, x_all), (cot, cot_all), (gates, gate_all))

    def hop(i, number, own, send_sem, dest):
        source, full = arrays[i]
        return remote(
            source if own else full.at[number],
            full.at[number],
            send_sem,
            block_recv.at[i, number],
            expert=dest,
        )

    def number_of(zz, yy, cc):
        return zz * 4 + yy * 2 + cc

    def down(i, s):
        return hop(i, number_of(z + s, y, core), s == 0, z_send.at[i, 0, s], me - 4)

    def up(i, s):
        return hop(i, number_of(z - s, y, core), s == 0, z_send.at[i, 1, s], me + 4)

    def over(i, zz, own=False):
        return hop(i, number_of(zz, y, core), own, y_send.at[i, zz], number_of(z, 1 - y, core))

    def beside(i, zz, yy, own=False):
        return hop(
            i, number_of(zz, yy, core), own, c_send.at[i, zz * 2 + yy], number_of(z, y, 1 - core)
        )

    def wait_block(i, number):
        hop(i, number, False, y_send.at[i, 0], lax.rem(me + 1, 16)).wait_recv()

    def passed_on(zz, which):
        for i in which:
            over(i, zz).start()
        for i in which:
            beside(i, zz, y).start()

    def line_step(s, which):
        @pl.when(z + 1 + s <= 3)
        def _():
            for i in which:
                wait_block(i, number_of(z + 1 + s, y, core))
                if s < 2:

                    @pl.when(z >= 1)
                    def _():
                        down(i, s + 1).start()

            passed_on(z + 1 + s, which)

        @pl.when(z - 1 - s >= 0)
        def _():
            for i in which:
                wait_block(i, number_of(z - 1 - s, y, core))
                if s < 2:

                    @pl.when(z <= 2)
                    def _():
                        up(i, s + 1).start()

            passed_on(z - 1 - s, which)

    def gate_column(b):
        mine = lax.broadcasted_iota(jnp.int32, gates.shape, 0) == partner[me]
        columns = []
        for side in range(2):
            row = jnp.sum(jnp.where(mine, gate_all[b * 2 + side], 0.0), axis=0, keepdims=True)
            columns.append(jnp.broadcast_to(row, (tok, tok)).T[:, :1])
        return jnp.concatenate(columns, axis=0)

    def to_core(i, b):
        return remote(
            part.at[i, b, 1 - core],
            from_core.at[i, b],
            s_send.at[i, b],
            s_recv.at[i, b],
            expert=z * 4 + y * 2 + 1 - core,
        )

    def to_over(i, zz):
        return remote(
            part.at[i, zz * 2 + 1 - y, core],
            from_over.at[i, zz],
            o_send.at[i, zz],
            o_recv.at[i, zz],
            expert=z * 4 + (1 - y) * 2 + core,
        )

    def on_line(i, zz, way):
        return remote(
            part.at[i, zz * 2 + y, core],
            from_line.at[i, zz, way],
            l_send.at[i, zz],
            l_recv.at[i, zz, way],
            expert=me + (4 if way else -4),
        )

    def added(i, b, source):
        part[i, b, core] = (part[i, b, core].astype(f32) + source.astype(f32)).astype(bf16)

    def place(t):
        mid = jnp.where(t <= 1, 3 - t, t - 2)
        return jnp.where(z == 0, 3 - t, jnp.where(z == 1, mid, jnp.where(z == 2, 3 - mid, t)))

    def chip_of(t):
        over = t < 4
        return place(lax.rem(t, 4)) * 2 + jnp.where(over, 1 - y, y)

    last = (((1,), (1,)), ((), ()))

    def forward_step(t):
        b = chip_of(t)
        rows = pl.ds(pl.multiple_of(b * 2 * tok, 256), 2 * tok)
        x_rows = x_all[pl.ds(b * 2, 2)].reshape(2 * tok, x_all.shape[2])
        pre_act = jnp.dot(x_rows, w_full[0], preferred_element_type=f32)
        lin_act = jnp.dot(x_rows, w_full[1], preferred_element_type=f32)
        sig = jax.nn.sigmoid(pre_act)
        silu = pre_act * sig
        hidden = (silu * lin_act).astype(bf16)
        hidden_all[rows, :] = hidden
        both_all[0, rows, :] = (lin_act * sig * (1.0 + pre_act * (1.0 - sig))).astype(bf16)
        both_all[1, rows, :] = silu.astype(bf16)
        out = lax.dot_general(hidden, w_full[2], last, preferred_element_type=f32)
        part[0, b] = (gate_column(b) * out).astype(bf16).reshape(2, tok, out.shape[1])
        to_core(0, b).start()

    def backward_step(t):
        b = chip_of(t)
        rows = pl.ds(pl.multiple_of(b * 2 * tok, 256), 2 * tok)
        cot_rows = cot_all[pl.ds(b * 2, 2)].reshape(2 * tok, x_all.shape[2])
        dy = (gate_column(b) * cot_rows.astype(f32)).astype(bf16)
        dy_all[pl.ds(b * 2, 2)] = dy.reshape(2, tok, x_all.shape[2])
        hidden_grad = jnp.dot(dy, w_full[2], preferred_element_type=f32)
        pre_grad = (hidden_grad * both_all[0, rows, :].astype(f32)).astype(bf16)
        lin_grad = (hidden_grad * both_all[1, rows, :].astype(f32)).astype(bf16)
        both_all[0, rows, :] = pre_grad
        both_all[1, rows, :] = lin_grad
        item = lax.dot_general(pre_grad, w_full[0], last, preferred_element_type=f32)
        item = item + lax.dot_general(lin_grad, w_full[1], last, preferred_element_type=f32)
        part[1, b] = item.astype(bf16).reshape(2, tok, item.shape[1])
        to_core(1, b).start()

    def core_sum(i, t):
        b = chip_of(t)
        to_core(i, b).wait_recv()
        added(i, b, from_core[i, b])

        @pl.when(t < 4)
        def _():
            to_over(i, b // 2).start()

    def own_block(i):
        return pltpu.make_async_copy(arrays[i][0], arrays[i][1].at[me], own_sem.at[i])

    def from_y(zz, which):
        for i in which:
            wait_block(i, number_of(zz, 1 - y, core))
            beside(i, zz, 1 - y).start()

    def exchange(plane):
        rows = pl.ds(pl.multiple_of(half * own_rows, own_rows), own_rows)
        part_rows = w_full.at[plane, rows, :]
        return remote(part_rows, part_rows, x_send.at[plane], x_recv.at[plane], dp=1 - half)

    def w_home(plane):
        for g in range(4):
            w_moves[plane].at_home(g)
        exchange(plane).start()

    plane_barrier(16, me)
    for move in w_moves:
        move.spread_out()
    number = lax.broadcasted_iota(jnp.int32, gates.shape, 0)
    total = jnp.zeros(gates.shape, f32)
    for k in range(ids.shape[0]):
        named = jnp.broadcast_to(ids[k : k + 1, :], gates.shape) == number
        total = total + jnp.where(named, gate_values[k : k + 1, :], 0.0)
    gates[...] = total
    def first_sends(which):
        for i in which:

            @pl.when(z >= 1)
            def _():
                down(i, 0).start()

            @pl.when(z <= 2)
            def _():
                up(i, 0).start()

            over(i, z, True).start()
            beside(i, z, y, True).start()
            own_block(i).start()

    def all_from_y(which):
        from_y(z, which)
        for s in range(3):

            @pl.when(z + 1 + s <= 3)
            def _():
                from_y(z + 1 + s, which)

            @pl.when(z - 1 - s >= 0)
            def _():
                from_y(z - 1 - s, which)

    def all_beside(which):
        for i in which:
            own_block(i).wait()
            for zz in range(4):
                for yy in range(2):
                    wait_block(i, number_of(zz, yy, 1 - core))

    rows_first, rows_later = (2, 0), (1,)
    first_sends(rows_first)
    fill_tables(partner, table, rank, slots)
    m_move.spread_out()
    for move in w_moves:
        move.cross()
    line_step(0, rows_first)
    first_sends(rows_later)
    w_moves[0].send_home()
    line_step(1, rows_first)
    w_moves[1].send_home()
    w_home(0)
    line_step(2, rows_first)
    w_moves[2].send_home()
    line_step(0, rows_later)
    w_home(1)
    all_from_y(rows_first)
    w_home(2)
    m_move.cross()
    line_step(1, rows_later)
    line_step(2, rows_later)
    v_move.spread_out()
    m_move.send_home()
    all_beside(rows_first)
    for plane in range(3):
        exchange(plane).wait()

    def forward(t, carry):
        forward_step(t)

        @pl.when(t >= 1)
        def _():
            core_sum(0, t - 1)

        return carry

    lax.fori_loop(0, 8, forward, 0)
    core_sum(0, 7)
    all_from_y(rows_later)
    v_move.cross()
    all_beside(rows_later)

    def backward(t, carry):
        backward_step(t)

        @pl.when(t >= 1)
        def _():
            core_sum(1, t - 1)

        return carry

    lax.fori_loop(0, 8, backward, 0)
    core_sum(1, 7)

    tile = own_rows // 2

    def weight_grads(base, put):
        def body(j, carry):
            rows = pl.ds(pl.multiple_of(base + j * tile, 256), tile)
            first = (((0,), (0,)), ((), ()))
            x_cols = x_all[:, :, rows].reshape(-1, tile)
            dy_cols = dy_all[:, :, rows].reshape(-1, tile)
            put(0, j, lax.dot_general(x_cols, both_all[0], first, preferred_element_type=f32))
            put(1, j, lax.dot_general(x_cols, both_all[1], first, preferred_element_type=f32))
            put(2, j, lax.dot_general(dy_cols, hidden_all[...], first, preferred_element_type=f32))
            return carry

        lax.fori_loop(0, 2, body, 0)

    def gift(j):
        rows = pl.ds(pl.multiple_of(j * tile, 256), tile)
        return remote(
            give.at[:, rows, :], given.at[:, rows, :], g_send.at[j], g_recv.at[j], dp=1 - half
        )

    def put_give(plane, j, value):
        give[plane, pl.ds(pl.multiple_of(j * tile, 256), tile), :] = value.astype(bf16)
        if plane == 2:
            gift(j).start()

    def put_keep(plane, j, value):
        keep[plane, pl.ds(pl.multiple_of(j * tile, 256), tile), :] = value.astype(bf16)

    def over_sum(i, zz):
        to_over(i, zz).wait_recv()
        added(i, zz * 2 + y, from_over[i, zz])

    def line_sums(i, far):
        for way in (1, 0):
            zz = z + far if way else z - far

            @pl.when(zz <= 3 if way else zz >= 0)
            def _():
                over_sum(i, zz)

                @pl.when(z >= 1 if way else z <= 2)
                def _():
                    on_line(i, zz, way).wait_recv()
                    added(i, zz * 2 + y, from_line[i, zz, way])

                on_line(i, zz, way).start()

    line_sums(0, 3)
    weight_grads((1 - half) * own_rows, put_give)
    line_sums(0, 2)
    v_move.send_home()
    line_sums(1, 3)
    line_sums(0, 1)
    weight_grads(half * own_rows, put_keep)
    line_sums(1, 2)
    line_sums(1, 1)
    for i, out in ((0, mixed), (1, token_grad)):
        over_sum(i, z)

        @pl.when(z >= 1)
        def _():
            on_line(i, z, 1).wait_recv()
            added(i, z * 2 + y, from_line[i, z, 1])

        @pl.when(z <= 2)
        def _():
            on_line(i, z, 0).wait_recv()
            added(i, z * 2 + y, from_line[i, z, 0])

        out[...] = part[i, z * 2 + y, core]
    for g in range(4):
        m_move.at_home(g)
        v_move.at_home(g)
    for j in range(2):
        gift(j).wait()
    for move in w_moves:
        move.sends_done()
    for i in range(3):
        for s in range(3):

            @pl.when(jnp.logical_and(z >= 1, z + s <= 3))
            def _():
                down(i, s).wait_send()

            @pl.when(jnp.logical_and(z <= 2, z - s >= 0))
            def _():
                up(i, s).wait_send()

        for zz in range(4):
            over(i, zz).wait_send()
            for yy in range(2):
                beside(i, zz, yy).wait_send()
    m_move.sends_done()
    v_move.sends_done()
    for i in range(2):
        for b in range(8):
            to_core(i, b).wait_send()
        for zz in range(4):
            to_over(i, zz).wait_send()

            @pl.when(zz != z)
            def _():
                on_line(i, zz, 1).wait_send()


def layer(slots, number, partner, ids, gate_values, x, cot, w, m, v):
    n = lax.axis_size("expert")
    vmem = pl.BlockSpec(memory_space=pltpu.VMEM)
    hbm = pl.BlockSpec(memory_space=pl.ANY)
    tok, model = x.shape
    planes, own_rows, width = v.shape
    bf16 = jnp.bfloat16
    dma = pltpu.SemaphoreType.DMA
    outs = [
        jax.ShapeDtypeStruct((tok, model), bf16),
        jax.ShapeDtypeStruct((tok, model), bf16),
        jax.ShapeDtypeStruct(v.shape, bf16),
        jax.ShapeDtypeStruct(v.shape, bf16),
        jax.ShapeDtypeStruct((planes, 2 * own_rows, width), bf16),
        jax.ShapeDtypeStruct(v.shape, bf16),
        jax.ShapeDtypeStruct(v.shape, bf16),
    ]
    return pl.pallas_call(
        functools.partial(layer_kernel, slots),
        out_shape=outs,
        in_specs=[pl.BlockSpec(memory_space=pltpu.SMEM)] + [vmem] * 2 + [hbm] * 5,
        out_specs=[vmem] * 7,
        scratch_shapes=[
            pltpu.SMEM((n,), jnp.int32),
            pltpu.SMEM((n,), jnp.int32),
            pltpu.VMEM((n, tok), jnp.float32),
            pltpu.VMEM((n, tok, model), bf16),
            pltpu.VMEM((n, tok, model), bf16),
            pltpu.VMEM((n, tok, model), bf16),
            pltpu.VMEM((n, n, tok), jnp.float32),
            pltpu.VMEM((2, n * tok, width), bf16),
            pltpu.VMEM((n * tok, width), bf16),
            pltpu.VMEM((2, n // 2, 2, tok, model), bf16),
            pltpu.VMEM((2, n // 2, tok, model), bf16),
            pltpu.VMEM((2, 4, tok, model), bf16),
            pltpu.VMEM((2, 4, 2, tok, model), bf16),
            pltpu.VMEM(v.shape, bf16),
            *(mover_scratch((1, *v.shape[1:]), n // 2, slots) * 3),
            *(mover_scratch(v.shape, n // 2, slots) * 2),
            dma((3, n)),
            dma((3, 2, 3)),
            dma((3, 4)),
            dma((3, 8)),
            dma((3,)),
            dma((3,)),
            dma((3,)),
            dma((2, 8)),
            dma((2, 8)),
            dma((2, 4)),
            dma((2, 4)),
            dma((2, 4)),
            dma((2, 4, 2)),
            dma((2,)),
            dma((2,)),
        ],
        compiler_params=pltpu.CompilerParams(
            collective_id=number, has_side_effects=True, vmem_limit_bytes=60 * 2**20
        ),
        cost_estimate=pl.CostEstimate(
            flops=15 * 10**9, bytes_accessed=200 * 2**20, transcendentals=0
        ),
    )(partner, ids, gate_values, x, cot, w, m, v)


def layer_and_step(slots, number, partner, ids, gate_values, x, cot, w, m, v):
    f32, bf16 = jnp.float32, jnp.bfloat16
    own_rows = w.shape[1]
    mixed, token_grad, keep, given, w_full, m_here, v_here = layer(
        slots, number, partner, ids, gate_values, x, cot, w, m, v
    )
    w_here = lax.dynamic_slice_in_dim(w_full, lax.axis_index("dp") * own_rows, own_rows, axis=1)
    grad = keep.astype(f32) + given.astype(f32)
    new_state = adam(*[a.astype(f32) for a in (w_here, m_here, v_here)], grad)
    return (mixed, token_grad, *[a.astype(bf16).transpose(1, 0, 2)[None] for a in new_state])


def shards_dense(
    tokens, cotangent, expert_ids, gate_weights, partner, weights, first_moment, second_moment
):
    half = lax.axis_size("expert") // 2
    number = jnp.arange(2 * half, dtype=jnp.int32)
    crossing = jnp.sum(jnp.where(partner >= half, number < half, False).astype(jnp.int32))
    old = [a[0].transpose(1, 0, 2) for a in (weights, first_moment, second_moment)]
    return lax.switch(
        jnp.where(crossing <= 4, 0, jnp.where(crossing <= 6, 1, 2)),
        [functools.partial(layer_and_step, slots, i) for i, slots in enumerate((4, 6, 8))],
        partner,
        expert_ids.T,
        gate_weights.T,
        tokens,
        cotangent,
        *old,
    )


def shards(*args):
    fits = lax.axis_size("dp") == 2 and lax.axis_size("expert") == 16
    if fits and args[0].shape[0] == 128 and args[5].shape[1] % 512 == 0:
        return shards_dense(*args)
    return shards_by_slot(*args)


def solution(mesh):
    in_specs = (
        P(("dp", "expert"), None),
        P(("dp", "expert"), None),
        P(("dp", "expert"), None),
        P(("dp", "expert"), None),
        P(),
        P("expert", "dp", None, None),
        P("expert", "dp", None, None),
        P("expert", "dp", None, None),
    )
    out_specs = (
        P(("dp", "expert"), None),
        P(("dp", "expert"), None),
        P("expert", "dp", None, None),
        P("expert", "dp", None, None),
        P("expert", "dp", None, None),
    )
    return jax.shard_map(shards, mesh=mesh, in_specs=in_specs, out_specs=out_specs, check_vma=False)
```

```python
import functools

import jax
import jax.numpy as jnp
from jax import lax
from jax.experimental import pallas as pl
from jax.experimental.pallas import tpu as pltpu
from jax.sharding import PartitionSpec as P

beta_one = 0.9
beta_two = 0.95
learn_rate = 0.01
decay_rate = 0.1
eps_adam = 1e-08
step_count = 100


def send_rows(parts):
    return (lax.all_to_all(parts[0], "expert", split_axis=0, concat_axis=0, tiled=True),)


def send_back(parts):
    return (lax.all_to_all(parts[0], "expert", split_axis=0, concat_axis=0, tiled=True),)


def shards_by_slot(
    tokens, cotangent, expert_ids, gate_weights, partner, weights, first_moment, second_moment
):
    experts_here = lax.axis_size("expert")
    tok_dev, model_width = tokens.shape
    top_count = expert_ids.shape[1]
    hidden_width = weights.shape[3]
    capacity = min(tok_dev, max(2, 5 * tok_dev * top_count // (4 * experts_here)))
    item_total = tok_dev * top_count
    slot_total = experts_here * capacity
    flat_ids = expert_ids.reshape(item_total)
    onehot = (flat_ids[:, None] == jnp.arange(experts_here, dtype=jnp.int32)[None, :]).astype(
        jnp.bfloat16
    )
    item_number = jnp.arange(item_total, dtype=jnp.int32)
    earlier = (item_number[:, None] > item_number[None, :]).astype(jnp.bfloat16)
    before = jnp.dot(earlier, onehot, preferred_element_type=jnp.float32)
    slot_of = jnp.sum(before * onehot.astype(jnp.float32), axis=1).astype(jnp.int32)
    position = flat_ids * capacity + slot_of
    source = (
        jnp.full((slot_total,), item_total, jnp.int32)
        .at[position]
        .set(jnp.arange(item_total, dtype=jnp.int32))
    )
    token_of = source // top_count
    zero_row = jnp.zeros((1, model_width), jnp.bfloat16)
    x_send = jnp.concatenate([tokens, zero_row], axis=0)[token_of].reshape(
        experts_here, capacity, model_width
    )
    gate_flat = gate_weights.reshape(item_total)
    gate_pad = jnp.concatenate([gate_flat, jnp.zeros((1,), jnp.float32)])
    cot_rows = jnp.concatenate([cotangent, zero_row], axis=0)[token_of].astype(jnp.float32)
    dy_send = (
        (gate_pad[source][:, None] * cot_rows)
        .astype(jnp.bfloat16)
        .reshape(experts_here, capacity, model_width)
    )
    gathered = lax.all_gather(weights, "dp", axis=1, tiled=True)[0]
    gate_up = gathered[:, 0:2, :].reshape(model_width, 2 * hidden_width)
    down_proj = gathered[:, 2, :]
    block_shape = (experts_here, capacity, model_width)
    (x_recv,) = send_rows((x_send,))
    forward_x_rows = x_recv.reshape(slot_total, model_width)
    both_proj = jnp.dot(forward_x_rows, gate_up, preferred_element_type=jnp.float32)
    pre_act = both_proj[:, :hidden_width]
    lin_act = both_proj[:, hidden_width:]
    sigmoid_pre = jax.nn.sigmoid(pre_act)
    silu_pre = pre_act * sigmoid_pre
    forward_hidden = (silu_pre * lin_act).astype(jnp.bfloat16)
    out_rows = jnp.dot(forward_hidden, down_proj.T, preferred_element_type=jnp.float32).astype(
        jnp.bfloat16
    )
    x_rows, saved, hidden, out_rows = (
        forward_x_rows,
        (pre_act, lin_act, sigmoid_pre, silu_pre),
        forward_hidden,
        out_rows,
    )
    (out_back,) = send_back((out_rows.reshape(block_shape),))
    (dy_recv,) = send_rows((dy_send,))
    pre_act, lin_act, sigmoid_pre, silu_pre = saved
    backward_dy_rows = dy_recv.reshape(slot_total, model_width)
    hidden_grad = jnp.dot(backward_dy_rows, down_proj, preferred_element_type=jnp.float32)
    pre_grad = (hidden_grad * lin_act * sigmoid_pre * (1.0 + pre_act * (1.0 - sigmoid_pre))).astype(
        jnp.bfloat16
    )
    lin_grad = (hidden_grad * silu_pre).astype(jnp.bfloat16)
    backward_both_grad = jnp.concatenate([pre_grad, lin_grad], axis=1)
    item_grad = jnp.dot(backward_both_grad, gate_up.T, preferred_element_type=jnp.float32).astype(
        jnp.bfloat16
    )
    dy_rows, both_grad, item_grad = (backward_dy_rows, backward_both_grad, item_grad)
    (grad_back,) = send_back((item_grad.reshape(block_shape),))
    out_items = (
        out_back.reshape(slot_total, model_width)[position].astype(jnp.float32) * gate_flat[:, None]
    )
    mixed = jnp.sum(out_items.reshape(tok_dev, top_count, model_width), axis=1).astype(jnp.bfloat16)
    grad_items = grad_back.reshape(slot_total, model_width)[position].astype(jnp.float32)
    token_grad = jnp.sum(grad_items.reshape(tok_dev, top_count, model_width), axis=1).astype(
        jnp.bfloat16
    )
    count = lax.axis_size("dp") * weights.shape[1]
    proj_grad = jnp.dot(x_rows.T, both_grad, preferred_element_type=jnp.float32)
    down_grad = jnp.dot(dy_rows.T, hidden, preferred_element_type=jnp.float32)
    grad_sum = lax.psum_scatter(
        jnp.concatenate(
            [proj_grad.reshape(count, 2, hidden_width), down_grad.reshape(count, 1, hidden_width)],
            axis=1,
        ).astype(jnp.bfloat16),
        "dp",
        scatter_dimension=0,
        tiled=True,
    ).astype(jnp.float32)
    w_old = weights[0].astype(jnp.float32)
    m_old = first_moment[0].astype(jnp.float32)
    v_old = second_moment[0].astype(jnp.float32)
    m_new = beta_one * m_old + (1.0 - beta_one) * grad_sum
    v_new = beta_two * v_old + (1.0 - beta_two) * grad_sum * grad_sum
    m_hat = m_new / (1.0 - beta_one**step_count)
    v_hat = v_new / (1.0 - beta_two**step_count)
    w_new = w_old - learn_rate * (m_hat / (jnp.sqrt(v_hat) + eps_adam) + decay_rate * w_old)
    pieces = (
        w_new.astype(jnp.bfloat16).reshape(experts_here, -1),
        m_new.astype(jnp.bfloat16).reshape(experts_here, -1),
        v_new.astype(jnp.bfloat16).reshape(experts_here, -1),
    )
    spread = (
        lax.all_to_all(pieces[0], "expert", split_axis=0, concat_axis=0, tiled=True),
        lax.all_to_all(pieces[1], "expert", split_axis=0, concat_axis=0, tiled=True),
        lax.all_to_all(pieces[2], "expert", split_axis=0, concat_axis=0, tiled=True),
    )
    ordered = (spread[0][partner], spread[1][partner], spread[2][partner])
    homed = (
        lax.all_to_all(ordered[0], "expert", split_axis=0, concat_axis=0, tiled=True),
        lax.all_to_all(ordered[1], "expert", split_axis=0, concat_axis=0, tiled=True),
        lax.all_to_all(ordered[2], "expert", split_axis=0, concat_axis=0, tiled=True),
    )
    new_weights = homed[0].reshape(weights.shape)
    new_first = homed[1].reshape(weights.shape)
    new_second = homed[2].reshape(weights.shape)
    return (mixed, token_grad, new_weights, new_first, new_second)


def adam(w_old, m_old, v_old, grad_sum):
    m_new = beta_one * m_old + (1.0 - beta_one) * grad_sum
    v_new = beta_two * v_old + (1.0 - beta_two) * grad_sum * grad_sum
    m_hat = m_new / (1.0 - beta_one**step_count)
    v_hat = v_new / (1.0 - beta_two**step_count)
    w_new = w_old - learn_rate * (m_hat / (jnp.sqrt(v_hat) + eps_adam) + decay_rate * w_old)
    return w_new, m_new, v_new


def plane_barrier(n, me):
    barrier = pltpu.get_barrier_semaphore()

    def body(step, carry):
        pl.semaphore_signal(
            barrier,
            inc=1,
            device_id={"expert": lax.rem(me + step, n)},
            device_id_type=pl.DeviceIdType.MESH,
        )
        return carry

    lax.fori_loop(1, n, body, 0)
    pl.semaphore_signal(
        barrier,
        inc=1,
        device_id={"dp": 1 - lax.axis_index("dp")},
        device_id_type=pl.DeviceIdType.MESH,
    )
    pl.semaphore_wait(barrier, n)


def remote(src, dst, send_sem, recv_sem, **where):
    return pltpu.make_async_remote_copy(
        src_ref=src,
        dst_ref=dst,
        send_sem=send_sem,
        recv_sem=recv_sem,
        device_id=where,
        device_id_type=pl.DeviceIdType.MESH,
    )


class Mover:
    def __init__(self, table, state, home, row_base, held, far, staged, sems):
        self.table, self.state, self.home, self.row_base = table, state, home, row_base
        self.held, self.far, self.staged = held, far, staged
        self.one_send, self.one_recv, self.b_send, self.b_recv = sems[:4]
        self.two_send, self.two_recv, self.own_sem = sems[4:]
        self.me = lax.axis_index("expert")
        self.n = staged.shape[0]
        self.slots = far.shape[0]
        self.side = self.me // self.n
        self.here = lax.rem(self.me, self.n)
        self.share = state.shape[1] // self.n

    def rows(self, number, base=0):
        return pl.ds(pl.multiple_of(base + number * self.share, self.share), self.share)

    def each(self, fn):
        def body(step, carry):
            fn(step, lax.rem(self.here + step, self.n))
            return carry

        lax.fori_loop(1, self.n, body, 0)

    def one(self, step, peer):
        return remote(
            self.state.at[:, self.rows(peer), :],
            self.held.at[self.here],
            self.one_send.at[step],
            self.one_recv.at[step],
            expert=self.side * self.n + peer,
        )

    def over(self, slot):
        return remote(
            self.staged.at[slot],
            self.far.at[slot],
            self.b_send.at[slot],
            self.b_recv.at[slot],
            expert=lax.rem(self.me + self.n, 2 * self.n),
        )

    def two(self, step, peer):
        return remote(
            self.staged.at[peer],
            self.home.at[:, self.rows(self.here, self.row_base), :],
            self.two_send.at[step],
            self.two_recv.at[step],
            expert=self.side * self.n + peer,
        )

    def own_share(self):
        return pltpu.make_async_copy(
            self.state.at[:, self.rows(self.here), :], self.held.at[self.here], self.own_sem
        )

    def spread_out(self):
        self.each(lambda step, peer: self.one(step, peer).start())
        self.own_share().start()

    def each_slot(self, fn):
        def body(slot, carry):
            fn(slot)
            return carry

        lax.fori_loop(0, self.slots, body, 0)

    def cross(self):
        self.each(lambda step, peer: self.one(step, peer).wait_recv())
        self.own_share().wait()

        def pick(slot):
            self.staged[slot] = self.held[self.table[self.n + slot]]
            self.over(slot).start()

        self.each_slot(pick)

    def send_home(self):
        self.each_slot(lambda slot: self.over(slot).wait())

        def chosen(home):
            at = self.table[home]
            near = self.held[jnp.minimum(at, self.n - 1)]
            return jnp.where(at < self.n, near, self.far[jnp.maximum(at - self.n, 0)])

        def pick(step, peer):
            self.staged[peer] = chosen(peer)
            self.two(step, peer).start()

        self.each(pick)
        self.home[:, self.rows(self.here, self.row_base), :] = chosen(self.here)

    def at_home(self, group):
        def body(number, carry):
            step = lax.rem(self.here - number + self.n, self.n)

            @pl.when(step > 0)
            def _():
                self.two(step, lax.rem(self.here + step, self.n)).wait_recv()

            return carry

        quarter = self.n // 4
        lax.fori_loop(group * quarter, (group + 1) * quarter, body, 0)

    def sends_done(self):
        self.each(lambda step, peer: self.one(step, peer).wait_send())
        self.each(lambda step, peer: self.two(step, peer).wait_send())


def mover_scratch(shape, n, slots):
    planes, own_rows, width = shape
    part = (planes, own_rows // n, width)
    dma = pltpu.SemaphoreType.DMA
    return [
        pltpu.VMEM((n, *part), jnp.bfloat16),
        pltpu.VMEM((slots, *part), jnp.bfloat16),
        pltpu.VMEM((n, *part), jnp.bfloat16),
        dma((n,)),
        dma((n,)),
        dma((slots,)),
        dma((slots,)),
        dma((n,)),
        dma((n,)),
        dma,
    ]


class Spreader:
    def __init__(self, partner, state, home, row_base, spread, ordered, sems):
        self.partner, self.state, self.home, self.row_base = partner, state, home, row_base
        self.spread, self.ordered = spread, ordered
        self.one_send, self.one_recv, self.two_send, self.two_recv, self.own_sem = sems
        self.me = lax.axis_index("expert")
        self.n = spread.shape[0]
        self.share = state.shape[1] // self.n

    def rows(self, number, base=0):
        return pl.ds(pl.multiple_of(base + number * self.share, self.share), self.share)

    def each(self, fn):
        def body(step, carry):
            fn(step, lax.rem(self.me + step, self.n))
            return carry

        lax.fori_loop(1, self.n, body, 0)

    def one(self, step, peer):
        return remote(
            self.state.at[:, self.rows(peer), :],
            self.spread.at[self.me],
            self.one_send.at[step],
            self.one_recv.at[step],
            expert=peer,
        )

    def two(self, step, peer):
        return remote(
            self.ordered.at[peer],
            self.home.at[:, self.rows(self.me, self.row_base), :],
            self.two_send.at[step],
            self.two_recv.at[step],
            expert=peer,
        )

    def spread_out(self):
        self.each(lambda step, peer: self.one(step, peer).start())
        self.own_share().start()

    def own_share(self):
        return pltpu.make_async_copy(
            self.state.at[:, self.rows(self.me), :], self.spread.at[self.me], self.own_sem
        )

    def send_home(self):
        self.each(lambda step, peer: self.one(step, peer).wait_recv())
        self.own_share().wait()

        def pick(step, carry):
            peer = lax.rem(self.me + step, self.n)
            self.ordered[peer] = self.spread[self.partner[peer]]
            self.two(step, peer).start()
            return carry

        lax.fori_loop(1, self.n, pick, 0)
        self.home[:, self.rows(self.me, self.row_base), :] = self.spread[self.partner[self.me]]

    def at_home(self, group):
        def body(number, carry):
            step = lax.rem(self.me - number + self.n, self.n)

            @pl.when(step > 0)
            def _():
                self.two(step, lax.rem(self.me + step, self.n)).wait_recv()

            return carry

        quarter = self.n // 4
        lax.fori_loop(group * quarter, (group + 1) * quarter, body, 0)

    def sends_done(self):
        self.each(lambda step, peer: self.one(step, peer).wait_send())
        self.each(lambda step, peer: self.two(step, peer).wait_send())


def spreader_scratch(shape, n):
    planes, own_rows, width = shape
    part = (n, planes, own_rows // n, width)
    return [pltpu.VMEM(part, jnp.bfloat16)] * 2 + [pltpu.SemaphoreType.DMA((n,))] * 4 + [pltpu.SemaphoreType.DMA]


def fill_tables(partner, table, rank, slots):
    n = partner.shape[0] // 2
    side = lax.axis_index("expert") // n
    for s in range(2):
        count = jnp.int32(0)
        for i in range(n):
            rank[s * n + i] = count
            count = count + jnp.where(partner[s * n + i] // n != s, 1, 0)
    for d in range(n):
        p = partner[side * n + d]
        table[d] = jnp.where(p // n == side, lax.rem(p, n), n + rank[p])
    for j in range(slots):
        chosen = jnp.int32(0)
        for i in range(n):
            hit = jnp.logical_and(partner[side * n + i] // n != side, rank[side * n + i] == j)
            chosen = jnp.where(hit, i, chosen)
        table[n + j] = chosen


def layer_kernel(
    slots,
    partner,
    ids,
    gate_values,
    x,
    cot,
    w,
    m,
    v,
    mixed,
    token_grad,
    keep,
    given,
    w_full,
    m_home,
    v_home,
    table,
    rank,
    gates,
    x_all,
    cot_all,
    dy_all,
    gate_all,
    both_all,
    hidden_all,
    part,
    from_core,
    from_over,
    from_line,
    give,
    *scratch,
):
    f32, bf16 = jnp.float32, jnp.bfloat16
    me = lax.axis_index("expert")
    half = lax.axis_index("dp")
    own_rows, width = w.shape[1], w.shape[2]
    tok = x.shape[0]
    z, y, core = me // 4, lax.rem(me // 2, 2), lax.rem(me, 2)
    movers = []
    moved = [(w.at[pl.ds(i, 1)], w_full.at[pl.ds(i, 1)], half * own_rows) for i in range(3)]
    for state, home, base in moved:
        own, scratch = scratch[:7], scratch[7:]
        movers.append(Spreader(partner, state, home, base, *own[:2], own[2:]))
    for state, home, base in ((m, m_home, 0), (v, v_home, 0)):
        own, scratch = scratch[:10], scratch[10:]
        movers.append(Mover(table, state, home, base, *own[:3], own[3:]))
    w_moves, m_move, v_move = movers[:3], movers[3], movers[4]
    block_recv, z_send, y_send, c_send, x_send, x_recv, own_sem = scratch[:7]
    s_send, s_recv, o_send, o_recv, l_send, l_recv, g_send, g_recv = scratch[7:]
    arrays = ((x, x_all), (cot, cot_all), (gates, gate_all))

    def hop(i, number, own, send_sem, dest):
        source, full = arrays[i]
        return remote(
            source if own else full.at[number],
            full.at[number],
            send_sem,
            block_recv.at[i, number],
            expert=dest,
        )

    def number_of(zz, yy, cc):
        return zz * 4 + yy * 2 + cc

    def down(i, s):
        return hop(i, number_of(z + s, y, core), s == 0, z_send.at[i, 0, s], me - 4)

    def up(i, s):
        return hop(i, number_of(z - s, y, core), s == 0, z_send.at[i, 1, s], me + 4)

    def over(i, zz, own=False):
        return hop(i, number_of(zz, y, core), own, y_send.at[i, zz], number_of(z, 1 - y, core))

    def beside(i, zz, yy, own=False):
        return hop(
            i, number_of(zz, yy, core), own, c_send.at[i, zz * 2 + yy], number_of(z, y, 1 - core)
        )

    def wait_block(i, number):
        hop(i, number, False, y_send.at[i, 0], lax.rem(me + 1, 16)).wait_recv()

    def passed_on(zz, which):
        for i in which:
            over(i, zz).start()
        for i in which:
            beside(i, zz, y).start()

    def line_step(s, which):
        @pl.when(z + 1 + s <= 3)
        def _():
            for i in which:
                wait_block(i, number_of(z + 1 + s, y, core))
                if s < 2:

                    @pl.when(z >= 1)
                    def _():
                        down(i, s + 1).start()

            passed_on(z + 1 + s, which)

        @pl.when(z - 1 - s >= 0)
        def _():
            for i in which:
                wait_block(i, number_of(z - 1 - s, y, core))
                if s < 2:

                    @pl.when(z <= 2)
                    def _():
                        up(i, s + 1).start()

            passed_on(z - 1 - s, which)

    def gate_column(b):
        mine = lax.broadcasted_iota(jnp.int32, gates.shape, 0) == partner[me]
        columns = []
        for side in range(2):
            row = jnp.sum(jnp.where(mine, gate_all[b * 2 + side], 0.0), axis=0, keepdims=True)
            columns.append(jnp.broadcast_to(row, (tok, tok)).T[:, :1])
        return jnp.concatenate(columns, axis=0)

    def to_core(i, b):
        return remote(
            part.at[i, b, 1 - core],
            from_core.at[i, b],
            s_send.at[i, b],
            s_recv.at[i, b],
            expert=z * 4 + y * 2 + 1 - core,
        )

    def to_over(i, zz):
        return remote(
            part.at[i, zz * 2 + 1 - y, core],
            from_over.at[i, zz],
            o_send.at[i, zz],
            o_recv.at[i, zz],
            expert=z * 4 + (1 - y) * 2 + core,
        )

    def on_line(i, zz, way):
        return remote(
            part.at[i, zz * 2 + y, core],
            from_line.at[i, zz, way],
            l_send.at[i, zz],
            l_recv.at[i, zz, way],
            expert=me + (4 if way else -4),
        )

    def added(i, b, source):
        part[i, b, core] = (part[i, b, core].astype(f32) + source.astype(f32)).astype(bf16)

    def place(t):
        mid = jnp.where(t <= 1, 3 - t, t - 2)
        return jnp.where(z == 0, 3 - t, jnp.where(z == 1, mid, jnp.where(z == 2, 3 - mid, t)))

    def chip_of(t):
        over = t < 4
        return place(lax.rem(t, 4)) * 2 + jnp.where(over, 1 - y, y)

    last = (((1,), (1,)), ((), ()))

    def forward_step(t):
        b = chip_of(t)
        rows = pl.ds(pl.multiple_of(b * 2 * tok, 256), 2 * tok)
        x_rows = x_all[pl.ds(b * 2, 2)].reshape(2 * tok, x_all.shape[2])
        pre_act = jnp.dot(x_rows, w_full[0], preferred_element_type=f32)
        lin_act = jnp.dot(x_rows, w_full[1], preferred_element_type=f32)
        sig = jax.nn.sigmoid(pre_act)
        silu = pre_act * sig
        hidden = (silu * lin_act).astype(bf16)
        hidden_all[rows, :] = hidden
        both_all[0, rows, :] = (lin_act * sig * (1.0 + pre_act * (1.0 - sig))).astype(bf16)
        both_all[1, rows, :] = silu.astype(bf16)
        out = lax.dot_general(hidden, w_full[2], last, preferred_element_type=f32)
        part[0, b] = (gate_column(b) * out).astype(bf16).reshape(2, tok, out.shape[1])
        to_core(0, b).start()

    def backward_step(t):
        b = chip_of(t)
        rows = pl.ds(pl.multiple_of(b * 2 * tok, 256), 2 * tok)
        cot_rows = cot_all[pl.ds(b * 2, 2)].reshape(2 * tok, x_all.shape[2])
        dy = (gate_column(b) * cot_rows.astype(f32)).astype(bf16)
        dy_all[pl.ds(b * 2, 2)] = dy.reshape(2, tok, x_all.shape[2])
        hidden_grad = jnp.dot(dy, w_full[2], preferred_element_type=f32)
        pre_grad = (hidden_grad * both_all[0, rows, :].astype(f32)).astype(bf16)
        lin_grad = (hidden_grad * both_all[1, rows, :].astype(f32)).astype(bf16)
        both_all[0, rows, :] = pre_grad
        both_all[1, rows, :] = lin_grad
        item = lax.dot_general(pre_grad, w_full[0], last, preferred_element_type=f32)
        item = item + lax.dot_general(lin_grad, w_full[1], last, preferred_element_type=f32)
        part[1, b] = item.astype(bf16).reshape(2, tok, item.shape[1])
        to_core(1, b).start()

    def core_sum(i, t):
        b = chip_of(t)
        to_core(i, b).wait_recv()
        added(i, b, from_core[i, b])

        @pl.when(t < 4)
        def _():
            to_over(i, b // 2).start()

    def own_block(i):
        return pltpu.make_async_copy(arrays[i][0], arrays[i][1].at[me], own_sem.at[i])

    def from_y(zz, which):
        for i in which:
            wait_block(i, number_of(zz, 1 - y, core))
            beside(i, zz, 1 - y).start()

    def exchange(plane):
        rows = pl.ds(pl.multiple_of(half * own_rows, own_rows), own_rows)
        part_rows = w_full.at[plane, rows, :]
        return remote(part_rows, part_rows, x_send.at[plane], x_recv.at[plane], dp=1 - half)

    def w_home(plane):
        for g in range(4):
            w_moves[plane].at_home(g)
        exchange(plane).start()

    plane_barrier(16, me)
    for move in w_moves:
        move.spread_out()
    number = lax.broadcasted_iota(jnp.int32, gates.shape, 0)
    total = jnp.zeros(gates.shape, f32)
    for k in range(ids.shape[0]):
        named = jnp.broadcast_to(ids[k : k + 1, :], gates.shape) == number
        total = total + jnp.where(named, gate_values[k : k + 1, :], 0.0)
    gates[...] = total
    def first_sends(which):
        for i in which:

            @pl.when(z >= 1)
            def _():
                down(i, 0).start()

            @pl.when(z <= 2)
            def _():
                up(i, 0).start()

            over(i, z, True).start()
            beside(i, z, y, True).start()
            own_block(i).start()

    def all_from_y(which):
        from_y(z, which)
        for s in range(3):

            @pl.when(z + 1 + s <= 3)
            def _():
                from_y(z + 1 + s, which)

            @pl.when(z - 1 - s >= 0)
            def _():
                from_y(z - 1 - s, which)

    def all_beside(which):
        for i in which:
            own_block(i).wait()
            for zz in range(4):
                for yy in range(2):
                    wait_block(i, number_of(zz, yy, 1 - core))

    rows_first, rows_later = (2, 0), (1,)
    first_sends(rows_first)
    fill_tables(partner, table, rank, slots)
    m_move.spread_out()
    line_step(0, rows_first)
    first_sends(rows_later)
    w_moves[0].send_home()
    line_step(1, rows_first)
    w_moves[1].send_home()
    w_home(0)
    line_step(2, rows_first)
    w_moves[2].send_home()
    line_step(0, rows_later)
    w_home(1)
    all_from_y(rows_first)
    w_home(2)
    m_move.cross()
    line_step(1, rows_later)
    line_step(2, rows_later)
    v_move.spread_out()
    m_move.send_home()
    all_beside(rows_first)
    for plane in range(3):
        exchange(plane).wait()

    def forward(t, carry):
        forward_step(t)

        @pl.when(t >= 1)
        def _():
            core_sum(0, t - 1)

        return carry

    lax.fori_loop(0, 8, forward, 0)
    core_sum(0, 7)
    all_from_y(rows_later)
    v_move.cross()
    all_beside(rows_later)

    def backward(t, carry):
        backward_step(t)

        @pl.when(t >= 1)
        def _():
            core_sum(1, t - 1)

        return carry

    lax.fori_loop(0, 8, backward, 0)
    core_sum(1, 7)

    tile = own_rows // 2

    def weight_grads(base, put):
        def body(j, carry):
            rows = pl.ds(pl.multiple_of(base + j * tile, 256), tile)
            first = (((0,), (0,)), ((), ()))
            x_cols = x_all[:, :, rows].reshape(-1, tile)
            dy_cols = dy_all[:, :, rows].reshape(-1, tile)
            put(0, j, lax.dot_general(x_cols, both_all[0], first, preferred_element_type=f32))
            put(1, j, lax.dot_general(x_cols, both_all[1], first, preferred_element_type=f32))
            put(2, j, lax.dot_general(dy_cols, hidden_all[...], first, preferred_element_type=f32))
            return carry

        lax.fori_loop(0, 2, body, 0)

    def gift(j):
        rows = pl.ds(pl.multiple_of(j * tile, 256), tile)
        return remote(
            give.at[:, rows, :], given.at[:, rows, :], g_send.at[j], g_recv.at[j], dp=1 - half
        )

    def put_give(plane, j, value):
        give[plane, pl.ds(pl.multiple_of(j * tile, 256), tile), :] = value.astype(bf16)
        if plane == 2:
            gift(j).start()

    def put_keep(plane, j, value):
        keep[plane, pl.ds(pl.multiple_of(j * tile, 256), tile), :] = value.astype(bf16)

    def over_sum(i, zz):
        to_over(i, zz).wait_recv()
        added(i, zz * 2 + y, from_over[i, zz])

    def line_sums(i, far):
        for way in (1, 0):
            zz = z + far if way else z - far

            @pl.when(zz <= 3 if way else zz >= 0)
            def _():
                over_sum(i, zz)

                @pl.when(z >= 1 if way else z <= 2)
                def _():
                    on_line(i, zz, way).wait_recv()
                    added(i, zz * 2 + y, from_line[i, zz, way])

                on_line(i, zz, way).start()

    line_sums(0, 3)
    weight_grads((1 - half) * own_rows, put_give)
    line_sums(0, 2)
    v_move.send_home()
    line_sums(1, 3)
    line_sums(0, 1)
    weight_grads(half * own_rows, put_keep)
    line_sums(1, 2)
    line_sums(1, 1)
    for i, out in ((0, mixed), (1, token_grad)):
        over_sum(i, z)

        @pl.when(z >= 1)
        def _():
            on_line(i, z, 1).wait_recv()
            added(i, z * 2 + y, from_line[i, z, 1])

        @pl.when(z <= 2)
        def _():
            on_line(i, z, 0).wait_recv()
            added(i, z * 2 + y, from_line[i, z, 0])

        out[...] = part[i, z * 2 + y, core]
    for g in range(4):
        m_move.at_home(g)
        v_move.at_home(g)
    for j in range(2):
        gift(j).wait()
    for move in w_moves:
        move.sends_done()
    for i in range(3):
        for s in range(3):

            @pl.when(jnp.logical_and(z >= 1, z + s <= 3))
            def _():
                down(i, s).wait_send()

            @pl.when(jnp.logical_and(z <= 2, z - s >= 0))
            def _():
                up(i, s).wait_send()

        for zz in range(4):
            over(i, zz).wait_send()
            for yy in range(2):
                beside(i, zz, yy).wait_send()
    m_move.sends_done()
    v_move.sends_done()
    for i in range(2):
        for b in range(8):
            to_core(i, b).wait_send()
        for zz in range(4):
            to_over(i, zz).wait_send()

            @pl.when(zz != z)
            def _():
                on_line(i, zz, 1).wait_send()


def layer(slots, number, partner, ids, gate_values, x, cot, w, m, v):
    n = lax.axis_size("expert")
    vmem = pl.BlockSpec(memory_space=pltpu.VMEM)
    hbm = pl.BlockSpec(memory_space=pl.ANY)
    tok, model = x.shape
    planes, own_rows, width = v.shape
    bf16 = jnp.bfloat16
    dma = pltpu.SemaphoreType.DMA
    outs = [
        jax.ShapeDtypeStruct((tok, model), bf16),
        jax.ShapeDtypeStruct((tok, model), bf16),
        jax.ShapeDtypeStruct(v.shape, bf16),
        jax.ShapeDtypeStruct(v.shape, bf16),
        jax.ShapeDtypeStruct((planes, 2 * own_rows, width), bf16),
        jax.ShapeDtypeStruct(v.shape, bf16),
        jax.ShapeDtypeStruct(v.shape, bf16),
    ]
    return pl.pallas_call(
        functools.partial(layer_kernel, slots),
        out_shape=outs,
        in_specs=[pl.BlockSpec(memory_space=pltpu.SMEM)] + [vmem] * 2 + [hbm] * 5,
        out_specs=[vmem] * 7,
        scratch_shapes=[
            pltpu.SMEM((n,), jnp.int32),
            pltpu.SMEM((n,), jnp.int32),
            pltpu.VMEM((n, tok), jnp.float32),
            pltpu.VMEM((n, tok, model), bf16),
            pltpu.VMEM((n, tok, model), bf16),
            pltpu.VMEM((n, tok, model), bf16),
            pltpu.VMEM((n, n, tok), jnp.float32),
            pltpu.VMEM((2, n * tok, width), bf16),
            pltpu.VMEM((n * tok, width), bf16),
            pltpu.VMEM((2, n // 2, 2, tok, model), bf16),
            pltpu.VMEM((2, n // 2, tok, model), bf16),
            pltpu.VMEM((2, 4, tok, model), bf16),
            pltpu.VMEM((2, 4, 2, tok, model), bf16),
            pltpu.VMEM(v.shape, bf16),
            *(spreader_scratch((1, *v.shape[1:]), n) * 3),
            *(mover_scratch(v.shape, n // 2, slots) * 2),
            dma((3, n)),
            dma((3, 2, 3)),
            dma((3, 4)),
            dma((3, 8)),
            dma((3,)),
            dma((3,)),
            dma((3,)),
            dma((2, 8)),
            dma((2, 8)),
            dma((2, 4)),
            dma((2, 4)),
            dma((2, 4)),
            dma((2, 4, 2)),
            dma((2,)),
            dma((2,)),
        ],
        compiler_params=pltpu.CompilerParams(
            collective_id=number, has_side_effects=True, vmem_limit_bytes=60 * 2**20
        ),
        cost_estimate=pl.CostEstimate(
            flops=15 * 10**9, bytes_accessed=200 * 2**20, transcendentals=0
        ),
    )(partner, ids, gate_values, x, cot, w, m, v)


def layer_and_step(slots, number, partner, ids, gate_values, x, cot, w, m, v):
    f32, bf16 = jnp.float32, jnp.bfloat16
    own_rows = w.shape[1]
    mixed, token_grad, keep, given, w_full, m_here, v_here = layer(
        slots, number, partner, ids, gate_values, x, cot, w, m, v
    )
    w_here = lax.dynamic_slice_in_dim(w_full, lax.axis_index("dp") * own_rows, own_rows, axis=1)
    grad = keep.astype(f32) + given.astype(f32)
    new_state = adam(*[a.astype(f32) for a in (w_here, m_here, v_here)], grad)
    return (mixed, token_grad, *[a.astype(bf16).transpose(1, 0, 2)[None] for a in new_state])


def shards_dense(
    tokens, cotangent, expert_ids, gate_weights, partner, weights, first_moment, second_moment
):
    half = lax.axis_size("expert") // 2
    number = jnp.arange(2 * half, dtype=jnp.int32)
    crossing = jnp.sum(jnp.where(partner >= half, number < half, False).astype(jnp.int32))
    old = [a[0].transpose(1, 0, 2) for a in (weights, first_moment, second_moment)]
    return lax.switch(
        jnp.where(crossing <= 4, 0, jnp.where(crossing <= 6, 1, 2)),
        [functools.partial(layer_and_step, slots, i) for i, slots in enumerate((4, 6, 8))],
        partner,
        expert_ids.T,
        gate_weights.T,
        tokens,
        cotangent,
        *old,
    )


def shards(*args):
    fits = lax.axis_size("dp") == 2 and lax.axis_size("expert") == 16
    if fits and args[0].shape[0] == 128 and args[5].shape[1] % 512 == 0:
        return shards_dense(*args)
    return shards_by_slot(*args)


def solution(mesh):
    in_specs = (
        P(("dp", "expert"), None),
        P(("dp", "expert"), None),
        P(("dp", "expert"), None),
        P(("dp", "expert"), None),
        P(),
        P("expert", "dp", None, None),
        P("expert", "dp", None, None),
        P("expert", "dp", None, None),
    )
    out_specs = (
        P(("dp", "expert"), None),
        P(("dp", "expert"), None),
        P("expert", "dp", None, None),
        P("expert", "dp", None, None),
        P("expert", "dp", None, None),
    )
    return jax.shard_map(shards, mesh=mesh, in_specs=in_specs, out_specs=out_specs, check_vma=False)
```

```python
import functools

import jax
import jax.numpy as jnp
from jax import lax
from jax.experimental import pallas as pl
from jax.experimental.pallas import tpu as pltpu
from jax.sharding import PartitionSpec as P

beta_one = 0.9
beta_two = 0.95
learn_rate = 0.01
decay_rate = 0.1
eps_adam = 1e-08
step_count = 100


def send_rows(parts):
    return (lax.all_to_all(parts[0], "expert", split_axis=0, concat_axis=0, tiled=True),)


def send_back(parts):
    return (lax.all_to_all(parts[0], "expert", split_axis=0, concat_axis=0, tiled=True),)


def shards_by_slot(
    tokens, cotangent, expert_ids, gate_weights, partner, weights, first_moment, second_moment
):
    experts_here = lax.axis_size("expert")
    tok_dev, model_width = tokens.shape
    top_count = expert_ids.shape[1]
    hidden_width = weights.shape[3]
    capacity = min(tok_dev, max(2, 5 * tok_dev * top_count // (4 * experts_here)))
    item_total = tok_dev * top_count
    slot_total = experts_here * capacity
    flat_ids = expert_ids.reshape(item_total)
    onehot = (flat_ids[:, None] == jnp.arange(experts_here, dtype=jnp.int32)[None, :]).astype(
        jnp.bfloat16
    )
    item_number = jnp.arange(item_total, dtype=jnp.int32)
    earlier = (item_number[:, None] > item_number[None, :]).astype(jnp.bfloat16)
    before = jnp.dot(earlier, onehot, preferred_element_type=jnp.float32)
    slot_of = jnp.sum(before * onehot.astype(jnp.float32), axis=1).astype(jnp.int32)
    position = flat_ids * capacity + slot_of
    source = (
        jnp.full((slot_total,), item_total, jnp.int32)
        .at[position]
        .set(jnp.arange(item_total, dtype=jnp.int32))
    )
    token_of = source // top_count
    zero_row = jnp.zeros((1, model_width), jnp.bfloat16)
    x_send = jnp.concatenate([tokens, zero_row], axis=0)[token_of].reshape(
        experts_here, capacity, model_width
    )
    gate_flat = gate_weights.reshape(item_total)
    gate_pad = jnp.concatenate([gate_flat, jnp.zeros((1,), jnp.float32)])
    cot_rows = jnp.concatenate([cotangent, zero_row], axis=0)[token_of].astype(jnp.float32)
    dy_send = (
        (gate_pad[source][:, None] * cot_rows)
        .astype(jnp.bfloat16)
        .reshape(experts_here, capacity, model_width)
    )
    gathered = lax.all_gather(weights, "dp", axis=1, tiled=True)[0]
    gate_up = gathered[:, 0:2, :].reshape(model_width, 2 * hidden_width)
    down_proj = gathered[:, 2, :]
    block_shape = (experts_here, capacity, model_width)
    (x_recv,) = send_rows((x_send,))
    forward_x_rows = x_recv.reshape(slot_total, model_width)
    both_proj = jnp.dot(forward_x_rows, gate_up, preferred_element_type=jnp.float32)
    pre_act = both_proj[:, :hidden_width]
    lin_act = both_proj[:, hidden_width:]
    sigmoid_pre = jax.nn.sigmoid(pre_act)
    silu_pre = pre_act * sigmoid_pre
    forward_hidden = (silu_pre * lin_act).astype(jnp.bfloat16)
    out_rows = jnp.dot(forward_hidden, down_proj.T, preferred_element_type=jnp.float32).astype(
        jnp.bfloat16
    )
    x_rows, saved, hidden, out_rows = (
        forward_x_rows,
        (pre_act, lin_act, sigmoid_pre, silu_pre),
        forward_hidden,
        out_rows,
    )
    (out_back,) = send_back((out_rows.reshape(block_shape),))
    (dy_recv,) = send_rows((dy_send,))
    pre_act, lin_act, sigmoid_pre, silu_pre = saved
    backward_dy_rows = dy_recv.reshape(slot_total, model_width)
    hidden_grad = jnp.dot(backward_dy_rows, down_proj, preferred_element_type=jnp.float32)
    pre_grad = (hidden_grad * lin_act * sigmoid_pre * (1.0 + pre_act * (1.0 - sigmoid_pre))).astype(
        jnp.bfloat16
    )
    lin_grad = (hidden_grad * silu_pre).astype(jnp.bfloat16)
    backward_both_grad = jnp.concatenate([pre_grad, lin_grad], axis=1)
    item_grad = jnp.dot(backward_both_grad, gate_up.T, preferred_element_type=jnp.float32).astype(
        jnp.bfloat16
    )
    dy_rows, both_grad, item_grad = (backward_dy_rows, backward_both_grad, item_grad)
    (grad_back,) = send_back((item_grad.reshape(block_shape),))
    out_items = (
        out_back.reshape(slot_total, model_width)[position].astype(jnp.float32) * gate_flat[:, None]
    )
    mixed = jnp.sum(out_items.reshape(tok_dev, top_count, model_width), axis=1).astype(jnp.bfloat16)
    grad_items = grad_back.reshape(slot_total, model_width)[position].astype(jnp.float32)
    token_grad = jnp.sum(grad_items.reshape(tok_dev, top_count, model_width), axis=1).astype(
        jnp.bfloat16
    )
    count = lax.axis_size("dp") * weights.shape[1]
    proj_grad = jnp.dot(x_rows.T, both_grad, preferred_element_type=jnp.float32)
    down_grad = jnp.dot(dy_rows.T, hidden, preferred_element_type=jnp.float32)
    grad_sum = lax.psum_scatter(
        jnp.concatenate(
            [proj_grad.reshape(count, 2, hidden_width), down_grad.reshape(count, 1, hidden_width)],
            axis=1,
        ).astype(jnp.bfloat16),
        "dp",
        scatter_dimension=0,
        tiled=True,
    ).astype(jnp.float32)
    w_old = weights[0].astype(jnp.float32)
    m_old = first_moment[0].astype(jnp.float32)
    v_old = second_moment[0].astype(jnp.float32)
    m_new = beta_one * m_old + (1.0 - beta_one) * grad_sum
    v_new = beta_two * v_old + (1.0 - beta_two) * grad_sum * grad_sum
    m_hat = m_new / (1.0 - beta_one**step_count)
    v_hat = v_new / (1.0 - beta_two**step_count)
    w_new = w_old - learn_rate * (m_hat / (jnp.sqrt(v_hat) + eps_adam) + decay_rate * w_old)
    pieces = (
        w_new.astype(jnp.bfloat16).reshape(experts_here, -1),
        m_new.astype(jnp.bfloat16).reshape(experts_here, -1),
        v_new.astype(jnp.bfloat16).reshape(experts_here, -1),
    )
    spread = (
        lax.all_to_all(pieces[0], "expert", split_axis=0, concat_axis=0, tiled=True),
        lax.all_to_all(pieces[1], "expert", split_axis=0, concat_axis=0, tiled=True),
        lax.all_to_all(pieces[2], "expert", split_axis=0, concat_axis=0, tiled=True),
    )
    ordered = (spread[0][partner], spread[1][partner], spread[2][partner])
    homed = (
        lax.all_to_all(ordered[0], "expert", split_axis=0, concat_axis=0, tiled=True),
        lax.all_to_all(ordered[1], "expert", split_axis=0, concat_axis=0, tiled=True),
        lax.all_to_all(ordered[2], "expert", split_axis=0, concat_axis=0, tiled=True),
    )
    new_weights = homed[0].reshape(weights.shape)
    new_first = homed[1].reshape(weights.shape)
    new_second = homed[2].reshape(weights.shape)
    return (mixed, token_grad, new_weights, new_first, new_second)


def adam(w_old, m_old, v_old, grad_sum):
    m_new = beta_one * m_old + (1.0 - beta_one) * grad_sum
    v_new = beta_two * v_old + (1.0 - beta_two) * grad_sum * grad_sum
    m_hat = m_new * (1.0 / (1.0 - beta_one**step_count))
    v_hat = v_new * (1.0 / (1.0 - beta_two**step_count))
    w_new = w_old - learn_rate * (m_hat / (jnp.sqrt(v_hat) + eps_adam) + decay_rate * w_old)
    return w_new, m_new, v_new


def plane_barrier(n, me):
    barrier = pltpu.get_barrier_semaphore()

    def body(step, carry):
        pl.semaphore_signal(
            barrier,
            inc=1,
            device_id={"expert": lax.rem(me + step, n)},
            device_id_type=pl.DeviceIdType.MESH,
        )
        return carry

    lax.fori_loop(1, n, body, 0)
    pl.semaphore_signal(
        barrier,
        inc=1,
        device_id={"dp": 1 - lax.axis_index("dp")},
        device_id_type=pl.DeviceIdType.MESH,
    )
    pl.semaphore_wait(barrier, n)


def remote(src, dst, send_sem, recv_sem, **where):
    return pltpu.make_async_remote_copy(
        src_ref=src,
        dst_ref=dst,
        send_sem=send_sem,
        recv_sem=recv_sem,
        device_id=where,
        device_id_type=pl.DeviceIdType.MESH,
    )


class Mover:
    def __init__(self, table, state, home, row_base, held, far, staged, sems):
        self.table, self.state, self.home, self.row_base = table, state, home, row_base
        self.held, self.far, self.staged = held, far, staged
        self.one_send, self.one_recv, self.b_send, self.b_recv = sems[:4]
        self.two_send, self.two_recv, self.own_sem = sems[4:]
        self.me = lax.axis_index("expert")
        self.n = staged.shape[0]
        self.slots = far.shape[0]
        self.side = self.me // self.n
        self.here = lax.rem(self.me, self.n)
        self.share = state.shape[1] // self.n

    def rows(self, number, base=0):
        return pl.ds(pl.multiple_of(base + number * self.share, self.share), self.share)

    def each(self, fn):
        def body(step, carry):
            fn(step, lax.rem(self.here + step, self.n))
            return carry

        lax.fori_loop(1, self.n, body, 0)

    def one(self, step, peer):
        return remote(
            self.state.at[:, self.rows(peer), :],
            self.held.at[self.here],
            self.one_send.at[step],
            self.one_recv.at[step],
            expert=self.side * self.n + peer,
        )

    def over(self, slot):
        return remote(
            self.staged.at[slot],
            self.far.at[slot],
            self.b_send.at[slot],
            self.b_recv.at[slot],
            expert=lax.rem(self.me + self.n, 2 * self.n),
        )

    def two(self, step, peer):
        return remote(
            self.staged.at[peer],
            self.home.at[:, self.rows(self.here, self.row_base), :],
            self.two_send.at[step],
            self.two_recv.at[step],
            expert=self.side * self.n + peer,
        )

    def own_share(self):
        return pltpu.make_async_copy(
            self.state.at[:, self.rows(self.here), :], self.held.at[self.here], self.own_sem
        )

    def spread_out(self):
        self.each(lambda step, peer: self.one(step, peer).start())
        self.own_share().start()

    def each_slot(self, fn):
        def body(slot, carry):
            fn(slot)
            return carry

        lax.fori_loop(0, self.slots, body, 0)

    def cross(self):
        self.each(lambda step, peer: self.one(step, peer).wait_recv())
        self.own_share().wait()

        def pick(slot):
            self.staged[slot] = self.held[self.table[self.n + slot]]
            self.over(slot).start()

        self.each_slot(pick)

    def send_home(self):
        self.each_slot(lambda slot: self.over(slot).wait())

        def chosen(home):
            at = self.table[home]
            near = self.held[jnp.minimum(at, self.n - 1)]
            return jnp.where(at < self.n, near, self.far[jnp.maximum(at - self.n, 0)])

        def pick(step, peer):
            self.staged[peer] = chosen(peer)
            self.two(step, peer).start()

        self.each(pick)
        self.home[:, self.rows(self.here, self.row_base), :] = chosen(self.here)

    def at_home(self, group):
        def body(number, carry):
            step = lax.rem(self.here - number + self.n, self.n)

            @pl.when(step > 0)
            def _():
                self.two(step, lax.rem(self.here + step, self.n)).wait_recv()

            return carry

        quarter = self.n // 4
        lax.fori_loop(group * quarter, (group + 1) * quarter, body, 0)

    def sends_done(self):
        self.each(lambda step, peer: self.one(step, peer).wait_send())
        self.each(lambda step, peer: self.two(step, peer).wait_send())


def mover_scratch(shape, n, slots):
    planes, own_rows, width = shape
    part = (planes, own_rows // n, width)
    dma = pltpu.SemaphoreType.DMA
    return [
        pltpu.VMEM((n, *part), jnp.bfloat16),
        pltpu.VMEM((slots, *part), jnp.bfloat16),
        pltpu.VMEM((n, *part), jnp.bfloat16),
        dma((n,)),
        dma((n,)),
        dma((slots,)),
        dma((slots,)),
        dma((n,)),
        dma((n,)),
        dma,
    ]


class Spreader:
    def __init__(self, partner, state, home, row_base, spread, ordered, sems):
        self.partner, self.state, self.home, self.row_base = partner, state, home, row_base
        self.spread, self.ordered = spread, ordered
        self.one_send, self.one_recv, self.two_send, self.two_recv, self.own_sem = sems
        self.me = lax.axis_index("expert")
        self.n = spread.shape[0]
        self.share = state.shape[1] // self.n

    def rows(self, number, base=0):
        return pl.ds(pl.multiple_of(base + number * self.share, self.share), self.share)

    def each(self, fn):
        def body(step, carry):
            fn(step, lax.rem(self.me + step, self.n))
            return carry

        lax.fori_loop(1, self.n, body, 0)

    def one(self, step, peer):
        return remote(
            self.state.at[:, self.rows(peer), :],
            self.spread.at[self.me],
            self.one_send.at[step],
            self.one_recv.at[step],
            expert=peer,
        )

    def two(self, step, peer):
        return remote(
            self.ordered.at[peer],
            self.home.at[:, self.rows(self.me, self.row_base), :],
            self.two_send.at[step],
            self.two_recv.at[step],
            expert=peer,
        )

    def spread_out(self):
        self.each(lambda step, peer: self.one(step, peer).start())
        self.own_share().start()

    def own_share(self):
        return pltpu.make_async_copy(
            self.state.at[:, self.rows(self.me), :], self.spread.at[self.me], self.own_sem
        )

    def send_home(self):
        self.each(lambda step, peer: self.one(step, peer).wait_recv())
        self.own_share().wait()

        def pick(step, carry):
            peer = lax.rem(self.me + step, self.n)
            self.ordered[peer] = self.spread[self.partner[peer]]
            self.two(step, peer).start()
            return carry

        lax.fori_loop(1, self.n, pick, 0)
        self.home[:, self.rows(self.me, self.row_base), :] = self.spread[self.partner[self.me]]

    def at_home(self, group):
        def body(number, carry):
            step = lax.rem(self.me - number + self.n, self.n)

            @pl.when(step > 0)
            def _():
                self.two(step, lax.rem(self.me + step, self.n)).wait_recv()

            return carry

        quarter = self.n // 4
        lax.fori_loop(group * quarter, (group + 1) * quarter, body, 0)

    def sends_done(self):
        self.each(lambda step, peer: self.one(step, peer).wait_send())
        self.each(lambda step, peer: self.two(step, peer).wait_send())


def spreader_scratch(shape, n):
    planes, own_rows, width = shape
    part = (n, planes, own_rows // n, width)
    return [pltpu.VMEM(part, jnp.bfloat16)] * 2 + [pltpu.SemaphoreType.DMA((n,))] * 4 + [pltpu.SemaphoreType.DMA]


def fill_tables(partner, table, rank, slots):
    n = partner.shape[0] // 2
    side = lax.axis_index("expert") // n
    for s in range(2):
        count = jnp.int32(0)
        for i in range(n):
            rank[s * n + i] = count
            count = count + jnp.where(partner[s * n + i] // n != s, 1, 0)
    for d in range(n):
        p = partner[side * n + d]
        table[d] = jnp.where(p // n == side, lax.rem(p, n), n + rank[p])
    for j in range(slots):
        chosen = jnp.int32(0)
        for i in range(n):
            hit = jnp.logical_and(partner[side * n + i] // n != side, rank[side * n + i] == j)
            chosen = jnp.where(hit, i, chosen)
        table[n + j] = chosen


def layer_kernel(
    slots,
    partner,
    ids,
    gate_values,
    x,
    cot,
    w,
    m,
    v,
    mixed,
    token_grad,
    keep,
    given,
    w_full,
    m_home,
    v_home,
    table,
    rank,
    gates,
    x_all,
    cot_all,
    dy_all,
    gate_all,
    both_all,
    hidden_all,
    part,
    from_core,
    from_over,
    from_line,
    give,
    *scratch,
):
    f32, bf16 = jnp.float32, jnp.bfloat16
    me = lax.axis_index("expert")
    half = lax.axis_index("dp")
    own_rows, width = w.shape[1], w.shape[2]
    tok = x.shape[0]
    z, y, core = me // 4, lax.rem(me // 2, 2), lax.rem(me, 2)
    movers = []
    moved = [(w.at[pl.ds(i, 1)], w_full.at[pl.ds(i, 1)], half * own_rows) for i in range(3)]
    for state, home, base in moved:
        own, scratch = scratch[:7], scratch[7:]
        movers.append(Spreader(partner, state, home, base, *own[:2], own[2:]))
    for state, home, base in ((m, m_home, 0), (v, v_home, 0)):
        own, scratch = scratch[:10], scratch[10:]
        movers.append(Mover(table, state, home, base, *own[:3], own[3:]))
    w_moves, m_move, v_move = movers[:3], movers[3], movers[4]
    block_recv, z_send, y_send, c_send, x_send, x_recv, own_sem = scratch[:7]
    s_send, s_recv, o_send, o_recv, l_send, l_recv, g_send, g_recv = scratch[7:]
    arrays = ((x, x_all), (cot, cot_all), (gates, gate_all))

    def hop(i, number, own, send_sem, dest):
        source, full = arrays[i]
        return remote(
            source if own else full.at[number],
            full.at[number],
            send_sem,
            block_recv.at[i, number],
            expert=dest,
        )

    def number_of(zz, yy, cc):
        return zz * 4 + yy * 2 + cc

    def down(i, s):
        return hop(i, number_of(z + s, y, core), s == 0, z_send.at[i, 0, s], me - 4)

    def up(i, s):
        return hop(i, number_of(z - s, y, core), s == 0, z_send.at[i, 1, s], me + 4)

    def over(i, zz, own=False):
        return hop(i, number_of(zz, y, core), own, y_send.at[i, zz], number_of(z, 1 - y, core))

    def beside(i, zz, yy, own=False):
        return hop(
            i, number_of(zz, yy, core), own, c_send.at[i, zz * 2 + yy], number_of(z, y, 1 - core)
        )

    def wait_block(i, number):
        hop(i, number, False, y_send.at[i, 0], lax.rem(me + 1, 16)).wait_recv()

    def passed_on(zz, which):
        for i in which:
            over(i, zz).start()
        for i in which:
            beside(i, zz, y).start()

    def line_step(s, which):
        @pl.when(z + 1 + s <= 3)
        def _():
            for i in which:
                wait_block(i, number_of(z + 1 + s, y, core))
                if s < 2:

                    @pl.when(z >= 1)
                    def _():
                        down(i, s + 1).start()

            passed_on(z + 1 + s, which)

        @pl.when(z - 1 - s >= 0)
        def _():
            for i in which:
                wait_block(i, number_of(z - 1 - s, y, core))
                if s < 2:

                    @pl.when(z <= 2)
                    def _():
                        up(i, s + 1).start()

            passed_on(z - 1 - s, which)

    def gate_column(b):
        mine = lax.broadcasted_iota(jnp.int32, gates.shape, 0) == partner[me]
        columns = []
        for side in range(2):
            row = jnp.sum(jnp.where(mine, gate_all[b * 2 + side], 0.0), axis=0, keepdims=True)
            columns.append(jnp.broadcast_to(row, (tok, tok)).T[:, :1])
        return jnp.concatenate(columns, axis=0)

    def to_core(i, b):
        return remote(
            part.at[i, b, 1 - core],
            from_core.at[i, b],
            s_send.at[i, b],
            s_recv.at[i, b],
            expert=z * 4 + y * 2 + 1 - core,
        )

    def to_over(i, zz):
        return remote(
            part.at[i, zz * 2 + 1 - y, core],
            from_over.at[i, zz],
            o_send.at[i, zz],
            o_recv.at[i, zz],
            expert=z * 4 + (1 - y) * 2 + core,
        )

    def on_line(i, zz, way):
        return remote(
            part.at[i, zz * 2 + y, core],
            from_line.at[i, zz, way],
            l_send.at[i, zz],
            l_recv.at[i, zz, way],
            expert=me + (4 if way else -4),
        )

    def added(i, b, source):
        part[i, b, core] = (part[i, b, core].astype(f32) + source.astype(f32)).astype(bf16)

    def place(t):
        mid = jnp.where(t <= 1, 3 - t, t - 2)
        return jnp.where(z == 0, 3 - t, jnp.where(z == 1, mid, jnp.where(z == 2, 3 - mid, t)))

    def chip_of(t):
        over = t < 4
        return place(lax.rem(t, 4)) * 2 + jnp.where(over, 1 - y, y)

    last = (((1,), (1,)), ((), ()))

    def forward_step(t):
        b = chip_of(t)
        rows = pl.ds(pl.multiple_of(b * 2 * tok, 256), 2 * tok)
        x_rows = x_all[pl.ds(b * 2, 2)].reshape(2 * tok, x_all.shape[2])
        pre_act = jnp.dot(x_rows, w_full[0], preferred_element_type=f32)
        lin_act = jnp.dot(x_rows, w_full[1], preferred_element_type=f32)
        sig = jax.nn.sigmoid(pre_act)
        silu = pre_act * sig
        hidden = (silu * lin_act).astype(bf16)
        hidden_all[rows, :] = hidden
        both_all[0, rows, :] = (lin_act * sig * (1.0 + pre_act * (1.0 - sig))).astype(bf16)
        both_all[1, rows, :] = silu.astype(bf16)
        out = lax.dot_general(hidden, w_full[2], last, preferred_element_type=f32)
        part[0, b] = (gate_column(b) * out).astype(bf16).reshape(2, tok, out.shape[1])
        to_core(0, b).start()

    def backward_step(t):
        b = chip_of(t)
        rows = pl.ds(pl.multiple_of(b * 2 * tok, 256), 2 * tok)
        cot_rows = cot_all[pl.ds(b * 2, 2)].reshape(2 * tok, x_all.shape[2])
        dy = (gate_column(b) * cot_rows.astype(f32)).astype(bf16)
        dy_all[pl.ds(b * 2, 2)] = dy.reshape(2, tok, x_all.shape[2])
        hidden_grad = jnp.dot(dy, w_full[2], preferred_element_type=f32)
        pre_grad = (hidden_grad * both_all[0, rows, :].astype(f32)).astype(bf16)
        lin_grad = (hidden_grad * both_all[1, rows, :].astype(f32)).astype(bf16)
        both_all[0, rows, :] = pre_grad
        both_all[1, rows, :] = lin_grad
        item = lax.dot_general(pre_grad, w_full[0], last, preferred_element_type=f32)
        item = item + lax.dot_general(lin_grad, w_full[1], last, preferred_element_type=f32)
        part[1, b] = item.astype(bf16).reshape(2, tok, item.shape[1])
        to_core(1, b).start()

    def core_sum(i, t):
        b = chip_of(t)
        to_core(i, b).wait_recv()
        added(i, b, from_core[i, b])

        @pl.when(t < 4)
        def _():
            to_over(i, b // 2).start()

    def own_block(i):
        return pltpu.make_async_copy(arrays[i][0], arrays[i][1].at[me], own_sem.at[i])

    def from_y(zz, which):
        for i in which:
            wait_block(i, number_of(zz, 1 - y, core))
            beside(i, zz, 1 - y).start()

    def exchange(plane):
        rows = pl.ds(pl.multiple_of(half * own_rows, own_rows), own_rows)
        part_rows = w_full.at[plane, rows, :]
        return remote(part_rows, part_rows, x_send.at[plane], x_recv.at[plane], dp=1 - half)

    def w_home(plane):
        for g in range(4):
            w_moves[plane].at_home(g)
        exchange(plane).start()

    plane_barrier(16, me)
    number = lax.broadcasted_iota(jnp.int32, gates.shape, 0)
    total = jnp.zeros(gates.shape, f32)
    for k in range(ids.shape[0]):
        named = jnp.broadcast_to(ids[k : k + 1, :], gates.shape) == number
        total = total + jnp.where(named, gate_values[k : k + 1, :], 0.0)
    gates[...] = total
    def first_sends(which):
        for i in which:

            @pl.when(z >= 1)
            def _():
                down(i, 0).start()

            @pl.when(z <= 2)
            def _():
                up(i, 0).start()

            over(i, z, True).start()
            beside(i, z, y, True).start()
            own_block(i).start()

    def all_from_y(which):
        from_y(z, which)
        for s in range(3):

            @pl.when(z + 1 + s <= 3)
            def _():
                from_y(z + 1 + s, which)

            @pl.when(z - 1 - s >= 0)
            def _():
                from_y(z - 1 - s, which)

    def all_beside(which):
        for i in which:
            own_block(i).wait()
            for zz in range(4):
                for yy in range(2):
                    wait_block(i, number_of(zz, yy, 1 - core))

    rows_first, rows_later = (2, 0), (1,)
    first_sends(rows_first)
    for move in w_moves:
        move.spread_out()
    fill_tables(partner, table, rank, slots)
    m_move.spread_out()
    line_step(0, rows_first)
    first_sends(rows_later)
    w_moves[0].send_home()
    line_step(1, rows_first)
    w_moves[1].send_home()
    w_home(0)
    line_step(2, rows_first)
    w_moves[2].send_home()
    line_step(0, rows_later)
    w_home(1)
    all_from_y(rows_first)
    w_home(2)
    m_move.cross()
    line_step(1, rows_later)
    line_step(2, rows_later)
    v_move.spread_out()
    m_move.send_home()
    all_beside(rows_first)
    for plane in range(3):
        exchange(plane).wait()

    def forward(t, carry):
        forward_step(t)

        @pl.when(t >= 1)
        def _():
            core_sum(0, t - 1)

        return carry

    lax.fori_loop(0, 8, forward, 0)
    core_sum(0, 7)
    all_from_y(rows_later)
    v_move.cross()
    all_beside(rows_later)

    def backward(t, carry):
        backward_step(t)

        @pl.when(t >= 1)
        def _():
            core_sum(1, t - 1)

        return carry

    lax.fori_loop(0, 8, backward, 0)
    core_sum(1, 7)

    tile = own_rows // 2

    def weight_grads(base, put):
        def body(j, carry):
            rows = pl.ds(pl.multiple_of(base + j * tile, 256), tile)
            first = (((0,), (0,)), ((), ()))
            x_cols = x_all[:, :, rows].reshape(-1, tile)
            dy_cols = dy_all[:, :, rows].reshape(-1, tile)
            put(0, j, lax.dot_general(x_cols, both_all[0], first, preferred_element_type=f32))
            put(1, j, lax.dot_general(x_cols, both_all[1], first, preferred_element_type=f32))
            put(2, j, lax.dot_general(dy_cols, hidden_all[...], first, preferred_element_type=f32))
            return carry

        lax.fori_loop(0, 2, body, 0)

    def gift(j):
        rows = pl.ds(pl.multiple_of(j * tile, 256), tile)
        return remote(
            give.at[:, rows, :], given.at[:, rows, :], g_send.at[j], g_recv.at[j], dp=1 - half
        )

    def put_give(plane, j, value):
        give[plane, pl.ds(pl.multiple_of(j * tile, 256), tile), :] = value.astype(bf16)
        if plane == 2:
            gift(j).start()

    def put_keep(plane, j, value):
        keep[plane, pl.ds(pl.multiple_of(j * tile, 256), tile), :] = value.astype(bf16)

    def over_sum(i, zz):
        to_over(i, zz).wait_recv()
        added(i, zz * 2 + y, from_over[i, zz])

    def line_sums(i, far):
        for way in (1, 0):
            zz = z + far if way else z - far

            @pl.when(zz <= 3 if way else zz >= 0)
            def _():
                over_sum(i, zz)

                @pl.when(z >= 1 if way else z <= 2)
                def _():
                    on_line(i, zz, way).wait_recv()
                    added(i, zz * 2 + y, from_line[i, zz, way])

                on_line(i, zz, way).start()

    line_sums(0, 3)
    weight_grads((1 - half) * own_rows, put_give)
    line_sums(0, 2)
    v_move.send_home()
    line_sums(1, 3)
    line_sums(0, 1)
    line_sums(1, 2)
    line_sums(1, 1)
    weight_grads(half * own_rows, put_keep)
    for i, out in ((0, mixed), (1, token_grad)):
        over_sum(i, z)

        @pl.when(z >= 1)
        def _():
            on_line(i, z, 1).wait_recv()
            added(i, z * 2 + y, from_line[i, z, 1])

        @pl.when(z <= 2)
        def _():
            on_line(i, z, 0).wait_recv()
            added(i, z * 2 + y, from_line[i, z, 0])

        out[...] = part[i, z * 2 + y, core]
    for g in range(4):
        m_move.at_home(g)
        v_move.at_home(g)
    for j in range(2):
        gift(j).wait()
    for move in w_moves:
        move.sends_done()
    for i in range(3):
        for s in range(3):

            @pl.when(jnp.logical_and(z >= 1, z + s <= 3))
            def _():
                down(i, s).wait_send()

            @pl.when(jnp.logical_and(z <= 2, z - s >= 0))
            def _():
                up(i, s).wait_send()

        for zz in range(4):
            over(i, zz).wait_send()
            for yy in range(2):
                beside(i, zz, yy).wait_send()
    m_move.sends_done()
    v_move.sends_done()
    for i in range(2):
        for b in range(8):
            to_core(i, b).wait_send()
        for zz in range(4):
            to_over(i, zz).wait_send()

            @pl.when(zz != z)
            def _():
                on_line(i, zz, 1).wait_send()


def layer(slots, number, partner, ids, gate_values, x, cot, w, m, v):
    n = lax.axis_size("expert")
    vmem = pl.BlockSpec(memory_space=pltpu.VMEM)
    hbm = pl.BlockSpec(memory_space=pl.ANY)
    tok, model = x.shape
    planes, own_rows, width = v.shape
    bf16 = jnp.bfloat16
    dma = pltpu.SemaphoreType.DMA
    outs = [
        jax.ShapeDtypeStruct((tok, model), bf16),
        jax.ShapeDtypeStruct((tok, model), bf16),
        jax.ShapeDtypeStruct(v.shape, bf16),
        jax.ShapeDtypeStruct(v.shape, bf16),
        jax.ShapeDtypeStruct((planes, 2 * own_rows, width), bf16),
        jax.ShapeDtypeStruct(v.shape, bf16),
        jax.ShapeDtypeStruct(v.shape, bf16),
    ]
    return pl.pallas_call(
        functools.partial(layer_kernel, slots),
        out_shape=outs,
        in_specs=[pl.BlockSpec(memory_space=pltpu.SMEM)] + [vmem] * 2 + [hbm] * 5,
        out_specs=[vmem] * 7,
        scratch_shapes=[
            pltpu.SMEM((n,), jnp.int32),
            pltpu.SMEM((n,), jnp.int32),
            pltpu.VMEM((n, tok), jnp.float32),
            pltpu.VMEM((n, tok, model), bf16),
            pltpu.VMEM((n, tok, model), bf16),
            pltpu.VMEM((n, tok, model), bf16),
            pltpu.VMEM((n, n, tok), jnp.float32),
            pltpu.VMEM((2, n * tok, width), bf16),
            pltpu.VMEM((n * tok, width), bf16),
            pltpu.VMEM((2, n // 2, 2, tok, model), bf16),
            pltpu.VMEM((2, n // 2, tok, model), bf16),
            pltpu.VMEM((2, 4, tok, model), bf16),
            pltpu.VMEM((2, 4, 2, tok, model), bf16),
            pltpu.VMEM(v.shape, bf16),
            *(spreader_scratch((1, *v.shape[1:]), n) * 3),
            *(mover_scratch(v.shape, n // 2, slots) * 2),
            dma((3, n)),
            dma((3, 2, 3)),
            dma((3, 4)),
            dma((3, 8)),
            dma((3,)),
            dma((3,)),
            dma((3,)),
            dma((2, 8)),
            dma((2, 8)),
            dma((2, 4)),
            dma((2, 4)),
            dma((2, 4)),
            dma((2, 4, 2)),
            dma((2,)),
            dma((2,)),
        ],
        compiler_params=pltpu.CompilerParams(
            collective_id=number, has_side_effects=True, vmem_limit_bytes=60 * 2**20
        ),
        cost_estimate=pl.CostEstimate(
            flops=15 * 10**9, bytes_accessed=200 * 2**20, transcendentals=0
        ),
    )(partner, ids, gate_values, x, cot, w, m, v)


def layer_and_step(slots, number, partner, ids, gate_values, x, cot, w, m, v):
    f32, bf16 = jnp.float32, jnp.bfloat16
    own_rows = w.shape[1]
    mixed, token_grad, keep, given, w_full, m_here, v_here = layer(
        slots, number, partner, ids, gate_values, x, cot, w, m, v
    )
    w_here = lax.dynamic_slice_in_dim(w_full, lax.axis_index("dp") * own_rows, own_rows, axis=1)
    grad = keep.astype(f32) + given.astype(f32)
    new_state = adam(*[a.astype(f32) for a in (w_here, m_here, v_here)], grad)
    return (mixed, token_grad, *[a.astype(bf16).transpose(1, 0, 2)[None] for a in new_state])


def shards_dense(
    tokens, cotangent, expert_ids, gate_weights, partner, weights, first_moment, second_moment
):
    half = lax.axis_size("expert") // 2
    number = jnp.arange(2 * half, dtype=jnp.int32)
    crossing = jnp.sum(jnp.where(partner >= half, number < half, False).astype(jnp.int32))
    old = [a[0].transpose(1, 0, 2) for a in (weights, first_moment, second_moment)]
    return lax.switch(
        jnp.where(crossing <= 4, 0, jnp.where(crossing <= 6, 1, 2)),
        [functools.partial(layer_and_step, slots, i) for i, slots in enumerate((4, 6, 8))],
        partner,
        expert_ids.T,
        gate_weights.T,
        tokens,
        cotangent,
        *old,
    )


def shards(*args):
    fits = lax.axis_size("dp") == 2 and lax.axis_size("expert") == 16
    if fits and args[0].shape[0] == 128 and args[5].shape[1] % 512 == 0:
        return shards_dense(*args)
    return shards_by_slot(*args)


def solution(mesh):
    in_specs = (
        P(("dp", "expert"), None),
        P(("dp", "expert"), None),
        P(("dp", "expert"), None),
        P(("dp", "expert"), None),
        P(),
        P("expert", "dp", None, None),
        P("expert", "dp", None, None),
        P("expert", "dp", None, None),
    )
    out_specs = (
        P(("dp", "expert"), None),
        P(("dp", "expert"), None),
        P("expert", "dp", None, None),
        P("expert", "dp", None, None),
        P("expert", "dp", None, None),
    )
    return jax.shard_map(shards, mesh=mesh, in_specs=in_specs, out_specs=out_specs, check_vma=False)
```
